32 devices in a mesh: gx: 2 (over y), gy: 4 (over x, core), gz: 4 (over z).
Axes of the slice: x: 2, y: 2, z: 4, core: 2. Of those that a mesh axis runs over, the one named last changes fastest.
Arguments:
- displacement: float32 [3, 4, 16, 512], P(None, 'gx', 'gy', 'gz'), may hold values from -0.4 to 0.4
- load: float32 [3, 4, 16, 512], P(None, 'gx', 'gy', 'gz'), may hold values from -12 to 12
- material: int32 [4, 16, 512], P('gx', 'gy', 'gz'), may hold values from 0 to 7, as said below
- free_node: int32 [4, 16, 512], P('gx', 'gy', 'gz'), may hold values 0 or 1
- table: float32 [8, 3], replicated, may hold values from 0.5 to 20, as said below
Outputs:
- increment: float32 [3, 4, 16, 512], P(None, 'gx', 'gy', 'gz')
- residual: float32 [3, 4, 16, 512], P(None, 'gx', 'gy', 'gz')
The draws below stay inside these ranges and needn't reach their ends.
Inputs may be any that keep to these rules, and one draw needn't show every extreme that they name: The material id of an element with third index k lies between band and band + 2, where band = (k * 6) // 512. `table`: all entries positive.
All inputs are finite; a program needn't handle non-finite values. No bound on the sum of `free_node` on one device may be relied on, other than what follows from the above.
Results may differ from the reference program's by a relative error of at most 0.0004.
Values sent between devices are 32-bit elements; how exact they have to be, the bound alone decides.
A program may use at most 64 MiB of HBM per device.

```python
import jax
import jax.numpy as jnp

NMAT = 8
OUTER = 2
NX = 4
NY = 16
NZ = 512


def draw_material(key, part):
    depth = jnp.arange(NZ, dtype=jnp.int32)
    band = depth * (NMAT - 2) // NZ
    offset = jax.random.randint(key, (NX, NY, NZ), 0, 3)
    return (band[None, None, :] + offset).astype(jnp.int32)


def draw_table(key, part):
    rows = jnp.arange(NMAT, dtype=jnp.float32)
    base = jnp.exp(rows * (jnp.log(3.0) / (NMAT - 1)))
    jitter = jnp.exp(jax.random.uniform(key, (NMAT, 3), jnp.float32, -0.4, 0.4))
    scale = jnp.array([1.0, 1.0, 4.0], jnp.float32)
    return (base[:, None] * jitter * scale[None, :]).astype(jnp.float32)


def place_ends(drawn, stream_key, low, top_value):
    place = [jax.random.randint(jax.random.fold_in(stream_key, axis), (), 0, length) for axis, length in enumerate(drawn.shape)]
    longest = drawn.shape.index(max(drawn.shape))
    neighbour = place[:longest] + [(place[longest] + 1) % drawn.shape[longest]] + place[longest + 1:]
    return drawn.at[tuple(place)].set(low).at[tuple(neighbour)].set(top_value)


def block_scale(key, dims, shards, low, largest):
    level, own = 1.0, jax.random.fold_in(key, 6)
    for position, parts in shards:
        heights = jnp.exp(jax.random.uniform(jax.random.fold_in(own, position), (parts,), jnp.float32, low / len(shards), largest / len(shards)))
        level = level * jnp.repeat(heights, dims[position] // parts).reshape([-1 if axis == position else 1 for axis in range(len(dims))])
    return level


def bell_draw(stream_key, extent, width, most, cuts=(), kind=jnp.bfloat16):
    factor_of = block_scale(stream_key, extent, cuts, -0.22, 0.18) if cuts else 1.0
    result = jax.random.normal(stream_key, extent, jnp.float32) * width * factor_of
    return jnp.minimum(jnp.maximum(result, -most), most).astype(kind)


def setup_inputs(seed: int = 0) -> dict:
    keys = jax.random.split(jax.random.key(seed), 6)
    return {
        "displacement": bell_draw(keys[0], (3, NX, NY, NZ), 0.08, 0.4, ((1, 2), (2, 4), (3, 4)), jnp.float32),
        "load": bell_draw(keys[1], (3, NX, NY, NZ), 2.0, 12.0, ((1, 2), (2, 4), (3, 4)), jnp.float32),
        "material": draw_material(jax.random.fold_in(keys[5], 71), 0),
        "free_node": place_ends((jax.random.randint(keys[3], (NX, NY, NZ), 0, 8) < 7).astype(jnp.int32), jax.random.fold_in(keys[3], 1), 0, 1),
        "table": draw_table(jax.random.fold_in(keys[5], 71), 0),
    }


CORNERS = [(a, b, c) for a in (0, 1) for b in (0, 1) for c in (0, 1)]
SHIFTS = (9.6, 51.4)
HALF_WIDTH = 29.5

def slopes(corner):
    return [0.25 * (2 * corner[d] - 1) for d in range(3)]

def gradient_tensor(pieces):
    return [[sum((pieces[n][i] * slopes(CORNERS[n])[j] for n in range(8))) for j in range(3)] for i in range(3)]

def material_state(grad, lame_first, shear):
    frame = [[grad[i][j] + (1.0 if i == j else 0.0) for j in range(3)] for i in range(3)]
    strain = [[0.5 * (sum((frame[k][i] * frame[k][j] for k in range(3))) - (1.0 if i == j else 0.0)) for j in range(3)] for i in range(3)]
    trace = strain[0][0] + strain[1][1] + strain[2][2]
    stress = [[2.0 * shear * strain[i][j] + (lame_first * trace if i == j else 0.0) for j in range(3)] for i in range(3)]
    left = [[sum((frame[i][j] * frame[k][j] for j in range(3))) for k in range(3)] for i in range(3)]
    return (frame, stress, left)

def lookup(material, table):
    columns = [jnp.zeros(material.shape, jnp.float32) for column in range(3)]
    for row in range(table.shape[0]):
        hit = material == row
        columns = [jnp.where(hit, table[row, column], columns[column]) for column in range(3)]
    return columns

def element_view(field, corner):
    return field[..., corner[0]:corner[0] + NX - 1, corner[1]:corner[1] + NY - 1, corner[2]:corner[2] + NZ - 1]

def operate(vector, free, state):
    frame, stress, left, lame_first, shear, mass = state
    masked = vector * free
    pieces = [element_view(masked, corner) for corner in CORNERS]
    grad = gradient_tensor(pieces)
    trace = sum((frame[k][j] * grad[k][j] for k in range(3) for j in range(3)))
    left_grad = [[sum((left[i][k] * grad[k][j] for k in range(3))) for j in range(3)] for i in range(3)]
    cross = [[sum((grad[l][k] * frame[l][j] for l in range(3))) for j in range(3)] for k in range(3)]
    twisted = [[sum((frame[i][k] * cross[k][j] for k in range(3))) for j in range(3)] for i in range(3)]
    curved = [[sum((grad[i][l] * stress[l][j] for l in range(3))) for j in range(3)] for i in range(3)]
    piola = [[lame_first * trace * frame[i][j] + shear * (left_grad[i][j] + twisted[i][j]) + curved[i][j] for j in range(3)] for i in range(3)]
    output = jnp.zeros_like(vector)
    for n, corner in enumerate(CORNERS):
        slope = slopes(corner)
        term = jnp.stack([sum((piola[i][j] * slope[j] for j in range(3))) + 0.125 * mass * pieces[n][i] for i in range(3)])
        output = output.at[:, corner[0]:corner[0] + NX - 1, corner[1]:corner[1] + NY - 1, corner[2]:corner[2] + NZ - 1].add(term)
    return free * output + (1.0 - free) * vector

def solve_small(matrix, vector):
    sym = 0.5 * (matrix + matrix.T)
    l00 = jnp.sqrt(sym[0, 0])
    l10 = sym[1, 0] / l00
    l20 = sym[2, 0] / l00
    l11 = jnp.sqrt(sym[1, 1] - l10 * l10)
    l21 = (sym[2, 1] - l20 * l10) / l11
    l22 = jnp.sqrt(sym[2, 2] - l20 * l20 - l21 * l21)
    y0 = vector[0] / l00
    y1 = (vector[1] - l10 * y0) / l11
    y2 = (vector[2] - l20 * y0 - l21 * y1) / l22
    c2 = y2 / l22
    c1 = (y1 - l21 * c2) / l11
    c0 = (y0 - l10 * c1 - l20 * c2) / l00
    return [c0, c1, c2]

def reference(displacement, load, material, free_node, table):
    elements = material[:NX - 1, :NY - 1, :NZ - 1]
    lame_first, shear, mass = lookup(elements, table)
    pieces = [element_view(displacement, corner) for corner in CORNERS]
    frame, stress, left = material_state(gradient_tensor(pieces), lame_first, shear)
    state = (frame, stress, left, lame_first, shear, mass)
    free = free_node.astype(jnp.float32)
    residual = load * free
    increment = jnp.zeros_like(residual)
    for outer in range(OUTER):
        basis = [residual]
        images = []
        for step in range(3):
            images.append(operate(basis[step], free, state))
            if step < 2:
                basis.append((images[step] - SHIFTS[step] * basis[step]) / HALF_WIDTH)
        matrix = jnp.stack([jnp.stack([jnp.sum(basis[i] * images[j]) for j in range(3)]) for i in range(3)])
        vector = jnp.stack([jnp.sum(basis[i] * residual) for i in range(3)])
        coeffs = solve_small(matrix, vector)
        increment = increment + sum((coeffs[j] * basis[j] for j in range(3)))
        residual = residual - sum((coeffs[j] * images[j] for j in range(3)))
    return (increment, residual)
```

```python
import functools

import jax
import jax.numpy as jnp
import numpy as np
from jax import lax
from jax.experimental import pallas as pl
from jax.experimental.pallas import tpu as pltpu
from jax.sharding import PartitionSpec as P

SHIFTS = (9.6, 51.4)
HALF_WIDTH = 29.5
CHAIN = SHIFTS + (30.5,) + SHIFTS + (30.5,)
STEPS = 6
FIELDS = 8
LANES = 128
PRODUCTS = [(i, j) for i in range(7) for j in range(i, 7) if i < 6]
F32 = jnp.float32


def place(t):
    return 32 * (t // 8) + t % 8


def tables():
    def times(x):
        out = np.zeros(7)
        for k in range(6):
            out[k] += CHAIN[k] * x[k]
            out[k + 1] += HALF_WIDTH * x[k]
        return out

    unit = np.eye(7)
    start = [unit[0]] + [-times(unit[j]) for j in range(3)]
    b, m = [start], []
    for j in range(3):
        m.append([times(x) for x in b[j]])
        if j < 2:
            b.append([(y - SHIFTS[j] * x) / HALF_WIDTH for x, y in zip(b[j], m[j])])
    forms = [(b[i], m[j]) for i in range(3) for j in range(3)] + [(b[i], start) for i in range(3)]
    wide = np.zeros((4, 4, 16, LANES))
    for f, (left, right) in enumerate(forms):
        for a in range(4):
            for t, (i, j) in enumerate(PRODUCTS):
                wide[0, a, f, place(t)] = left[a][i]
                wide[1, a, f, place(t)] = left[a][j] if i != j else 0.0
                wide[2, a, f, place(t)] = right[a][i]
                wide[3, a, f, place(t)] = right[a][j]
    last = np.zeros((16, LANES))
    for a in range(4):
        for k in range(7):
            last[a, k] = 1.0 if 0 < a == k + 1 else 0.0
            last[a, 16 + k] = start[a][k]
            for j in range(3):
                last[4 + 4 * j + a, k] = b[j][a][k]
                last[4 + 4 * j + a, 16 + k] = -m[j][a][k]
    return np.concatenate([wide.reshape(-1, LANES), last]).astype(np.float32)


def solve_small(gram, right):
    sym = [[0.5 * (gram[i][j] + gram[j][i]) for j in range(3)] for i in range(3)]
    l00 = jnp.sqrt(sym[0][0])
    l10 = sym[1][0] / l00
    l20 = sym[2][0] / l00
    l11 = jnp.sqrt(sym[1][1] - l10 * l10)
    l21 = (sym[2][1] - l20 * l10) / l11
    l22 = jnp.sqrt(sym[2][2] - l20 * l20 - l21 * l21)
    y0 = right[0] / l00
    y1 = (right[1] - l10 * y0) / l11
    y2 = (right[2] - l20 * y0 - l21 * y1) / l22
    c2 = y2 / l22
    c1 = (y1 - l21 * c2) / l11
    c0 = (y0 - l10 * c1 - l20 * c2) / l00
    return [c0, c1, c2]


def two_sum(a, b):
    s = a + b
    t = s - a
    return s, (a - (s - t)) + (b - t)


def add_pair(p, q):
    s, e = two_sum(p[0], q[0])
    return s, e + (p[1] + q[1])


def split(a):
    t = 4097.0 * a
    high = t - (t - a)
    return high, a - high


def two_product(a, b):
    p = a * b
    (ah, al), (bh, bl) = split(a), split(b)
    return p, ((ah * bh - p) + ah * bl + al * bh) + al * bl


def loop(count, body):
    if count <= 32:
        for i in range(count):
            body(i)
    else:

        def step(i, carry):
            body(i)
            return carry

        lax.fori_loop(0, count, step, 0)


def when(condition, body):
    if isinstance(condition, bool):
        if condition:
            body()
    else:
        pl.when(condition)(body)


class Plan:
    def __init__(self, grid, shard):
        self.grid, self.shard = grid, shard
        ngx, ngy, ngz = grid
        sx, sy, sz = shard
        self.n = ngx * ngy
        self.nz = ngz * sz
        self.halo = STEPS
        self.counts = [self.n] * ngz
        self.own = -(-self.nz // sum(self.counts))
        self.span = self.own + 2 * self.halo
        self.pitch = 1 << (self.span - 1).bit_length()
        self.packed = LANES // self.pitch
        self.groups = ngx * sx // self.packed
        self.mixed = LANES // (sx * self.pitch)
        self.tiles = FIELDS // self.mixed
        self.stride = LANES // (3 * sx)
        self.workers = -(-self.nz // self.own)
        self.base = [sum(self.counts[:z]) for z in range(ngz)]
        own, halo = self.own, self.halo
        self.to_low = [max(0, (sz * z - own - halo) // own + 1) for z in range(ngz)]
        self.to_high = [
            min(self.workers - 1, -(-(sz * z + sz + halo) // own) - 1) for z in range(ngz)
        ]
        self.from_low = [sz * z // own for z in range(ngz)]
        self.from_high = [(sz * z + sz - 1) // own for z in range(ngz)]
        self.sends = max(b - a + 1 for a, b in zip(self.to_low, self.to_high))
        self.returns = max(b - a + 1 for a, b in zip(self.from_low, self.from_high))
        assert sz == LANES and 8 % sy == 0 and own <= self.stride and LANES % self.pitch == 0


def pick(values, z):
    if all(v == values[0] for v in values):
        return values[0]
    out = values[0]
    for k in range(1, len(values)):
        out = jnp.where(z >= k, values[k], out)
    return out


def kernel(
    plan,
    disp_hbm,
    load_hbm,
    mat_hbm,
    free_hbm,
    table_hbm,
    const_hbm,
    out_ref,
    raw,
    flags,
    pack,
    recv,
    basis,
    fields,
    state,
    parts,
    back,
    vt,
    sums,
    const,
    table_ref,
    in_sem,
    send_sem,
    recv_sem,
    back_send,
    back_recv,
    sum_send,
    sum_recv,
):
    ngx, ngy, ngz = plan.grid
    sx, sy, sz = plan.shard
    n, own, halo, pitch = plan.n, plan.own, plan.halo, plan.pitch
    nx, ny = ngx * sx, ngy * sy
    groups, mixed, tiles = plan.groups, plan.mixed, plan.tiles
    total = n * ngz
    gx, gy, gz = lax.axis_index("gx"), lax.axis_index("gy"), lax.axis_index("gz")
    p = gx * ngy + gy
    me = p * ngz + gz
    worker = pick(plan.base, gz) + p
    first = own * worker - halo

    fetched = [
        pltpu.make_async_copy(disp_hbm, raw.at[pl.ds(0, 3)], in_sem.at[0]),
        pltpu.make_async_copy(load_hbm, raw.at[pl.ds(3, 3)], in_sem.at[1]),
        pltpu.make_async_copy(mat_hbm, flags.at[0], in_sem.at[2]),
        pltpu.make_async_copy(free_hbm, flags.at[1], in_sem.at[3]),
        pltpu.make_async_copy(table_hbm, table_ref, in_sem.at[4]),
        pltpu.make_async_copy(const_hbm, const, in_sem.at[5]),
    ]
    for copy in fetched:
        copy.start()

    def other(k):
        d = me + k
        return jnp.where(d >= total, d - total, d)

    def address(d):
        return {"gx": d // (ngy * ngz), "gy": lax.rem(d // ngz, ngy), "gz": lax.rem(d, ngz)}

    def where_is(d):
        return dict(device_id=d, device_id_type=pl.DeviceIdType.LOGICAL)

    barrier = pltpu.get_barrier_semaphore()
    loop(total - 1, lambda k: pl.semaphore_signal(barrier, inc=1, **where_is(other(k + 1))))

    for copy in fetched[:4]:
        copy.wait()
    raw[6] = flags[0].astype(F32)
    raw[7] = flags[1].astype(F32)

    lane = lax.broadcasted_iota(jnp.int32, (8, LANES), 1)
    row = lax.broadcasted_iota(jnp.int32, (8, LANES), 0)
    per = 8 // sy
    stacks = -(-tiles // per)
    held = []
    for t in range(stacks):
        part = []
        for e in range(mixed * sx):
            f, i = e // sx, e % sx
            rows = [raw[mixed * min(per * t + h, tiles - 1) + f, i] for h in range(per)]
            part.append(jnp.concatenate(rows, axis=0))
        held.append(part)

    to_low = pick(plan.to_low, gz)
    to_count = pick([b - a + 1 for a, b in zip(plan.to_low, plan.to_high)], gz)

    def home(w):
        z = 0
        for k in range(1, ngz):
            z = z + jnp.where(w >= plan.base[k], 1, 0)
        return (w - pick(plan.base, z)) * ngz + z

    def prepare(j):
        w = to_low + j
        offset = sz * gz - (own * w - halo)
        for t in range(stacks):
            out = None
            for e, v in enumerate(held[t]):
                moved = pltpu.roll(v, lax.rem(offset + (pitch * e + 8 * LANES), LANES), 1)
                out = moved if out is None else jnp.where(lane >= pitch * e, moved, out)
            for h in range(min(per, tiles - per * t)):
                pack[j, per * t + h] = out[sy * h : sy * (h + 1)]

    loop(plan.sends, prepare)

    pl.semaphore_wait(barrier, total - 1)

    def piece(j, start):
        w = to_low + j
        slot = jnp.where(sz * gz > jnp.maximum(own * w - halo, 0), 1, 0)
        d = home(w)
        dst = recv.at[slot, :, gx, gy]
        remote = pltpu.make_async_remote_copy(
            src_ref=pack.at[j],
            dst_ref=dst,
            send_sem=send_sem.at[0],
            recv_sem=recv_sem.at[slot],
            **where_is(d),
        )
        valid = True if plan.sends == min(
            b - a + 1 for a, b in zip(plan.to_low, plan.to_high)
        ) else j < to_count
        if start:
            when(valid & (d != me), remote.start)
            when(
                valid & (d == me),
                lambda: pltpu.make_async_copy(pack.at[j], dst, recv_sem.at[slot]).start(),
            )
        else:
            when(valid & (d != me), remote.wait_send)

    loop(plan.sends, lambda j: piece(j, True))

    def settle(ref, sem):
        pltpu.make_async_copy(ref, ref, sem).wait()

    settled = jnp.maximum(first, 0)
    low_slab = lax.div(settled, sz)
    edge = sz * (low_slab + 1)
    two = (first + plan.span > edge) & (low_slab + 1 < ngz)
    settle(recv.at[0], recv_sem.at[0])
    when(two, lambda: settle(recv.at[1], recv_sem.at[1]))

    wide_lane = lax.broadcasted_iota(jnp.int32, (ny, LANES), 1)
    depth = lax.rem(wide_lane, pitch)
    plane = depth + first
    near = plane < edge
    seg = sx * pitch

    def gather_rows(slot, k, x):
        return jnp.concatenate([recv[slot, k, x, g] for g in range(ngy)], axis=0)

    def source(k, x):
        return jnp.where(near, gather_rows(0, k, x), gather_rows(1, k, x))

    def unpack(k, g):
        parts_in = [source(k, g * mixed + d) for d in range(mixed)]
        out = []
        for f in range(mixed):
            v = None
            for d in range(mixed):
                s = (d - f) * seg % LANES
                moved = pltpu.roll(parts_in[d], s, 1) if s else parts_in[d]
                v = moved if v is None else jnp.where(wide_lane >= d * seg, moved, v)
            out.append(v)
        return out

    got = [[None] * groups for _ in range(FIELDS)]
    for g in range(groups):
        for k in range(tiles):
            for f, v in enumerate(unpack(k, g)):
                got[mixed * k + f][g] = v

    span = range(groups)

    def next_z(a):
        return [pltpu.roll(v, LANES - 1, 1) for v in a]

    def last_z(a):
        return [pltpu.roll(v, 1, 1) for v in a]

    def next_y(a):
        return [pltpu.roll(v, ny - 1, 0) for v in a]

    def last_y(a):
        return [pltpu.roll(v, 1, 0) for v in a]

    def next_x(a):
        moved = [pltpu.roll(v, LANES - pitch, 1) for v in a]
        if groups == 1:
            return moved
        return [
            jnp.where(wide_lane >= LANES - pitch, moved[min(g + 1, groups - 1)], moved[g])
            for g in span
        ]

    def last_x(a):
        moved = [pltpu.roll(v, pitch, 1) for v in a]
        if groups == 1:
            return moved
        return [jnp.where(wide_lane < pitch, moved[max(g - 1, 0)], moved[g]) for g in span]

    def both(op, *lists):
        return [op(*vs) for vs in zip(*lists)]

    add = functools.partial(both, lambda a, b: a + b)
    sub = functools.partial(both, lambda a, b: a - b)

    def gradient(vector):
        grad = []
        for v in vector:
            moved = next_z(v)
            total_z, change = add(v, moved), sub(moved, v)
            shifted = next_y(total_z)
            flat, tilt, rise = add(total_z, shifted), sub(shifted, total_z), add(change, next_y(change))
            grad.append(
                [sub(next_x(flat), flat), add(next_x(tilt), tilt), add(next_x(rise), rise)]
            )
        return grad

    pairs = [(0, 0), (0, 1), (0, 2), (1, 1), (1, 2), (2, 2)]
    free = got[7]
    for c in range(3):
        for g in span:
            basis[0, c, g] = got[3 + c][g] * free[g]
    grad = gradient([got[0], got[1], got[2]])
    fetched[4].wait()
    mass = []
    high = lax.broadcasted_iota(jnp.int32, (ny, LANES), 0)
    for g in span:
        valid = (high <= ny - 2) & (plane >= 0) & (plane <= plan.nz - 2) & (depth <= plan.span - 2)
        valid = valid & (lax.div(wide_lane, pitch) + g * plan.packed <= nx - 2)
        material = got[6][g]
        zero = jnp.zeros((ny, LANES), F32)
        lame, shear, heavy = zero, zero, zero
        for r in range(table_ref.shape[1]):
            hit = material == float(r)
            lame = jnp.where(hit, table_ref[0, r], lame)
            shear = jnp.where(hit, table_ref[1, r], shear)
            heavy = jnp.where(hit, table_ref[2, r], heavy)
        lame = jnp.where(valid, lame * 0.0625, 0.0)
        shear = jnp.where(valid, shear * 0.0625, 0.0)
        mass.append(jnp.where(valid, heavy * 0.125, 0.0))
        frame = [
            [0.25 * grad[i][j][g] + (1.0 if i == j else 0.0) for j in range(3)] for i in range(3)
        ]
        strain = {}
        for i, j in pairs:
            v = sum(frame[k][i] * frame[k][j] for k in range(3))
            strain[i, j] = 0.5 * (v - 1.0 if i == j else v)
        bulk = lame * (strain[0, 0] + strain[1, 1] + strain[2, 2])
        for i in range(3):
            for j in range(3):
                state[3 * i + j, g] = frame[i][j]
        for spot, (i, j) in enumerate(pairs):
            v = 2.0 * shear * strain[i, j]
            state[9 + spot, g] = v + bulk if i == j else v
        state[15, g] = lame
        state[16, g] = shear
    mass = add(mass, last_x(mass))
    mass = add(mass, last_y(mass))
    mass = add(mass, last_z(mass))
    for g in span:
        fields[0, g] = free[g]
        fields[1, g] = free[g] * (1.0 / HALF_WIDTH)
        fields[2, g] = (free[g] * mass[g] + (1.0 - free[g])) * (1.0 / HALF_WIDTH)

    rows8 = [pl.ds(8 * r, 8) for r in range(ny // 8)]

    def apply(j):
        grad = gradient([[basis[j, c, g] * fields[0, g] for g in span] for c in range(3)])
        pio = [[[[None] * len(rows8) for _ in span] for _ in range(3)] for _ in range(3)]
        for g in span:
            for r, at in enumerate(rows8):
                d = [[grad[c][q][g][8 * r : 8 * r + 8] for q in range(3)] for c in range(3)]
                f = [[state[3 * i + k, g, at] for k in range(3)] for i in range(3)]
                pulled = [
                    [sum(f[k][a] * d[k][b] for k in range(3)) for b in range(3)] for a in range(3)
                ]
                lame, shear = state[15, g, at], state[16, g, at]
                bulk = lame * (pulled[0][0] + pulled[1][1] + pulled[2][2])
                t, s = {}, {}
                for spot, (a, b) in enumerate(pairs):
                    v = shear * (pulled[a][b] + pulled[b][a])
                    t[a, b] = t[b, a] = v + bulk if a == b else v
                    s[a, b] = s[b, a] = state[9 + spot, g, at]
                for i in range(3):
                    for b in range(3):
                        v = sum(f[i][k] * t[k, b] for k in range(3))
                        pio[i][b][g][r] = v + sum(d[i][k] * s[k, b] for k in range(3))
        for c in range(3):
            e = [[jnp.concatenate(pio[c][b][g], axis=0) for g in span] for b in range(3)]
            across = sub(last_x(e[0]), e[0])
            along = add(last_x(e[1]), e[1])
            up = add(last_x(e[2]), e[2])
            flat = add(last_y(add(across, along)), sub(across, along))
            up = add(up, last_y(up))
            out = add(last_z(add(flat, up)), sub(flat, up))
            for g in span:
                basis[j + 1, c, g] = fields[1, g] * out[g] + (
                    fields[2, g] - CHAIN[j] / HALF_WIDTH
                ) * basis[j, c, g]

    for j in range(STEPS):
        apply(j)

    mine = (depth >= halo) & (depth < halo + own) & (plane < plan.nz)
    spots = [(c, g, r) for c in range(3) for g in span for r in range(ny // 8)]
    for k in range(7):
        v = [
            jnp.where(mine[8 * r : 8 * r + 8], basis[k, c, g, rows8[r]], 0.0) for c, g, r in spots
        ]
        top = jnp.abs(v[0])
        for u in v[1:]:
            top = jnp.maximum(top, jnp.abs(u))
        grain = top * (32768.0 * max(1, len(v) // 6))
        for s, u in enumerate(v):
            coarse = (u + grain) - grain
            parts[0, k, s] = coarse
            parts[1, k, s] = u - coarse
    pairs_of = {}
    for i in range(6):
        acc = {j: [None, None] for j in range(i, 7)}
        for s in range(len(spots)):
            ch, cl = parts[0, i, s], parts[1, i, s]
            for j in range(i, 7):
                dh, dl = parts[0, j, s], parts[1, j, s]
                new = [ch * dh, cl * (dh + ch + dl) if i == j else ch * dl + cl * (dh + dl)]
                acc[j] = new if s == 0 else [acc[j][0] + new[0], acc[j][1] + new[1]]
        for j in range(i, 7):
            pairs_of[i, j] = acc[j]
    items = [tuple(pairs_of[q]) for q in PRODUCTS]
    blank = (jnp.zeros((8, LANES), F32), jnp.zeros((8, LANES), F32))
    items = items + [blank] * (32 - len(items))

    def merge(a, b, mask, shift, axis):
        size = 8 if axis == 0 else LANES
        first_in, second_in = [], []
        for u, v in zip(a, b):
            if 2 * shift == size:
                first_in.append(jnp.where(mask, u, v))
                second_in.append(pltpu.roll(jnp.where(mask, v, u), shift, axis))
            else:
                first_in.append(jnp.where(mask, u, pltpu.roll(v, shift, axis)))
                second_in.append(jnp.where(mask, pltpu.roll(u, size - shift, axis), v))
        return add_pair(first_in, second_in)

    tall = []
    for q in range(4):
        it = items[8 * q : 8 * q + 8]
        one = [merge(it[r], it[r + 4], row < 4, 4, 0) for r in range(4)]
        twice = [merge(one[r], one[r + 2], lax.rem(row, 4) < 2, 2, 0) for r in range(2)]
        tall.append(merge(twice[0], twice[1], lax.rem(row, 2) < 1, 1, 0))
    half = [merge(tall[q], tall[q + 2], lane < 64, 64, 1) for q in range(2)]
    whole = merge(half[0], half[1], lax.rem(lane, 64) < 32, 32, 1)
    for s in (16, 8, 4, 2, 1):
        whole = add_pair(whole, [pltpu.roll(u, LANES - s, 1) for u in whole])
    spread = [pltpu.roll(u, 0, 1, stride=1, stride_axis=0) for u in whole]
    keep = lax.rem(lane, 32) == row
    flat = jnp.where(keep, spread[0], 0.0) + pltpu.roll(jnp.where(keep, spread[1], 0.0), 8, 1)
    sums[me] = jnp.sum(flat, axis=0, keepdims=True)

    def share(k, start):
        copy = pltpu.make_async_remote_copy(
            src_ref=sums.at[me],
            dst_ref=sums.at[me],
            send_sem=sum_send.at[0],
            recv_sem=sum_recv.at[0],
            **where_is(other(k)),
        )
        copy.start()

    loop(total - 1, lambda k: share(k + 1, True))

    stride = plan.stride
    for k in range(1, 7):
        for x in range(ngx):
            g, d = x // mixed, x % mixed
            out = None
            for c in range(3):
                for i in range(sx):
                    e = c * sx + i
                    s = (e * stride - ((d * sx + i) * pitch + halo)) % LANES
                    v = basis[k, c, g]
                    moved = pltpu.roll(v, s, 1) if s else v
                    out = moved if out is None else jnp.where(wide_lane >= e * stride, moved, out)
            for y in range(ngy):
                back[x, y, k - 1] = out[sy * y : sy * (y + 1)]

    own_low = lax.div(own * worker, sz)
    own_high = lax.div(jnp.minimum(own * worker + own, plan.nz) - 1, sz)
    straddles = sz % own != 0

    def give(q, start):
        x, y = (q // ngy, q % ngy) if isinstance(q, int) else (lax.div(q, ngy), lax.rem(q, ngy))

        def to(z):
            d = q * ngz + z
            dst = vt.at[worker - pick(plan.from_low, z)]
            remote = pltpu.make_async_remote_copy(
                src_ref=back.at[x, y],
                dst_ref=dst,
                send_sem=back_send.at[0],
                recv_sem=back_recv.at[0],
                **where_is(d),
            )
            if start:
                when(d != me, remote.start)
                when(
                    d == me,
                    lambda: pltpu.make_async_copy(back.at[x, y], dst, back_recv.at[0]).start(),
                )
            else:
                when(d != me, remote.wait_send)

        to(own_low)
        if straddles:
            when(own_high > own_low, lambda: to(own_high))

    loop(n, lambda q: give(q, True))
    fetched[5].wait()

    counts = [b - a + 1 for a, b in zip(plan.from_low, plan.from_high)]
    if min(counts) == plan.returns:
        settle(vt, back_recv.at[0])
    else:
        for z in range(ngz):
            when(gz == z, lambda z=z: settle(vt.at[pl.ds(0, counts[z])], back_recv.at[0]))

    mates = [(k, c, i) for k in range(0, 6, 2) for c in range(3) for i in range(sx)]

    def collect(j, accs):
        w = pick(plan.from_low, gz) + j
        offset = own * w - sz * gz
        inside = (lane >= offset) & (lane < offset + own)
        if min(counts) != plan.returns:
            inside = inside & (j < pick(counts, gz))
        new = []
        stacked = [jnp.concatenate([vt[j, k], vt[j, k + 1]], axis=0) for k in range(0, 6, 2)]
        for (k, c, i), acc in zip(mates, accs):
            s = lax.rem(offset - (c * sx + i) * stride + 2 * LANES, LANES)
            moved = pltpu.roll(stacked[k // 2], s, 1)
            new.append(jnp.where(inside, moved, acc))
        return tuple(new)

    accs = tuple(jnp.zeros((8, LANES), F32) for _ in mates)
    if plan.returns <= 16:
        for j in range(plan.returns):
            accs = collect(j, accs)
    else:
        accs = lax.fori_loop(0, plan.returns, collect, accs)

    settle(sums.at[pl.ds(0, total - 1)], sum_recv.at[0])

    def reduce_sums():
        def piece_of(d):
            v = sums[d]
            return v, pltpu.roll(v, LANES - 8, 1)

        if total <= 32:
            level = [piece_of(d) for d in range(total)]
            while len(level) > 1:
                nxt = [add_pair(level[a], level[a + 1]) for a in range(0, len(level) - 1, 2)]
                level = nxt + ([level[-1]] if len(level) % 2 else [])
            return level[0]
        zero = jnp.zeros((1, LANES), F32)
        return lax.fori_loop(0, total, lambda d, a: add_pair(a, piece_of(d)), (zero, zero))

    gram_high, gram_low = reduce_sums()
    gram_high, gram_low = two_sum(gram_high, gram_low)
    real = lax.rem(lax.broadcasted_iota(jnp.int32, (1, LANES), 1), 32) < 8
    gram_high = jnp.broadcast_to(jnp.where(real, gram_high, 0.0), (8, LANES))
    gram_low = jnp.broadcast_to(jnp.where(real, gram_low, 0.0), (8, LANES))

    def entry(i, j):
        s = place(PRODUCTS.index((min(i, j), max(i, j))))
        return pltpu.roll(gram_high, LANES - s, 1) if s else gram_high

    first_gram = [
        [HALF_WIDTH * entry(i, j + 1) + CHAIN[j] * entry(i, j) for j in range(3)]
        for i in range(3)
    ]
    c = solve_small(first_gram, [entry(i, 0) for i in range(3)])
    c = [jnp.broadcast_to(v[:, 0:1], (8, LANES)) for v in c]

    def affine(load_at):
        return ((load_at(0) + c_now[0] * load_at(1)) + c_now[1] * load_at(2)) + c_now[2] * load_at(3)

    c_now = c
    done = []
    for v in range(2):
        side = [
            affine(lambda a, s=s: const[pl.ds((4 * s + a) * 16 + 8 * v, 8), :]) for s in range(4)
        ]
        weight = add_pair(two_product(side[0], side[3]), two_product(side[1], side[2]))
        high_part, low_part = two_product(gram_high, weight[0])
        pair = (high_part, low_part + (gram_high * weight[1] + gram_low * weight[0]))
        for s in (64, 32, 4, 2, 1):
            pair = add_pair(pair, [pltpu.roll(u, LANES - s, 1) for u in pair])
        done.append(pair[0] + pair[1])

    def form(f):
        return jnp.broadcast_to(done[f // 8][f % 8 : f % 8 + 1], (8, LANES))

    d = solve_small([[form(3 * i + j) for j in range(3)] for i in range(3)], [form(9 + i) for i in range(3)])
    d = [jnp.broadcast_to(v[0:1, 0:1], (1, LANES)) for v in d]
    c_now = [v[0:1] for v in c]
    tail = 16 * 16
    coef = affine(lambda a: const[pl.ds(tail + a, 1), :])
    for j in range(3):
        coef = coef + d[j] * affine(lambda a: const[pl.ds(tail + 4 + 4 * j + a, 1), :])

    def spread_coef(k):
        return jnp.broadcast_to(coef[:, k : k + 1], (8, LANES))

    for slot in range(2):
        w = [spread_coef(16 * slot + k) for k in range(7)]
        duo = [jnp.where(row < sy, w[k + 1], w[k + 2]) for k in range(0, 6, 2)]
        for cc in range(3):
            for i in range(sx):
                v = None
                for k in range(0, 6, 2):
                    u = duo[k // 2] * accs[mates.index((k, cc, i))]
                    v = u if v is None else v + u
                start_part = raw[3 + cc, i] * raw[7, i]
                out_ref[slot, cc, i] = w[0][0:sy] * start_part + (v[0:sy] + v[sy : 2 * sy])

    loop(plan.sends, lambda j: piece(j, False))
    loop(n, lambda q: give(q, False))
    settle(sums.at[pl.ds(0, total - 1)], sum_send.at[0])


def per_device(displacement, load, material, free_node, table):
    shard = displacement.shape[1:]
    sx, sy, sz = shard
    grid = tuple(lax.axis_size(a) for a in ("gx", "gy", "gz"))
    plan = Plan(grid, shard)
    ngx, ngy, ngz = grid
    ny = ngy * sy
    groups = plan.groups
    const = jnp.asarray(tables())
    buffers = [
        pltpu.VMEM((FIELDS, sx, sy, sz), F32),
        pltpu.VMEM((2, sx, sy, sz), jnp.int32),
        pltpu.VMEM((plan.sends, plan.tiles, sy, LANES), F32),
        pltpu.VMEM((2, plan.tiles, ngx, ngy, sy, LANES), F32),
        pltpu.VMEM((7, 3, groups, ny, LANES), F32),
        pltpu.VMEM((3, groups, ny, LANES), F32),
        pltpu.VMEM((17, groups, ny, LANES), F32),
        pltpu.VMEM((2, 7, 3 * groups * ny // 8, 8, LANES), F32),
        pltpu.VMEM((ngx, ngy, 6, sy, LANES), F32),
        pltpu.VMEM((plan.returns, 6, sy, LANES), F32),
        pltpu.VMEM((plan.n * ngz, 1, LANES), F32),
        pltpu.VMEM(const.shape, F32),
        pltpu.SMEM(table.shape[::-1], F32),
        pltpu.SemaphoreType.DMA((6,)),
        pltpu.SemaphoreType.DMA((1,)),
        pltpu.SemaphoreType.DMA((2,)),
        pltpu.SemaphoreType.DMA((1,)),
        pltpu.SemaphoreType.DMA((1,)),
        pltpu.SemaphoreType.DMA((1,)),
        pltpu.SemaphoreType.DMA((1,)),
    ]
    operands = (displacement, load, material, free_node, table.T, const)
    both = pl.pallas_call(
        functools.partial(kernel, plan),
        out_shape=jax.ShapeDtypeStruct((2,) + displacement.shape, F32),
        in_specs=[pl.BlockSpec(memory_space=pltpu.HBM)] * 6,
        out_specs=pl.BlockSpec(memory_space=pltpu.VMEM),
        scratch_shapes=buffers,
        compiler_params=pltpu.CompilerParams(
            collective_id=0, has_side_effects=True, vmem_limit_bytes=32 << 20
        ),
    )(*(pltpu.with_memory_space_constraint(a, pltpu.HBM) for a in operands))
    return both[0], both[1]


def solution(mesh):
    in_specs = (
        P(None, "gx", "gy", "gz"),
        P(None, "gx", "gy", "gz"),
        P("gx", "gy", "gz"),
        P("gx", "gy", "gz"),
        P(),
    )
    out_specs = (P(None, "gx", "gy", "gz"), P(None, "gx", "gy", "gz"))
    return jax.shard_map(
        per_device, mesh=mesh, in_specs=in_specs, out_specs=out_specs, check_vma=False
    )
```

```python
import functools

import jax
import jax.numpy as jnp
import numpy as np
from jax import lax
from jax.experimental import pallas as pl
from jax.experimental.pallas import tpu as pltpu
from jax.sharding import PartitionSpec as P

SHIFTS = (9.6, 51.4)
HALF_WIDTH = 29.5
CHAIN = SHIFTS + (30.5,) + SHIFTS + (30.5,)
STEPS = 6
FIELDS = 8
LANES = 128
PRODUCTS = [(i, j) for i in range(7) for j in range(i, 7) if i < 6]
F32 = jnp.float32


def place(t):
    return 32 * (t // 8) + t % 8


def bits(x):
    top = np.asarray(x, np.float32)
    t = np.float32(4097.0) * top
    high = t - (t - top)
    return high, top - high, (x - top.astype(np.float64)).astype(np.float32)


def tables():
    width = 1.0 / np.float64(np.float32(1.0 / HALF_WIDTH))
    chain = np.array([np.float64(np.float32(x / HALF_WIDTH)) * width for x in CHAIN] + [0.0])

    def shifted(x):
        return np.concatenate([[0.0], x[:-1]])

    def times(x):
        return chain * x + width * shifted(x)

    unit = np.eye(7)
    b = [[unit[0]] + [-times(unit[j]) for j in range(3)]]
    for j in range(2):
        b.append([(times(x) - SHIFTS[j] * x) / HALF_WIDTH for x in b[j]])
    forms = [(i, j) for i in range(3) for j in range(3)] + [(i, None) for i in range(3)]
    wide = np.zeros((6, 4, 16, LANES))
    turn = np.zeros((3, 16, LANES))
    for f, (i, j) in enumerate(forms):
        for t, (one, two) in enumerate(PRODUCTS):
            at = place(t)
            turn[:, f, at] = (1.0, 1.0, 0.0) if j is None else (chain[one], chain[two], width)
            for a in range(4):
                left, right = b[i][a], b[j or 0][a]
                wide[0, a, f, at] = left[one]
                wide[1, a, f, at] = left[two] if one != two else 0.0
                wide[2, a, f, at] = right[one]
                wide[3, a, f, at] = right[two]
                wide[4, a, f, at] = shifted(right)[one]
                wide[5, a, f, at] = shifted(right)[two]
    last = np.zeros((2, 4, 8, LANES))
    final = np.zeros((2, 8, LANES))
    for k in range(7):
        final[:, :3, k] = np.array([[chain[k]], [width]])
        final[0, :3, 32 + k] = 1.0
        final[0, 3, k] = final[0, 3, 32 + k] = 1.0
        for a in range(4):
            for j in range(3):
                last[0, a, j, k] = last[0, a, j, 32 + k] = b[j][a][k]
                last[1, a, j, k] = shifted(b[j][a])[k]
            last[0, a, 3, k] = b[0][a][k]
            last[0, a, 3, 32 + k] = -1.0 if 0 < a == k + 1 else 0.0
    blocks = [wide, *(np.stack(bits(x)) for x in turn), last, *(np.stack(bits(x)) for x in final)]
    return np.concatenate([x.reshape(-1, LANES).astype(np.float32) for x in blocks])


def solve_small(gram, right):
    sym = [[0.5 * (gram[i][j] + gram[j][i]) for j in range(3)] for i in range(3)]
    l00 = jnp.sqrt(sym[0][0])
    l10 = sym[1][0] / l00
    l20 = sym[2][0] / l00
    l11 = jnp.sqrt(sym[1][1] - l10 * l10)
    l21 = (sym[2][1] - l20 * l10) / l11
    l22 = jnp.sqrt(sym[2][2] - l20 * l20 - l21 * l21)
    y0 = right[0] / l00
    y1 = (right[1] - l10 * y0) / l11
    y2 = (right[2] - l20 * y0 - l21 * y1) / l22
    c2 = y2 / l22
    c1 = (y1 - l21 * c2) / l11
    c0 = (y0 - l10 * c1 - l20 * c2) / l00
    return [c0, c1, c2]


def two_sum(a, b):
    s = a + b
    t = s - a
    return s, (a - (s - t)) + (b - t)


def add_pair(p, q):
    s, e = two_sum(p[0], q[0])
    return s, e + (p[1] + q[1])


def split(a):
    t = 4097.0 * a
    high = t - (t - a)
    return high, a - high


def two_product(a, b):
    p = a * b
    (ah, al), (bh, bl) = split(a), split(b)
    return p, ((ah * bh - p) + ah * bl + al * bh) + al * bl


def loop(count, body):
    if count <= 32:
        for i in range(count):
            body(i)
    else:

        def step(i, carry):
            body(i)
            return carry

        lax.fori_loop(0, count, step, 0)


def when(condition, body):
    if isinstance(condition, bool):
        if condition:
            body()
    else:
        pl.when(condition)(body)


class Plan:
    def __init__(self, grid, shard):
        self.grid, self.shard = grid, shard
        ngx, ngy, ngz = grid
        sx, sy, sz = shard
        self.n = ngx * ngy
        self.nz = ngz * sz
        self.halo = STEPS
        total = self.n * ngz
        self.pitch = 1 << (-(-self.nz // total) + 2 * self.halo - 1).bit_length()
        spare = total - -(-self.nz // (self.pitch - 2 * self.halo))
        self.counts = [self.n] * (ngz - 1) + [max(2, self.n - spare)]
        self.own = -(-self.nz // sum(self.counts))
        self.span = self.own + 2 * self.halo
        self.hops = [q // ngy + q % ngy // 2 for q in range(self.n)]
        far = max(self.hops) + ngz
        self.within = [sum(h + z <= k for h in self.hops for z in range(ngz)) for k in range(far)]
        self.packed = LANES // self.pitch
        self.groups = ngx * sx // self.packed
        self.mixed = LANES // (sx * self.pitch)
        self.tiles = FIELDS // self.mixed
        self.stride = LANES // (3 * sx)
        self.workers = -(-self.nz // self.own)
        self.base = [sum(self.counts[:z]) for z in range(ngz)]
        own, halo = self.own, self.halo
        self.to_low = [max(0, (sz * z - own - halo) // own + 1) for z in range(ngz)]
        self.to_high = [
            min(self.workers - 1, -(-(sz * z + sz + halo) // own) - 1) for z in range(ngz)
        ]
        self.from_low = [sz * z // own for z in range(ngz)]
        self.from_high = [(sz * z + sz - 1) // own for z in range(ngz)]
        self.sends = max(b - a + 1 for a, b in zip(self.to_low, self.to_high))
        self.returns = max(b - a + 1 for a, b in zip(self.from_low, self.from_high))
        assert sz == LANES and 8 == 2 * sy and own <= self.stride and LANES % self.pitch == 0


def pick(values, z):
    if all(v == values[0] for v in values):
        return values[0]
    out = values[0]
    for k in range(1, len(values)):
        out = jnp.where(z >= k, values[k], out)
    return out


def kernel(
    plan,
    disp_hbm,
    load_hbm,
    mat_hbm,
    free_hbm,
    table_hbm,
    const_hbm,
    out_ref,
    raw,
    flags,
    pack,
    recv,
    basis,
    fields,
    state,
    parts,
    back,
    vt,
    sums,
    const,
    table_ref,
    in_sem,
    send_sem,
    recv_sem,
    back_send,
    back_recv,
    sum_send,
    sum_recv,
    entered,
):
    ngx, ngy, ngz = plan.grid
    sx, sy, sz = plan.shard
    n, own, halo, pitch = plan.n, plan.own, plan.halo, plan.pitch
    nx, ny = ngx * sx, ngy * sy
    groups, mixed, tiles = plan.groups, plan.mixed, plan.tiles
    total = n * ngz
    gx, gy, gz = lax.axis_index("gx"), lax.axis_index("gy"), lax.axis_index("gz")
    p = gx * ngy + gy
    me = p * ngz + gz
    count = pick(plan.counts, gz)
    worker = pick(plan.base, gz) + count - 1 - p
    is_worker = (p < count) & (worker < plan.workers)
    first = own * worker - halo
    settled = jnp.maximum(first, 0)
    low_slab = jnp.minimum(lax.div(settled, sz), ngz - 1)
    edge = sz * (low_slab + 1)
    two = (first + plan.span > edge) & (low_slab + 1 < ngz)
    my_hops = pick(plan.hops, p) + gz

    fetched = [
        pltpu.make_async_copy(disp_hbm, raw.at[pl.ds(0, 3)], in_sem.at[0]),
        pltpu.make_async_copy(load_hbm, raw.at[pl.ds(3, 3)], in_sem.at[1]),
        pltpu.make_async_copy(mat_hbm, flags.at[0], in_sem.at[2]),
        pltpu.make_async_copy(free_hbm, flags.at[1], in_sem.at[3]),
        pltpu.make_async_copy(table_hbm, table_ref, in_sem.at[4]),
        pltpu.make_async_copy(const_hbm, const, in_sem.at[5]),
    ]
    for copy in fetched:
        copy.start()

    def where_is(d):
        return dict(device_id=d, device_id_type=pl.DeviceIdType.LOGICAL)

    def hops_of(d):
        q, z = d // ngz, d % ngz
        return q // ngy + q % ngy // 2 + z

    barrier = pltpu.get_barrier_semaphore()

    def greet(d):
        pl.semaphore_signal(barrier, inc=1, **where_is(d))

    def greet_slab(z):
        def one(q):
            d = q * ngz + z
            when(pick(plan.hops, q) + z < my_hops, lambda: greet(d))

        loop(n, one)

    when(is_worker, lambda: greet_slab(low_slab))
    when(is_worker & two, lambda: greet_slab(low_slab + 1))
    loop(total, lambda d: when((hops_of(d) >= my_hops) & (me != d), lambda: greet(d)))

    for copy in fetched[:4]:
        copy.wait()
    raw[6] = flags[0].astype(F32)
    raw[7] = flags[1].astype(F32)

    lane = lax.broadcasted_iota(jnp.int32, (8, LANES), 1)
    row = lax.broadcasted_iota(jnp.int32, (8, LANES), 0)
    per = 8 // sy
    stacks = -(-tiles // per)
    held = []
    for t in range(stacks):
        part = []
        for e in range(mixed * sx):
            f, i = e // sx, e % sx
            rows = [raw[mixed * min(per * t + h, tiles - 1) + f, i] for h in range(per)]
            part.append(jnp.concatenate(rows, axis=0))
        held.append(part)

    to_low = pick(plan.to_low, gz)
    to_count = pick([b - a + 1 for a, b in zip(plan.to_low, plan.to_high)], gz)

    def route(j):
        w = to_low + j
        z = 0
        for k in range(1, ngz):
            z = z + jnp.where(w >= plan.base[k], 1, 0)
        q = pick([b + c - 1 for b, c in zip(plan.base, plan.counts)], z) - w
        slot = jnp.where(sz * gz > jnp.maximum(own * w - halo, 0), 1, 0)
        return j < to_count, slot, q * ngz + z, pick(plan.hops, q) + z

    def prepare(j):
        w = to_low + j
        offset = sz * gz - (own * w - halo)
        for t in range(stacks):
            out = None
            for e, v in enumerate(held[t]):
                moved = pltpu.roll(v, lax.rem(offset + (pitch * e + 8 * LANES), LANES), 1)
                out = moved if out is None else jnp.where(lane >= pitch * e, moved, out)
            for h in range(min(per, tiles - per * t)):
                pack[j, per * t + h] = out[sy * h : sy * (h + 1)]

    loop(plan.sends, prepare)

    expected = pick(plan.within, my_hops) - 1
    if plan.sends <= 32:
        routes = [route(j) for j in range(plan.sends)]
        for valid, _, _, hops in routes:
            expected = expected + jnp.where(valid & (hops > my_hops), 1, 0)
    else:
        routes = None

        def count_late(j, late):
            valid, _, _, hops = route(j)
            return late + jnp.where(valid & (hops > my_hops), 1, 0)

        expected = lax.fori_loop(0, plan.sends, count_late, expected)
    pl.semaphore_wait(barrier, expected)

    def piece(j, start):
        valid, slot, d, _ = routes[j] if routes else route(j)
        dst = recv.at[slot, :, gx, gy]
        remote = pltpu.make_async_remote_copy(
            src_ref=pack.at[j],
            dst_ref=dst,
            send_sem=send_sem.at[0],
            recv_sem=recv_sem.at[slot],
            **where_is(d),
        )
        if start:
            when(valid & (d != me), remote.start)
            when(
                valid & (d == me),
                lambda: pltpu.make_async_copy(pack.at[j], dst, recv_sem.at[slot]).start(),
            )
        else:
            when(valid & (d != me), remote.wait_send)

    loop(plan.sends, lambda j: piece(j, True))
    loop(
        total,
        lambda d: when(
            hops_of(d) < my_hops,
            lambda: pl.semaphore_signal(entered, inc=1, **where_is(d)),
        ),
    )

    def settle(ref, sem):
        pltpu.make_async_copy(ref, ref, sem).wait()

    def work():
        settle(recv.at[0], recv_sem.at[0])
        when(two, lambda: settle(recv.at[1], recv_sem.at[1]))

        wide_lane = lax.broadcasted_iota(jnp.int32, (ny, LANES), 1)
        depth = lax.rem(wide_lane, pitch)
        plane = depth + first
        near = plane < edge
        seg = sx * pitch

        def gather_rows(slot, k, x):
            return jnp.concatenate([recv[slot, k, x, g] for g in range(ngy)], axis=0)

        def source(k, x):
            return jnp.where(near, gather_rows(0, k, x), gather_rows(1, k, x))

        def unpack(k, g):
            parts_in = [source(k, g * mixed + d) for d in range(mixed)]
            out = []
            for f in range(mixed):
                v = None
                for d in range(mixed):
                    s = (d - f) * seg % LANES
                    moved = pltpu.roll(parts_in[d], s, 1) if s else parts_in[d]
                    v = moved if v is None else jnp.where(wide_lane >= d * seg, moved, v)
                out.append(v)
            return out

        got = [[None] * groups for _ in range(FIELDS)]
        for g in range(groups):
            for k in range(tiles):
                for f, v in enumerate(unpack(k, g)):
                    got[mixed * k + f][g] = v

        span = range(groups)

        def next_z(a):
            return [pltpu.roll(v, LANES - 1, 1) for v in a]

        def last_z(a):
            return [pltpu.roll(v, 1, 1) for v in a]

        def next_y(a):
            return [pltpu.roll(v, ny - 1, 0) for v in a]

        def last_y(a):
            return [pltpu.roll(v, 1, 0) for v in a]

        def next_x(a):
            moved = [pltpu.roll(v, LANES - pitch, 1) for v in a]
            if groups == 1:
                return moved
            return [
                jnp.where(wide_lane >= LANES - pitch, moved[min(g + 1, groups - 1)], moved[g])
                for g in span
            ]

        def last_x(a):
            moved = [pltpu.roll(v, pitch, 1) for v in a]
            if groups == 1:
                return moved
            return [jnp.where(wide_lane < pitch, moved[max(g - 1, 0)], moved[g]) for g in span]

        def both(op, *lists):
            return [op(*vs) for vs in zip(*lists)]

        add = functools.partial(both, lambda a, b: a + b)
        sub = functools.partial(both, lambda a, b: a - b)

        def gradient(vector):
            grad = []
            for v in vector:
                moved = next_z(v)
                total_z, change = add(v, moved), sub(moved, v)
                shifted = next_y(total_z)
                flat, tilt, rise = add(total_z, shifted), sub(shifted, total_z), add(change, next_y(change))
                grad.append(
                    [sub(next_x(flat), flat), add(next_x(tilt), tilt), add(next_x(rise), rise)]
                )
            return grad

        pairs = [(0, 0), (0, 1), (0, 2), (1, 1), (1, 2), (2, 2)]
        free = got[7]
        for c in range(3):
            for g in span:
                basis[0, c, g] = got[3 + c][g] * free[g]
        grad = gradient([got[0], got[1], got[2]])
        mass = []
        high = lax.broadcasted_iota(jnp.int32, (ny, LANES), 0)
        for g in span:
            valid = (high <= ny - 2) & (plane >= 0) & (plane <= plan.nz - 2) & (depth <= plan.span - 2)
            valid = valid & (lax.div(wide_lane, pitch) + g * plan.packed <= nx - 2)
            material = got[6][g]
            zero = jnp.zeros((ny, LANES), F32)
            lame, shear, heavy = zero, zero, zero
            for r in range(table_ref.shape[1]):
                hit = material == float(r)
                lame = jnp.where(hit, table_ref[0, r], lame)
                shear = jnp.where(hit, table_ref[1, r], shear)
                heavy = jnp.where(hit, table_ref[2, r], heavy)
            lame = jnp.where(valid, lame * 0.0625, 0.0)
            shear = jnp.where(valid, shear * 0.0625, 0.0)
            mass.append(jnp.where(valid, heavy * 0.125, 0.0))
            frame = [
                [0.25 * grad[i][j][g] + (1.0 if i == j else 0.0) for j in range(3)] for i in range(3)
            ]
            strain = {}
            for i, j in pairs:
                v = sum(frame[k][i] * frame[k][j] for k in range(3))
                strain[i, j] = 0.5 * (v - 1.0 if i == j else v)
            bulk = lame * (strain[0, 0] + strain[1, 1] + strain[2, 2])
            for i in range(3):
                for j in range(3):
                    state[3 * i + j, g] = frame[i][j]
            for spot, (i, j) in enumerate(pairs):
                v = 2.0 * shear * strain[i, j]
                state[9 + spot, g] = v + bulk if i == j else v
            state[15, g] = lame
            state[16, g] = shear
        mass = add(mass, last_x(mass))
        mass = add(mass, last_y(mass))
        mass = add(mass, last_z(mass))
        for g in span:
            fields[0, g] = free[g]
            fields[1, g] = free[g] * (1.0 / HALF_WIDTH)
            fields[2, g] = (free[g] * mass[g] + (1.0 - free[g])) * (1.0 / HALF_WIDTH)

        rows8 = [pl.ds(8 * r, 8) for r in range(ny // 8)]

        def apply(j):
            grad = gradient([[basis[j, c, g] * fields[0, g] for g in span] for c in range(3)])
            pio = [[[[None] * len(rows8) for _ in span] for _ in range(3)] for _ in range(3)]
            for g in span:
                for r, at in enumerate(rows8):
                    d = [[grad[c][q][g][8 * r : 8 * r + 8] for q in range(3)] for c in range(3)]
                    f = [[state[3 * i + k, g, at] for k in range(3)] for i in range(3)]
                    pulled = [
                        [sum(f[k][a] * d[k][b] for k in range(3)) for b in range(3)] for a in range(3)
                    ]
                    lame, shear = state[15, g, at], state[16, g, at]
                    bulk = lame * (pulled[0][0] + pulled[1][1] + pulled[2][2])
                    t, s = {}, {}
                    for spot, (a, b) in enumerate(pairs):
                        v = shear * (pulled[a][b] + pulled[b][a])
                        t[a, b] = t[b, a] = v + bulk if a == b else v
                        s[a, b] = s[b, a] = state[9 + spot, g, at]
                    for i in range(3):
                        for b in range(3):
                            v = sum(f[i][k] * t[k, b] for k in range(3))
                            pio[i][b][g][r] = v + sum(d[i][k] * s[k, b] for k in range(3))
            for c in range(3):
                e = [[jnp.concatenate(pio[c][b][g], axis=0) for g in span] for b in range(3)]
                across = sub(last_x(e[0]), e[0])
                along = add(last_x(e[1]), e[1])
                up = add(last_x(e[2]), e[2])
                flat = add(last_y(add(across, along)), sub(across, along))
                up = add(up, last_y(up))
                out = add(last_z(add(flat, up)), sub(flat, up))
                for g in span:
                    basis[j + 1, c, g] = fields[1, g] * out[g] + (
                        fields[2, g] - CHAIN[j] / HALF_WIDTH
                    ) * basis[j, c, g]

        for j in range(STEPS):
            apply(j)

        mine = (depth >= halo) & (depth < halo + own) & (plane < plan.nz)
        spots = [(c, g, r) for c in range(3) for g in span for r in range(ny // 8)]
        for k in range(7):
            v = [
                jnp.where(mine[8 * r : 8 * r + 8], basis[k, c, g, rows8[r]], 0.0) for c, g, r in spots
            ]
            top = jnp.abs(v[0])
            for u in v[1:]:
                top = jnp.maximum(top, jnp.abs(u))
            grain = top * (32768.0 * max(1, len(v) // 6))
            for s, u in enumerate(v):
                coarse = (u + grain) - grain
                parts[0, k, s] = coarse
                parts[1, k, s] = u - coarse
        pairs_of = {}
        for i in range(6):
            acc = {j: [None, None] for j in range(i, 7)}
            for s in range(len(spots)):
                ch, cl = parts[0, i, s], parts[1, i, s]
                for j in range(i, 7):
                    dh, dl = parts[0, j, s], parts[1, j, s]
                    new = [ch * dh, cl * (dh + ch + dl) if i == j else ch * dl + cl * (dh + dl)]
                    acc[j] = new if s == 0 else [acc[j][0] + new[0], acc[j][1] + new[1]]
            for j in range(i, 7):
                pairs_of[i, j] = acc[j]
        items = [tuple(pairs_of[q]) for q in PRODUCTS]
        blank = (jnp.zeros((8, LANES), F32), jnp.zeros((8, LANES), F32))
        items = items + [blank] * (32 - len(items))

        def merge(a, b, mask, shift, axis):
            size = 8 if axis == 0 else LANES
            first_in, second_in = [], []
            for u, v in zip(a, b):
                if 2 * shift == size:
                    first_in.append(jnp.where(mask, u, v))
                    second_in.append(pltpu.roll(jnp.where(mask, v, u), shift, axis))
                else:
                    first_in.append(jnp.where(mask, u, pltpu.roll(v, shift, axis)))
                    second_in.append(jnp.where(mask, pltpu.roll(u, size - shift, axis), v))
            return add_pair(first_in, second_in)

        tall = []
        for q in range(4):
            it = items[8 * q : 8 * q + 8]
            one = [merge(it[r], it[r + 4], row < 4, 4, 0) for r in range(4)]
            twice = [merge(one[r], one[r + 2], lax.rem(row, 4) < 2, 2, 0) for r in range(2)]
            tall.append(merge(twice[0], twice[1], lax.rem(row, 2) < 1, 1, 0))
        half = [merge(tall[q], tall[q + 2], lane < 64, 64, 1) for q in range(2)]
        whole = merge(half[0], half[1], lax.rem(lane, 64) < 32, 32, 1)
        for s in (16, 8, 4, 2, 1):
            whole = add_pair(whole, [pltpu.roll(u, LANES - s, 1) for u in whole])
        spread = [pltpu.roll(u, 0, 1, stride=1, stride_axis=0) for u in whole]
        keep = lax.rem(lane, 32) == row
        flat = jnp.where(keep, spread[0], 0.0) + pltpu.roll(jnp.where(keep, spread[1], 0.0), 8, 1)
        sums[worker] = jnp.sum(flat, axis=0, keepdims=True)

    fetched[4].wait()
    when(is_worker, work)
    late = total - pick(plan.within, my_hops)
    when(late > 0, lambda: pl.semaphore_wait(entered, late))

    stride = plan.stride

    def share(d):
        when(
            me != d,
            pltpu.make_async_remote_copy(
                src_ref=sums.at[worker],
                dst_ref=sums.at[worker],
                send_sem=sum_send.at[0],
                recv_sem=sum_recv.at[0],
                **where_is(d),
            ).start,
        )

    def give_back():
        loop(total, share)
        wide_lane = lax.broadcasted_iota(jnp.int32, (ny, LANES), 1)
        for k in range(1, 7):
            for x in range(ngx):
                g, d = x // mixed, x % mixed
                out = None
                for c in range(3):
                    for i in range(sx):
                        e = c * sx + i
                        s = (e * stride - ((d * sx + i) * pitch + halo)) % LANES
                        v = basis[k, c, g]
                        moved = pltpu.roll(v, s, 1) if s else v
                        out = moved if out is None else jnp.where(wide_lane >= e * stride, moved, out)
                for y in range(ngy):
                    back[x, y, k - 1] = out[sy * y : sy * (y + 1)]
        loop(n, lambda q: give(q, True))

    own_low = jnp.minimum(lax.div(own * worker, sz), ngz - 1)
    own_high = lax.div(jnp.minimum(own * worker + own, plan.nz) - 1, sz)
    straddles = sz % own != 0

    def give(q, start):
        x, y = (q // ngy, q % ngy) if isinstance(q, int) else (lax.div(q, ngy), lax.rem(q, ngy))

        def to(z):
            d = q * ngz + z
            dst = vt.at[worker - pick(plan.from_low, z)]
            remote = pltpu.make_async_remote_copy(
                src_ref=back.at[x, y],
                dst_ref=dst,
                send_sem=back_send.at[0],
                recv_sem=back_recv.at[0],
                **where_is(d),
            )
            if start:
                when(d != me, remote.start)
                when(
                    d == me,
                    lambda: pltpu.make_async_copy(back.at[x, y], dst, back_recv.at[0]).start(),
                )
            else:
                when(d != me, remote.wait_send)

        to(own_low)
        if straddles:
            when(own_high > own_low, lambda: to(own_high))

    when(is_worker, give_back)
    fetched[5].wait()

    counts = [b - a + 1 for a, b in zip(plan.from_low, plan.from_high)]
    if min(counts) == plan.returns:
        settle(vt, back_recv.at[0])
    else:
        for z in range(ngz):
            when(gz == z, lambda z=z: settle(vt.at[pl.ds(0, counts[z])], back_recv.at[0]))

    mates = [(k, c, i) for k in range(0, 6, 2) for c in range(3) for i in range(sx)]

    def collect(j, accs):
        w = pick(plan.from_low, gz) + j
        offset = own * w - sz * gz
        inside = (lane >= offset) & (lane < offset + own)
        if min(counts) != plan.returns:
            inside = inside & (j < pick(counts, gz))
        new = []
        stacked = [jnp.concatenate([vt[j, k], vt[j, k + 1]], axis=0) for k in range(0, 6, 2)]
        for (k, c, i), acc in zip(mates, accs):
            s = lax.rem(offset - (c * sx + i) * stride + 2 * LANES, LANES)
            moved = pltpu.roll(stacked[k // 2], s, 1)
            new.append(jnp.where(inside, moved, acc))
        return tuple(new)

    accs = tuple(jnp.zeros((8, LANES), F32) for _ in mates)
    if plan.returns <= 16:
        for j in range(plan.returns):
            accs = collect(j, accs)
    else:
        accs = lax.fori_loop(0, plan.returns, collect, accs)

    active = plan.workers
    when(is_worker, lambda: settle(sums.at[pl.ds(0, active - 1)], sum_recv.at[0]))
    when(jnp.logical_not(is_worker), lambda: settle(sums, sum_recv.at[0]))

    def reduce_sums():
        def piece_of(d):
            v = sums[d]
            return v, pltpu.roll(v, LANES - 8, 1)

        if active <= 32:
            level = [piece_of(d) for d in range(active)]
            while len(level) > 1:
                nxt = [add_pair(level[a], level[a + 1]) for a in range(0, len(level) - 1, 2)]
                level = nxt + ([level[-1]] if len(level) % 2 else [])
            return level[0]
        zero = jnp.zeros((1, LANES), F32)
        return lax.fori_loop(0, active, lambda d, a: add_pair(a, piece_of(d)), (zero, zero))

    gram_high, gram_low = reduce_sums()
    gram_high, gram_low = two_sum(gram_high, gram_low)
    real = lax.rem(lax.broadcasted_iota(jnp.int32, (1, LANES), 1), 32) < 8
    gram_high = jnp.broadcast_to(jnp.where(real, gram_high, 0.0), (8, LANES))
    gram_low = jnp.broadcast_to(jnp.where(real, gram_low, 0.0), (8, LANES))

    def entry(i, j):
        s = place(PRODUCTS.index((min(i, j), max(i, j))))
        return pltpu.roll(gram_high, LANES - s, 1) if s else gram_high

    first_gram = [
        [HALF_WIDTH * entry(i, j + 1) + CHAIN[j] * entry(i, j) for j in range(3)]
        for i in range(3)
    ]
    c = solve_small(first_gram, [entry(i, 0) for i in range(3)])
    c = [jnp.broadcast_to(v[:, 0:1], (8, LANES)) for v in c]

    def affine(c, load_at):
        return ((load_at(0) + c[0] * load_at(1)) + c[1] * load_at(2)) + c[2] * load_at(3)

    def scaled(at, size, x):
        ch, cl, rest = (const[pl.ds(q, size), :] for q in at)
        xh, xl = split(x)
        p = (ch + cl) * x
        return p, (((ch * xh - p) + ch * xl + cl * xh) + cl * xl) + rest * x

    done = []
    for v in range(2):
        side = [
            affine(c, lambda a, s=s: const[pl.ds((4 * s + a) * 16 + 8 * v, 8), :])
            for s in range(6)
        ]
        turn = [[24 * 16 + (3 * q + part) * 16 + 8 * v for part in range(3)] for q in range(3)]
        image = [
            add_pair(scaled(turn[q], 8, side[2 + q]), scaled(turn[2], 8, side[4 + q]))
            for q in range(2)
        ]

        def times_pair(x, pair):
            p, e = two_product(x, pair[0])
            return p, e + x * pair[1]

        weight = add_pair(times_pair(side[0], image[1]), times_pair(side[1], image[0]))
        high_part, low_part = two_product(gram_high, weight[0])
        pair = (high_part, low_part + (gram_high * weight[1] + gram_low * weight[0]))
        for s in (64, 32, 4, 2, 1):
            pair = add_pair(pair, [pltpu.roll(u, LANES - s, 1) for u in pair])
        done.append(pair[0] + pair[1])

    def form(f):
        return jnp.broadcast_to(done[f // 8][f % 8 : f % 8 + 1], (8, LANES))

    gram = [[form(3 * i + j) for j in range(3)] for i in range(3)]
    d = solve_small(gram, [form(9 + i) for i in range(3)])
    d = [jnp.broadcast_to(v[:, 0:1], (8, LANES)) for v in d]
    base_at = 24 * 16 + 9 * 16
    vector = affine(c, lambda a: const[pl.ds(base_at + 8 * a, 8), :])
    moved = affine(c, lambda a: const[pl.ds(base_at + 32 + 8 * a, 8), :])
    turn = [[base_at + 64 + 8 * (3 * q + part) for part in range(3)] for q in range(2)]
    image = add_pair(scaled(turn[0], 8, vector), scaled(turn[1], 8, moved))
    factor = jnp.where(row == 0, -d[0], jnp.where(row == 1, -d[1], jnp.where(row == 2, -d[2], 1.0)))
    coef = times_pair(factor, image)
    coef = add_pair(coef, [pltpu.roll(u, 6, 0) for u in coef])
    coef = add_pair(coef, [pltpu.roll(u, 7, 0) for u in coef])
    coef = two_sum(coef[0][0:1], coef[1][0:1])

    def spread_coef(part, k):
        return jnp.broadcast_to(coef[part][:, k : k + 1], (8, LANES))

    for slot in range(2):
        sets = [[-spread_coef(0, 32 + k) for k in range(7)]]
        if slot == 1:
            sets = [[spread_coef(part, k) for k in range(7)] for part in range(2)]
        duo = [
            [jnp.where(row < sy, w[k + 1], w[k + 2]) for w in sets] for k in range(0, 6, 2)
        ]
        for cc in range(3):
            for i in range(sx):
                v = None
                for k in range(0, 6, 2):
                    held_k = accs[mates.index((k, cc, i))]
                    u = duo[k // 2][0] * held_k
                    for extra in duo[k // 2][1:]:
                        u = u + extra * held_k
                    v = u if v is None else v + u
                start_part = raw[3 + cc, i] * raw[7, i]
                head = sets[0][0][0:sy] * start_part
                for extra in sets[1:]:
                    head = head + extra[0][0:sy] * start_part
                out_ref[slot, cc, i] = head + (v[0:sy] + v[sy : 2 * sy])

    loop(plan.sends, lambda j: piece(j, False))

    def sent():
        loop(n, lambda q: give(q, False))
        left = total - 1
        while left:
            rows = min(left, active)
            settle(sums.at[pl.ds(0, rows)], sum_send.at[0])
            left -= rows

    when(is_worker, sent)


def per_device(displacement, load, material, free_node, table):
    shard = displacement.shape[1:]
    sx, sy, sz = shard
    grid = tuple(lax.axis_size(a) for a in ("gx", "gy", "gz"))
    plan = Plan(grid, shard)
    ngx, ngy, ngz = grid
    ny = ngy * sy
    groups = plan.groups
    const = jnp.asarray(tables())
    buffers = [
        pltpu.VMEM((FIELDS, sx, sy, sz), F32),
        pltpu.VMEM((2, sx, sy, sz), jnp.int32),
        pltpu.VMEM((plan.sends, plan.tiles, sy, LANES), F32),
        pltpu.VMEM((2, plan.tiles, ngx, ngy, sy, LANES), F32),
        pltpu.VMEM((7, 3, groups, ny, LANES), F32),
        pltpu.VMEM((3, groups, ny, LANES), F32),
        pltpu.VMEM((17, groups, ny, LANES), F32),
        pltpu.VMEM((2, 7, 3 * groups * ny // 8, 8, LANES), F32),
        pltpu.VMEM((ngx, ngy, 6, sy, LANES), F32),
        pltpu.VMEM((plan.returns, 6, sy, LANES), F32),
        pltpu.VMEM((plan.workers, 1, LANES), F32),
        pltpu.VMEM(const.shape, F32),
        pltpu.SMEM(table.shape[::-1], F32),
        pltpu.SemaphoreType.DMA((6,)),
        pltpu.SemaphoreType.DMA((1,)),
        pltpu.SemaphoreType.DMA((2,)),
        pltpu.SemaphoreType.DMA((1,)),
        pltpu.SemaphoreType.DMA((1,)),
        pltpu.SemaphoreType.DMA((1,)),
        pltpu.SemaphoreType.DMA((1,)),
        pltpu.SemaphoreType.REGULAR,
    ]
    operands = (displacement, load, material, free_node, table.T, const)
    both = pl.pallas_call(
        functools.partial(kernel, plan),
        out_shape=jax.ShapeDtypeStruct((2,) + displacement.shape, F32),
        in_specs=[pl.BlockSpec(memory_space=pltpu.HBM)] * 6,
        out_specs=pl.BlockSpec(memory_space=pltpu.VMEM),
        scratch_shapes=buffers,
        compiler_params=pltpu.CompilerParams(
            collective_id=0, has_side_effects=True, vmem_limit_bytes=32 << 20
        ),
    )(*(pltpu.with_memory_space_constraint(a, pltpu.HBM) for a in operands))
    return both[0], both[1]


def solution(mesh):
    in_specs = (
        P(None, "gx", "gy", "gz"),
        P(None, "gx", "gy", "gz"),
        P("gx", "gy", "gz"),
        P("gx", "gy", "gz"),
        P(),
    )
    out_specs = (P(None, "gx", "gy", "gz"), P(None, "gx", "gy", "gz"))
    return jax.shard_map(
        per_device, mesh=mesh, in_specs=in_specs, out_specs=out_specs, check_vma=False
    )
```

```python
import functools

import jax
import jax.numpy as jnp
import numpy as np
from jax import lax
from jax.experimental import pallas as pl
from jax.experimental.pallas import tpu as pltpu
from jax.sharding import PartitionSpec as P

SHIFTS = (9.6, 51.4)
HALF_WIDTH = 29.5
CHAIN = SHIFTS + (30.5,) + SHIFTS + (30.5,)
STEPS = 6
FIELDS = 8
LANES = 128
PRODUCTS = [(i, j) for i in range(7) for j in range(i, 7) if i < 6]
F32 = jnp.float32


def place(t):
    return 32 * (t // 8) + 8 + t % 8


def bits(x):
    top = np.asarray(x, np.float32)
    t = np.float32(4097.0) * top
    high = t - (t - top)
    return high, top - high, (x - top.astype(np.float64)).astype(np.float32)


def tables():
    width = 1.0 / np.float64(np.float32(1.0 / HALF_WIDTH))
    chain = np.array([np.float64(np.float32(x / HALF_WIDTH)) * width for x in CHAIN] + [0.0])

    def shifted(x):
        return np.concatenate([[0.0], x[:-1]])

    def times(x):
        return chain * x + width * shifted(x)

    unit = np.eye(7)
    b = [[unit[0]] + [-times(unit[j]) for j in range(3)]]
    for j in range(2):
        b.append([(times(x) - SHIFTS[j] * x) / HALF_WIDTH for x in b[j]])
    forms = [(i, j) for i in range(3) for j in range(3)] + [(i, None) for i in range(3)]
    wide = np.zeros((6, 4, 16, LANES))
    turn = np.zeros((3, 16, LANES))
    for f, (i, j) in enumerate(forms):
        for t, (one, two) in enumerate(PRODUCTS):
            at = place(t)
            turn[:, f, at] = (1.0, 1.0, 0.0) if j is None else (chain[one], chain[two], width)
            for a in range(4):
                left, right = b[i][a], b[j or 0][a]
                wide[0, a, f, at] = left[one]
                wide[1, a, f, at] = left[two] if one != two else 0.0
                wide[2, a, f, at] = right[one]
                wide[3, a, f, at] = right[two]
                wide[4, a, f, at] = shifted(right)[one]
                wide[5, a, f, at] = shifted(right)[two]
    last = np.zeros((2, 4, 8, LANES))
    final = np.zeros((2, 8, LANES))
    for k in range(7):
        final[:, :3, k] = np.array([[chain[k]], [width]])
        final[0, :3, 32 + k] = 1.0
        final[0, 3, k] = final[0, 3, 32 + k] = 1.0
        for a in range(4):
            for j in range(3):
                last[0, a, j, k] = last[0, a, j, 32 + k] = b[j][a][k]
                last[1, a, j, k] = shifted(b[j][a])[k]
            last[0, a, 3, k] = b[0][a][k]
            last[0, a, 3, 32 + k] = -1.0 if 0 < a == k + 1 else 0.0
    blocks = [wide, *(np.stack(bits(x)) for x in turn), last, *(np.stack(bits(x)) for x in final)]
    return np.concatenate([x.reshape(-1, LANES).astype(np.float32) for x in blocks])


def solve_small(gram, right):
    sym = [[0.5 * (gram[i][j] + gram[j][i]) for j in range(3)] for i in range(3)]
    r0 = 1.0 / sym[0][0]
    l10 = sym[1][0] * r0
    l20 = sym[2][0] * r0
    r1 = 1.0 / (sym[1][1] - l10 * sym[1][0])
    e = sym[2][1] - l20 * sym[1][0]
    l21 = e * r1
    d2 = sym[2][2] - l20 * sym[2][0] - l21 * e
    y1 = right[1] - l10 * right[0]
    c2 = (right[2] - l20 * right[0] - l21 * y1) / d2
    c1 = y1 * r1 - l21 * c2
    c0 = right[0] * r0 - l10 * c1 - l20 * c2
    return [c0, c1, c2]


def two_sum(a, b):
    s = a + b
    t = s - a
    return s, (a - (s - t)) + (b - t)


def add_pair(p, q):
    s, e = two_sum(p[0], q[0])
    return s, e + (p[1] + q[1])


def add_all(pairs):
    while len(pairs) > 1:
        rest = pairs[len(pairs) & ~1 :]
        pairs = [add_pair(p, q) for p, q in zip(pairs[::2], pairs[1::2])] + rest
    return pairs[0]


def split(a):
    t = 4097.0 * a
    high = t - (t - a)
    return high, a - high


def two_product(a, b):
    p = a * b
    (ah, al), (bh, bl) = split(a), split(b)
    return p, ((ah * bh - p) + ah * bl + al * bh) + al * bl


def loop(count, body):
    if count <= 32:
        for i in range(count):
            body(i)
    else:

        def step(i, carry):
            body(i)
            return carry

        lax.fori_loop(0, count, step, 0)


def when(condition, body):
    if isinstance(condition, bool):
        if condition:
            body()
    else:
        pl.when(condition)(body)


class Plan:
    def __init__(self, grid, shard):
        self.grid, self.shard = grid, shard
        ngx, ngy, ngz = grid
        sx, sy, sz = shard
        self.n = ngx * ngy
        self.nz = ngz * sz
        self.halo = STEPS
        total = self.n * ngz
        self.pitch = 1 << (-(-self.nz // total) + 2 * self.halo - 1).bit_length()
        spare = total - -(-self.nz // (self.pitch - 2 * self.halo))
        self.counts = [self.n] * (ngz - 1) + [max(2, self.n - spare)]
        self.own = -(-self.nz // sum(self.counts))
        self.span = self.own + 2 * self.halo
        self.packed = LANES // self.pitch
        self.groups = ngx * sx // self.packed
        self.mixed = LANES // (sx * self.pitch)
        self.tiles = FIELDS // self.mixed
        self.stride = LANES // (3 * sx)
        self.workers = -(-self.nz // self.own)
        self.base = [sum(self.counts[:z]) for z in range(ngz)]
        own, halo = self.own, self.halo
        self.to_low = [max(0, (sz * z - own - halo) // own + 1) for z in range(ngz)]
        self.to_high = [
            min(self.workers - 1, -(-(sz * z + sz + halo) // own) - 1) for z in range(ngz)
        ]
        self.from_low = [sz * z // own for z in range(ngz)]
        self.from_high = [(sz * z + sz - 1) // own for z in range(ngz)]
        self.sends = max(b - a + 1 for a, b in zip(self.to_low, self.to_high))
        self.returns = max(b - a + 1 for a, b in zip(self.from_low, self.from_high))
        assert sz == LANES and 8 == 2 * sy and own <= self.stride and LANES % self.pitch == 0


def pick(values, z):
    if all(v == values[0] for v in values):
        return values[0]
    out = values[0]
    for k in range(1, len(values)):
        out = jnp.where(z >= k, values[k], out)
    return out


def kernel(
    plan,
    disp_hbm,
    load_hbm,
    mat_hbm,
    free_hbm,
    table_hbm,
    const_hbm,
    out_ref,
    raw,
    flags,
    pack,
    recv,
    basis,
    fields,
    state,
    parts,
    back,
    vt,
    sums,
    const,
    table_ref,
    in_sem,
    send_sem,
    recv_sem,
    back_send,
    back_recv,
    sum_send,
    sum_recv,
    entered,
):
    ngx, ngy, ngz = plan.grid
    sx, sy, sz = plan.shard
    n, own, halo, pitch = plan.n, plan.own, plan.halo, plan.pitch
    nx, ny = ngx * sx, ngy * sy
    groups, mixed, tiles = plan.groups, plan.mixed, plan.tiles
    total = n * ngz
    gx, gy, gz = lax.axis_index("gx"), lax.axis_index("gy"), lax.axis_index("gz")
    p = gx * ngy + gy
    me = p * ngz + gz
    count = pick(plan.counts, gz)
    worker = pick(plan.base, gz) + count - 1 - p
    is_worker = (p < count) & (worker < plan.workers)
    first = own * worker - halo
    settled = jnp.maximum(first, 0)
    low_slab = jnp.minimum(lax.div(settled, sz), ngz - 1)
    edge = sz * (low_slab + 1)
    two = (first + plan.span > edge) & (low_slab + 1 < ngz)
    last = total - 1

    fetched = [
        pltpu.make_async_copy(disp_hbm, raw.at[pl.ds(0, 3)], in_sem.at[0]),
        pltpu.make_async_copy(load_hbm, raw.at[pl.ds(3, 3)], in_sem.at[1]),
        pltpu.make_async_copy(mat_hbm, flags.at[0], in_sem.at[2]),
        pltpu.make_async_copy(free_hbm, flags.at[1], in_sem.at[3]),
        pltpu.make_async_copy(table_hbm, table_ref, in_sem.at[4]),
        pltpu.make_async_copy(const_hbm, const, in_sem.at[5]),
    ]
    for copy in fetched:
        copy.start()

    def where_is(d):
        return dict(device_id=d, device_id_type=pl.DeviceIdType.LOGICAL)

    barrier = pltpu.get_barrier_semaphore()

    def greet(d):
        pl.semaphore_signal(barrier, inc=1, **where_is(d))

    def greet_slab(z):
        def one(q):
            d = q * ngz + z
            when((d != me) & (d != last), lambda: greet(d))

        loop(n, one)

    when(is_worker, lambda: greet_slab(low_slab))
    when(is_worker & two, lambda: greet_slab(low_slab + 1))
    when(me != last, lambda: greet(last))

    for copy in fetched[:4]:
        copy.wait()
    raw[6] = flags[0].astype(F32)
    raw[7] = flags[1].astype(F32)

    lane = lax.broadcasted_iota(jnp.int32, (8, LANES), 1)
    row = lax.broadcasted_iota(jnp.int32, (8, LANES), 0)
    per = 8 // sy
    stacks = -(-tiles // per)
    held = []
    for t in range(stacks):
        part = []
        for e in range(mixed * sx):
            f, i = e // sx, e % sx
            rows = [raw[mixed * min(per * t + h, tiles - 1) + f, i] for h in range(per)]
            part.append(jnp.concatenate(rows, axis=0))
        held.append(part)

    to_low = pick(plan.to_low, gz)
    to_count = pick([b - a + 1 for a, b in zip(plan.to_low, plan.to_high)], gz)

    def route(j):
        w = to_low + j
        z = 0
        for k in range(1, ngz):
            z = z + jnp.where(w >= plan.base[k], 1, 0)
        q = pick([b + c - 1 for b, c in zip(plan.base, plan.counts)], z) - w
        slot = jnp.where(sz * gz > jnp.maximum(own * w - halo, 0), 1, 0)
        return j < to_count, slot, q * ngz + z

    def prepare(j):
        w = to_low + j
        offset = sz * gz - (own * w - halo)
        for t in range(stacks):
            out = None
            for e, v in enumerate(held[t]):
                moved = pltpu.roll(v, lax.rem(offset + (pitch * e + 8 * LANES), LANES), 1)
                out = moved if out is None else jnp.where(lane >= pitch * e, moved, out)
            for h in range(min(per, tiles - per * t)):
                pack[j, per * t + h] = out[sy * h : sy * (h + 1)]

    loop(plan.sends, prepare)

    expected = to_count
    if plan.sends <= 32:
        routes = [route(j) for j in range(plan.sends)]
        for valid, _, d in routes:
            expected = expected - jnp.where(valid & (d == me), 1, 0)
    else:
        routes = None

        def count_self(j, seen):
            valid, _, d = route(j)
            return seen - jnp.where(valid & (d == me), 1, 0)

        expected = lax.fori_loop(0, plan.sends, count_self, expected)
    expected = jnp.where(me == last, total - 1, expected)
    pl.semaphore_wait(barrier, expected)

    def piece(j, start):
        valid, slot, d = routes[j] if routes else route(j)
        dst = recv.at[slot, :, gx, gy]
        remote = pltpu.make_async_remote_copy(
            src_ref=pack.at[j],
            dst_ref=dst,
            send_sem=send_sem.at[0],
            recv_sem=recv_sem.at[slot],
            **where_is(d),
        )
        if start:
            when(valid & (d != me), remote.start)
            when(
                valid & (d == me),
                lambda: pltpu.make_async_copy(pack.at[j], dst, recv_sem.at[slot]).start(),
            )
        else:
            when(valid & (d != me), remote.wait_send)

    loop(plan.sends, lambda j: piece(j, True))

    def announce():
        loop(total - 1, lambda d: pl.semaphore_signal(entered, inc=1, **where_is(d)))

    when(me == last, announce)

    def settle(ref, sem):
        pltpu.make_async_copy(ref, ref, sem).wait()

    def work():
        settle(recv.at[0], recv_sem.at[0])
        when(two, lambda: settle(recv.at[1], recv_sem.at[1]))

        wide_lane = lax.broadcasted_iota(jnp.int32, (ny, LANES), 1)
        depth = lax.rem(wide_lane, pitch)
        plane = depth + first
        near = plane < edge
        seg = sx * pitch

        def gather_rows(slot, k, x):
            return jnp.concatenate([recv[slot, k, x, g] for g in range(ngy)], axis=0)

        def source(k, x):
            return jnp.where(near, gather_rows(0, k, x), gather_rows(1, k, x))

        def unpack(k, g):
            parts_in = [source(k, g * mixed + d) for d in range(mixed)]
            out = []
            for f in range(mixed):
                v = None
                for d in range(mixed):
                    s = (d - f) * seg % LANES
                    moved = pltpu.roll(parts_in[d], s, 1) if s else parts_in[d]
                    v = moved if v is None else jnp.where(wide_lane >= d * seg, moved, v)
                out.append(v)
            return out

        got = [[None] * groups for _ in range(FIELDS)]
        for g in range(groups):
            for k in range(tiles):
                for f, v in enumerate(unpack(k, g)):
                    got[mixed * k + f][g] = v

        span = range(groups)

        def next_y(a):
            return [pltpu.roll(v, ny - 1, 0) for v in a]

        def last_y(a):
            return [pltpu.roll(v, 1, 0) for v in a]

        def forward(a, x, z):
            moved = [pltpu.roll(v, LANES - pitch * x - z, 1) for v in a]
            if groups == 1 or not x:
                return moved
            wrap = wide_lane >= LANES - pitch
            return [jnp.where(wrap, moved[min(g + 1, groups - 1)], moved[g]) for g in span]

        def backward(a, x, z):
            moved = [pltpu.roll(v, pitch * x + z, 1) for v in a]
            if groups == 1 or not x:
                return moved
            wrap = wide_lane < pitch
            return [jnp.where(wrap, moved[max(g - 1, 0)], moved[g]) for g in span]

        def both(op, *lists):
            return [op(*vs) for vs in zip(*lists)]

        add = functools.partial(both, lambda a, b: a + b)
        sub = functools.partial(both, lambda a, b: a - b)

        def gradient(vector):
            grad = []
            for v in vector:
                above, over, far = forward(v, 0, 1), forward(v, 1, 0), forward(v, 1, 1)
                near_z, far_z = add(v, above), add(over, far)
                wide, flat = sub(far_z, near_z), add(far_z, near_z)
                rise = add(sub(above, v), sub(far, over))
                grad.append([add(next_y(wide), wide), sub(next_y(flat), flat), add(next_y(rise), rise)])
            return grad

        pairs = [(0, 0), (0, 1), (0, 2), (1, 1), (1, 2), (2, 2)]
        free = got[7]
        for c in range(3):
            for g in span:
                basis[0, c, g] = got[3 + c][g] * free[g]
        grad = gradient([got[0], got[1], got[2]])
        mass = []
        high = lax.broadcasted_iota(jnp.int32, (ny, LANES), 0)
        for g in span:
            valid = (high <= ny - 2) & (plane >= 0) & (plane <= plan.nz - 2) & (depth <= plan.span - 2)
            valid = valid & (lax.div(wide_lane, pitch) + g * plan.packed <= nx - 2)
            material = got[6][g]
            zero = jnp.zeros((ny, LANES), F32)
            lame, shear, heavy = zero, zero, zero
            for r in range(table_ref.shape[1]):
                hit = material == float(r)
                lame = jnp.where(hit, table_ref[0, r], lame)
                shear = jnp.where(hit, table_ref[1, r], shear)
                heavy = jnp.where(hit, table_ref[2, r], heavy)
            lame = jnp.where(valid, lame * 0.0625, 0.0)
            shear = jnp.where(valid, shear * 0.0625, 0.0)
            mass.append(jnp.where(valid, heavy * 0.125, 0.0))
            frame = [
                [0.25 * grad[i][j][g] + (1.0 if i == j else 0.0) for j in range(3)] for i in range(3)
            ]
            strain = {}
            for i, j in pairs:
                v = sum(frame[k][i] * frame[k][j] for k in range(3))
                strain[i, j] = 0.5 * (v - 1.0 if i == j else v)
            bulk = lame * (strain[0, 0] + strain[1, 1] + strain[2, 2])
            for i in range(3):
                for j in range(3):
                    state[3 * i + j, g] = frame[i][j]
            for spot, (i, j) in enumerate(pairs):
                v = 2.0 * shear * strain[i, j]
                state[9 + spot, g] = v + bulk if i == j else v
            state[15, g] = lame
            state[16, g] = shear
        mass = add(mass, last_y(mass))
        mass = add(
            add(mass, backward(mass, 0, 1)), add(backward(mass, 1, 0), backward(mass, 1, 1))
        )
        for g in span:
            fields[0, g] = free[g]
            fields[1, g] = free[g] * (1.0 / HALF_WIDTH)
            fields[2, g] = (free[g] * mass[g] + (1.0 - free[g])) * (1.0 / HALF_WIDTH)

        rows8 = [pl.ds(8 * r, 8) for r in range(ny // 8)]

        def apply(j):
            grad = gradient([[basis[j, c, g] * fields[0, g] for g in span] for c in range(3)])
            pio = [[[[None] * len(rows8) for _ in span] for _ in range(3)] for _ in range(3)]
            for g in span:
                for r, at in enumerate(rows8):
                    d = [[grad[c][q][g][8 * r : 8 * r + 8] for q in range(3)] for c in range(3)]
                    f = [[state[3 * i + k, g, at] for k in range(3)] for i in range(3)]
                    pulled = [
                        [sum(f[k][a] * d[k][b] for k in range(3)) for b in range(3)] for a in range(3)
                    ]
                    lame, shear = state[15, g, at], state[16, g, at]
                    bulk = lame * (pulled[0][0] + pulled[1][1] + pulled[2][2])
                    t, s = {}, {}
                    for spot, (a, b) in enumerate(pairs):
                        v = shear * (pulled[a][b] + pulled[b][a])
                        t[a, b] = t[b, a] = v + bulk if a == b else v
                        s[a, b] = s[b, a] = state[9 + spot, g, at]
                    for i in range(3):
                        for b in range(3):
                            v = sum(f[i][k] * t[k, b] for k in range(3))
                            pio[i][b][g][r] = v + sum(d[i][k] * s[k, b] for k in range(3))
            for c in range(3):
                e = [[jnp.concatenate(pio[c][b][g], axis=0) for g in span] for b in range(3)]
                wide = add(e[0], last_y(e[0]))
                tilt = sub(last_y(e[1]), e[1])
                rise = add(e[2], last_y(e[2]))
                minus, plus = sub(tilt, wide), add(tilt, wide)
                out = add(
                    add(sub(minus, rise), backward(add(minus, rise), 0, 1)),
                    add(backward(sub(plus, rise), 1, 0), backward(add(plus, rise), 1, 1)),
                )
                for g in span:
                    basis[j + 1, c, g] = fields[1, g] * out[g] + (
                        fields[2, g] - CHAIN[j] / HALF_WIDTH
                    ) * basis[j, c, g]

        for j in range(STEPS):
            apply(j)

        mine = (depth >= halo) & (depth < halo + own) & (plane < plan.nz)
        spots = [(c, g, r) for c in range(3) for g in span for r in range(ny // 8)]
        for k in range(7):
            v = [
                jnp.where(mine[8 * r : 8 * r + 8], basis[k, c, g, rows8[r]], 0.0) for c, g, r in spots
            ]
            top = jnp.abs(v[0])
            for u in v[1:]:
                top = jnp.maximum(top, jnp.abs(u))
            grain = top * (32768.0 * max(1, len(v) // 6))
            for s, u in enumerate(v):
                coarse = (u + grain) - grain
                parts[0, k, s] = coarse
                parts[1, k, s] = u - coarse
        pairs_of = {}
        for i in range(6):
            acc = {j: [None, None] for j in range(i, 7)}
            for s in range(len(spots)):
                ch, cl = parts[0, i, s], parts[1, i, s]
                for j in range(i, 7):
                    dh, dl = parts[0, j, s], parts[1, j, s]
                    new = [ch * dh, cl * (dh + ch + dl) if i == j else ch * dl + cl * (dh + dl)]
                    acc[j] = new if s == 0 else [acc[j][0] + new[0], acc[j][1] + new[1]]
            for j in range(i, 7):
                pairs_of[i, j] = acc[j]
        items = [tuple(pairs_of[q]) for q in PRODUCTS]
        blank = (jnp.zeros((8, LANES), F32), jnp.zeros((8, LANES), F32))
        items = items + [blank] * (32 - len(items))

        def merge(a, b, mask, shift, axis):
            size = 8 if axis == 0 else LANES
            first_in, second_in = [], []
            for u, v in zip(a, b):
                if 2 * shift == size:
                    first_in.append(jnp.where(mask, u, v))
                    second_in.append(pltpu.roll(jnp.where(mask, v, u), shift, axis))
                else:
                    first_in.append(jnp.where(mask, u, pltpu.roll(v, shift, axis)))
                    second_in.append(jnp.where(mask, pltpu.roll(u, size - shift, axis), v))
            return add_pair(first_in, second_in)

        tall = []
        for q in range(4):
            it = items[8 * q : 8 * q + 8]
            one = [merge(it[r], it[r + 4], row < 4, 4, 0) for r in range(4)]
            twice = [merge(one[r], one[r + 2], lax.rem(row, 4) < 2, 2, 0) for r in range(2)]
            tall.append(merge(twice[0], twice[1], lax.rem(row, 2) < 1, 1, 0))
        quarter = lane // 32

        def turned(j):
            out = []
            for part in range(2):
                v = None
                for q in range(4):
                    u = tall[q][part]
                    u = pltpu.roll(u, LANES - 32 * j, 1) if j else u
                    v = u if v is None else jnp.where(quarter >= q, u, v)
                out.append(v)
            return out

        whole = add_all([turned(j) for j in range(4)])
        whole = add_all(
            [[pltpu.roll(u, LANES - 8 * j, 1) if j else u for u in whole] for j in range(4)]
        )
        whole = add_all(
            [
                [pltpu.roll(u, 8 - j, 1, stride=1, stride_axis=0) for u in whole]
                for j in range(8)
            ]
        )
        keep = lax.rem(lane, 32) == row + 8
        ends = [jnp.sum(jnp.where(keep, u, 0.0), axis=0, keepdims=True) for u in whole]
        sums[worker] = jnp.concatenate(ends, axis=0)

    fetched[4].wait()
    when(is_worker, work)
    when(me != last, lambda: pl.semaphore_wait(entered, 1))

    stride = plan.stride

    def share(d):
        when(
            me != d,
            pltpu.make_async_remote_copy(
                src_ref=sums.at[worker],
                dst_ref=sums.at[worker],
                send_sem=sum_send.at[0],
                recv_sem=sum_recv.at[0],
                **where_is(d),
            ).start,
        )

    def give_back():
        loop(total, share)
        wide_lane = lax.broadcasted_iota(jnp.int32, (ny, LANES), 1)
        for k in range(1, 7):
            for x in range(ngx):
                g, d = x // mixed, x % mixed
                out = None
                for c in range(3):
                    for i in range(sx):
                        e = c * sx + i
                        s = (e * stride - ((d * sx + i) * pitch + halo)) % LANES
                        v = basis[k, c, g]
                        moved = pltpu.roll(v, s, 1) if s else v
                        out = moved if out is None else jnp.where(wide_lane >= e * stride, moved, out)
                for y in range(ngy):
                    back[x, y, k - 1] = out[sy * y : sy * (y + 1)]
        loop(n, lambda q: give(q, True))

    own_low = jnp.minimum(lax.div(own * worker, sz), ngz - 1)
    own_high = lax.div(jnp.minimum(own * worker + own, plan.nz) - 1, sz)
    straddles = sz % own != 0

    def give(q, start):
        x, y = (q // ngy, q % ngy) if isinstance(q, int) else (lax.div(q, ngy), lax.rem(q, ngy))

        def to(z):
            d = q * ngz + z
            dst = vt.at[worker - pick(plan.from_low, z)]
            remote = pltpu.make_async_remote_copy(
                src_ref=back.at[x, y],
                dst_ref=dst,
                send_sem=back_send.at[0],
                recv_sem=back_recv.at[0],
                **where_is(d),
            )
            if start:
                when(d != me, remote.start)
                when(
                    d == me,
                    lambda: pltpu.make_async_copy(back.at[x, y], dst, back_recv.at[0]).start(),
                )
            else:
                when(d != me, remote.wait_send)

        to(own_low)
        if straddles:
            when(own_high > own_low, lambda: to(own_high))

    when(is_worker, give_back)
    fetched[5].wait()

    counts = [b - a + 1 for a, b in zip(plan.from_low, plan.from_high)]
    if min(counts) == plan.returns:
        settle(vt, back_recv.at[0])
    else:
        for z in range(ngz):
            when(gz == z, lambda z=z: settle(vt.at[pl.ds(0, counts[z])], back_recv.at[0]))

    mates = [(k, c, i) for k in range(0, 6, 2) for c in range(3) for i in range(sx)]

    def collect(j, accs):
        w = pick(plan.from_low, gz) + j
        offset = own * w - sz * gz
        inside = (lane >= offset) & (lane < offset + own)
        if min(counts) != plan.returns:
            inside = inside & (j < pick(counts, gz))
        new = []
        stacked = [jnp.concatenate([vt[j, k], vt[j, k + 1]], axis=0) for k in range(0, 6, 2)]
        for (k, c, i), acc in zip(mates, accs):
            s = lax.rem(offset - (c * sx + i) * stride + 2 * LANES, LANES)
            moved = pltpu.roll(stacked[k // 2], s, 1)
            new.append(jnp.where(inside, moved, acc))
        return tuple(new)

    accs = tuple(jnp.zeros((8, LANES), F32) for _ in mates)
    if plan.returns <= 16:
        for j in range(plan.returns):
            accs = collect(j, accs)
    else:
        accs = lax.fori_loop(0, plan.returns, collect, accs)

    active = plan.workers
    when(is_worker, lambda: settle(sums.at[pl.ds(0, active - 1)], sum_recv.at[0]))
    when(jnp.logical_not(is_worker), lambda: settle(sums, sum_recv.at[0]))

    def reduce_sums():
        zero = jnp.zeros((2, LANES), F32)
        if active <= 32:
            return add_all([(sums[d], zero) for d in range(active)])
        return lax.fori_loop(
            0, active, lambda d, a: add_pair(a, (sums[d], zero)), (zero, zero)
        )

    raw_sum, lost = reduce_sums()
    gram_high, gram_low = two_sum(raw_sum[0:1], raw_sum[1:2] + lost[0:1])
    gram_high = jnp.broadcast_to(gram_high, (8, LANES))
    gram_low = jnp.broadcast_to(gram_low, (8, LANES))

    def entry(i, j):
        s = place(PRODUCTS.index((min(i, j), max(i, j))))
        return jnp.broadcast_to(gram_high[:, s : s + 1], (8, LANES))

    first_gram = [
        [HALF_WIDTH * entry(i, j + 1) + CHAIN[j] * entry(i, j) for j in range(3)]
        for i in range(3)
    ]
    c = solve_small(first_gram, [entry(i, 0) for i in range(3)])

    def affine(c, load_at):
        return ((load_at(0) + c[0] * load_at(1)) + c[1] * load_at(2)) + c[2] * load_at(3)

    def scaled(at, size, x):
        ch, cl, rest = (const[pl.ds(q, size), :] for q in at)
        xh, xl = split(x)
        p = (ch + cl) * x
        return p, (((ch * xh - p) + ch * xl + cl * xh) + cl * xl) + rest * x

    done = []
    for v in range(2):
        side = [
            affine(c, lambda a, s=s: const[pl.ds((4 * s + a) * 16 + 8 * v, 8), :])
            for s in range(6)
        ]
        turn = [[24 * 16 + (3 * q + part) * 16 + 8 * v for part in range(3)] for q in range(3)]
        image = [
            add_pair(scaled(turn[q], 8, side[2 + q]), scaled(turn[2], 8, side[4 + q]))
            for q in range(2)
        ]

        def times_pair(x, pair):
            p, e = two_product(x, pair[0])
            return p, e + x * pair[1]

        weight = add_pair(times_pair(side[0], image[1]), times_pair(side[1], image[0]))
        high_part, low_part = two_product(gram_high, weight[0])
        pair = (high_part, low_part + (gram_high * weight[1] + gram_low * weight[0]))
        for s, times in ((32, 4), (1, 8)):
            pair = add_all(
                [[pltpu.roll(u, LANES - s * q, 1) if q else u for u in pair] for q in range(times)]
            )
        done.append(jnp.broadcast_to((pair[0] + pair[1])[:, 8:9], (8, LANES)))

    def form(f):
        return jnp.broadcast_to(done[f // 8][f % 8 : f % 8 + 1], (8, LANES))

    gram = [[form(3 * i + j) for j in range(3)] for i in range(3)]
    d = solve_small(gram, [form(9 + i) for i in range(3)])
    base_at = 24 * 16 + 9 * 16
    vector = affine(c, lambda a: const[pl.ds(base_at + 8 * a, 8), :])
    moved = affine(c, lambda a: const[pl.ds(base_at + 32 + 8 * a, 8), :])
    turn = [[base_at + 64 + 8 * (3 * q + part) for part in range(3)] for q in range(2)]
    image = add_pair(scaled(turn[0], 8, vector), scaled(turn[1], 8, moved))
    factor = jnp.where(row == 0, -d[0], jnp.where(row == 1, -d[1], jnp.where(row == 2, -d[2], 1.0)))
    coef = times_pair(factor, image)
    coef = add_pair(coef, [pltpu.roll(u, 6, 0) for u in coef])
    coef = add_pair(coef, [pltpu.roll(u, 7, 0) for u in coef])
    coef = two_sum(coef[0][0:1], coef[1][0:1])

    def spread_coef(part, k):
        return jnp.broadcast_to(coef[part][:, k : k + 1], (8, LANES))

    for slot in range(2):
        sets = [[-spread_coef(0, 32 + k) for k in range(7)]]
        if slot == 1:
            sets = [[spread_coef(part, k) for k in range(7)] for part in range(2)]
        duo = [
            [jnp.where(row < sy, w[k + 1], w[k + 2]) for w in sets] for k in range(0, 6, 2)
        ]
        for cc in range(3):
            for i in range(sx):
                v = None
                for k in range(0, 6, 2):
                    held_k = accs[mates.index((k, cc, i))]
                    u = duo[k // 2][0] * held_k
                    for extra in duo[k // 2][1:]:
                        u = u + extra * held_k
                    v = u if v is None else v + u
                start_part = raw[3 + cc, i] * raw[7, i]
                head = sets[0][0][0:sy] * start_part
                for extra in sets[1:]:
                    head = head + extra[0][0:sy] * start_part
                out_ref[slot, cc, i] = head + (v[0:sy] + v[sy : 2 * sy])

    loop(plan.sends, lambda j: piece(j, False))

    def sent():
        loop(n, lambda q: give(q, False))
        left = total - 1
        while left:
            rows = min(left, active)
            settle(sums.at[pl.ds(0, rows)], sum_send.at[0])
            left -= rows

    when(is_worker, sent)


def per_device(displacement, load, material, free_node, table):
    shard = displacement.shape[1:]
    sx, sy, sz = shard
    grid = tuple(lax.axis_size(a) for a in ("gx", "gy", "gz"))
    plan = Plan(grid, shard)
    ngx, ngy, ngz = grid
    ny = ngy * sy
    groups = plan.groups
    const = jnp.asarray(tables())
    buffers = [
        pltpu.VMEM((FIELDS, sx, sy, sz), F32),
        pltpu.VMEM((2, sx, sy, sz), jnp.int32),
        pltpu.VMEM((plan.sends, plan.tiles, sy, LANES), F32),
        pltpu.VMEM((2, plan.tiles, ngx, ngy, sy, LANES), F32),
        pltpu.VMEM((7, 3, groups, ny, LANES), F32),
        pltpu.VMEM((3, groups, ny, LANES), F32),
        pltpu.VMEM((17, groups, ny, LANES), F32),
        pltpu.VMEM((2, 7, 3 * groups * ny // 8, 8, LANES), F32),
        pltpu.VMEM((ngx, ngy, 6, sy, LANES), F32),
        pltpu.VMEM((plan.returns, 6, sy, LANES), F32),
        pltpu.VMEM((plan.workers, 2, LANES), F32),
        pltpu.VMEM(const.shape, F32),
        pltpu.SMEM(table.shape[::-1], F32),
        pltpu.SemaphoreType.DMA((6,)),
        pltpu.SemaphoreType.DMA((1,)),
        pltpu.SemaphoreType.DMA((2,)),
        pltpu.SemaphoreType.DMA((1,)),
        pltpu.SemaphoreType.DMA((1,)),
        pltpu.SemaphoreType.DMA((1,)),
        pltpu.SemaphoreType.DMA((1,)),
        pltpu.SemaphoreType.REGULAR,
    ]
    operands = (displacement, load, material, free_node, table.T, const)
    both = pl.pallas_call(
        functools.partial(kernel, plan),
        out_shape=jax.ShapeDtypeStruct((2,) + displacement.shape, F32),
        in_specs=[pl.BlockSpec(memory_space=pltpu.HBM)] * 6,
        out_specs=pl.BlockSpec(memory_space=pltpu.VMEM),
        scratch_shapes=buffers,
        compiler_params=pltpu.CompilerParams(
            collective_id=0, has_side_effects=True, vmem_limit_bytes=32 << 20
        ),
    )(*(pltpu.with_memory_space_constraint(a, pltpu.HBM) for a in operands))
    return both[0], both[1]


def solution(mesh):
    in_specs = (
        P(None, "gx", "gy", "gz"),
        P(None, "gx", "gy", "gz"),
        P("gx", "gy", "gz"),
        P("gx", "gy", "gz"),
        P(),
    )
    out_specs = (P(None, "gx", "gy", "gz"), P(None, "gx", "gy", "gz"))
    return jax.shard_map(
        per_device, mesh=mesh, in_specs=in_specs, out_specs=out_specs, check_vma=False
    )
```

```python
import functools

import jax
import jax.numpy as jnp
import numpy as np
from jax import lax
from jax.experimental import pallas as pl
from jax.experimental.pallas import tpu as pltpu
from jax.sharding import PartitionSpec as P

SHIFTS = (9.6, 51.4)
HALF_WIDTH = 29.5
CHAIN = SHIFTS + (30.5,) + SHIFTS + (30.5,)
STEPS = 6
FIELDS = 8
ORDER = (0, 3, 1, 4, 2, 5, 6, 7)
LANES = 128
PRODUCTS = {(i, j): t for t, (i, j) in enumerate((i, j) for i in range(6) for j in range(i, 6))}
PRODUCTS.update({(i, 6): 24 + i for i in range(6)})
EARLY = {(i, j): t for t, (i, j) in enumerate((i, j) for i in range(3) for j in range(i, 4))}
F32 = jnp.float32


def place(t):
    return 32 * (t // 8) + 8 + t % 8


def bits(x):
    top = np.asarray(x, np.float32)
    t = np.float32(4097.0) * top
    high = t - (t - top)
    return high, top - high, (x - top.astype(np.float64)).astype(np.float32)


def tables():
    width = 1.0 / np.float64(np.float32(1.0 / HALF_WIDTH))
    chain = np.array([np.float64(np.float32(x / HALF_WIDTH)) * width for x in CHAIN] + [0.0])

    def shifted(x):
        return np.concatenate([[0.0], x[:-1]])

    def times(x):
        return chain * x + width * shifted(x)

    unit = np.eye(7)
    b = [[unit[0]] + [-times(unit[j]) for j in range(3)]]
    for j in range(2):
        b.append([(times(x) - SHIFTS[j] * x) / HALF_WIDTH for x in b[j]])
    forms = [(i, j) for i in range(3) for j in range(3)] + [(i, None) for i in range(3)]
    wide = np.zeros((6, 4, 16, LANES))
    turn = np.zeros((3, 16, LANES))
    for f, (i, j) in enumerate(forms):
        for (one, two), t in PRODUCTS.items():
            at = place(t)
            turn[:, f, at] = (1.0, 1.0, 0.0) if j is None else (chain[one], chain[two], width)
            for a in range(4):
                left, right = b[i][a], b[j or 0][a]
                wide[0, a, f, at] = left[one]
                wide[1, a, f, at] = left[two] if one != two else 0.0
                wide[2, a, f, at] = right[one]
                wide[3, a, f, at] = right[two]
                wide[4, a, f, at] = shifted(right)[one]
                wide[5, a, f, at] = shifted(right)[two]
    last = np.zeros((2, 4, 8, LANES))
    final = np.zeros((2, 8, LANES))
    for k in range(7):
        final[:, :3, k] = np.array([[chain[k]], [width]])
        final[0, :3, 32 + k] = 1.0
        final[0, 3, k] = final[0, 3, 32 + k] = 1.0
        for a in range(4):
            for j in range(3):
                last[0, a, j, k] = last[0, a, j, 32 + k] = b[j][a][k]
                last[1, a, j, k] = shifted(b[j][a])[k]
            last[0, a, 3, k] = b[0][a][k]
            last[0, a, 3, 32 + k] = -1.0 if 0 < a == k + 1 else 0.0
    blocks = [wide, *(np.stack(bits(x)) for x in turn), last, *(np.stack(bits(x)) for x in final)]
    return np.concatenate([x.reshape(-1, LANES).astype(np.float32) for x in blocks])


def solve_small(gram, right):
    sym = [[0.5 * (gram[i][j] + gram[j][i]) for j in range(3)] for i in range(3)]
    r0 = 1.0 / sym[0][0]
    l10 = sym[1][0] * r0
    l20 = sym[2][0] * r0
    r1 = 1.0 / (sym[1][1] - l10 * sym[1][0])
    e = sym[2][1] - l20 * sym[1][0]
    l21 = e * r1
    d2 = sym[2][2] - l20 * sym[2][0] - l21 * e
    y1 = right[1] - l10 * right[0]
    c2 = (right[2] - l20 * right[0] - l21 * y1) / d2
    c1 = y1 * r1 - l21 * c2
    c0 = right[0] * r0 - l10 * c1 - l20 * c2
    return [c0, c1, c2]


def two_sum(a, b):
    s = a + b
    t = s - a
    return s, (a - (s - t)) + (b - t)


def add_pair(p, q):
    s, e = two_sum(p[0], q[0])
    return s, e + (p[1] + q[1])


def add_parts(p, q):
    return add_pair(p, q) if len(p) == 2 else (p[0] + q[0],)


def add_all(terms):
    while len(terms) > 1:
        rest = terms[len(terms) & ~1 :]
        terms = [add_parts(p, q) for p, q in zip(terms[::2], terms[1::2])] + rest
    return terms[0]


def split(a):
    t = 4097.0 * a
    high = t - (t - a)
    return high, a - high


def two_product(a, b):
    p = a * b
    (ah, al), (bh, bl) = split(a), split(b)
    return p, ((ah * bh - p) + ah * bl + al * bh) + al * bl


def loop(count, body):
    if count <= 32:
        for i in range(count):
            body(i)
    else:

        def step(i, carry):
            body(i)
            return carry

        lax.fori_loop(0, count, step, 0)


def when(condition, body):
    if isinstance(condition, bool):
        if condition:
            body()
    else:
        pl.when(condition)(body)


class Plan:
    def __init__(self, grid, shard):
        self.grid, self.shard = grid, shard
        ngx, ngy, ngz = grid
        sx, sy, sz = shard
        self.n = ngx * ngy
        self.nz = ngz * sz
        self.halo = STEPS
        total = self.n * ngz
        self.pitch = 1 << (-(-self.nz // total) + 2 * self.halo - 1).bit_length()
        spare = total - -(-self.nz // (self.pitch - 2 * self.halo))
        self.counts = [self.n] * (ngz - 1) + [max(2, self.n - spare)]
        self.own = -(-self.nz // sum(self.counts))
        self.span = self.own + 2 * self.halo
        self.packed = LANES // self.pitch
        self.groups = ngx * sx // self.packed
        self.mixed = LANES // (sx * self.pitch)
        self.tiles = FIELDS // self.mixed
        self.stride = LANES // (3 * sx)
        self.workers = -(-self.nz // self.own)
        self.base = [sum(self.counts[:z]) for z in range(ngz)]
        own, halo = self.own, self.halo
        self.to_low = [max(0, (sz * z - own - halo) // own + 1) for z in range(ngz)]
        self.to_high = [
            min(self.workers - 1, -(-(sz * z + sz + halo) // own) - 1) for z in range(ngz)
        ]
        self.from_low = [sz * z // own for z in range(ngz)]
        self.from_high = [(sz * z + sz - 1) // own for z in range(ngz)]
        self.sends = max(b - a + 1 for a, b in zip(self.to_low, self.to_high))
        self.returns = max(b - a + 1 for a, b in zip(self.from_low, self.from_high))
        assert sz == LANES and 8 == 2 * sy and own <= self.stride and LANES % self.pitch == 0


def pick(values, z):
    if all(v == values[0] for v in values):
        return values[0]
    out = values[0]
    for k in range(1, len(values)):
        out = jnp.where(z >= k, values[k], out)
    return out


def kernel(
    plan,
    disp_hbm,
    load_hbm,
    mat_hbm,
    free_hbm,
    table_hbm,
    const_hbm,
    out_ref,
    raw,
    flags,
    pack,
    recv,
    basis,
    fields,
    state,
    parts,
    back,
    vt,
    first_sums,
    sums,
    talls,
    const,
    table_ref,
    in_sem,
    send_sem,
    recv_sem,
    back_send,
    back_recv,
    sum_send,
    sum_recv,
    entered,
):
    ngx, ngy, ngz = plan.grid
    sx, sy, sz = plan.shard
    n, own, halo, pitch = plan.n, plan.own, plan.halo, plan.pitch
    nx, ny = ngx * sx, ngy * sy
    groups, mixed, tiles = plan.groups, plan.mixed, plan.tiles
    total = n * ngz
    gx, gy, gz = lax.axis_index("gx"), lax.axis_index("gy"), lax.axis_index("gz")
    p = gx * ngy + gy
    me = p * ngz + gz
    count = pick(plan.counts, gz)
    worker = pick(plan.base, gz) + count - 1 - p
    is_worker = (p < count) & (worker < plan.workers)
    first = own * worker - halo
    settled = jnp.maximum(first, 0)
    low_slab = jnp.minimum(lax.div(settled, sz), ngz - 1)
    edge = sz * (low_slab + 1)
    two = (first + plan.span > edge) & (low_slab + 1 < ngz)
    last = total - 1

    fetched = [
        pltpu.make_async_copy(disp_hbm, raw.at[pl.ds(0, 3)], in_sem.at[0]),
        pltpu.make_async_copy(load_hbm, raw.at[pl.ds(3, 3)], in_sem.at[1]),
        pltpu.make_async_copy(mat_hbm, flags.at[0], in_sem.at[2]),
        pltpu.make_async_copy(free_hbm, flags.at[1], in_sem.at[3]),
        pltpu.make_async_copy(table_hbm, table_ref, in_sem.at[4]),
        pltpu.make_async_copy(const_hbm, const, in_sem.at[5]),
    ]
    for copy in fetched:
        copy.start()

    def where_is(d):
        return dict(device_id=d, device_id_type=pl.DeviceIdType.LOGICAL)

    barrier = pltpu.get_barrier_semaphore()

    def greet(d):
        pl.semaphore_signal(barrier, inc=1, **where_is(d))

    def greet_slab(z):
        def one(q):
            d = q * ngz + z
            when((d != me) & (d != last), lambda: greet(d))

        loop(n, one)

    when(is_worker, lambda: greet_slab(low_slab))
    when(is_worker & two, lambda: greet_slab(low_slab + 1))
    when(me != last, lambda: greet(last))

    for copy in fetched[:4]:
        copy.wait()
    raw[6] = flags[0].astype(F32)
    raw[7] = flags[1].astype(F32)

    lane = lax.broadcasted_iota(jnp.int32, (8, LANES), 1)
    row = lax.broadcasted_iota(jnp.int32, (8, LANES), 0)
    per = 8 // sy
    stacks = -(-tiles // per)
    held = []
    for t in range(stacks):
        part = []
        for e in range(mixed * sx):
            f, i = e // sx, e % sx
            rows = [
                raw[ORDER[mixed * min(per * t + h, tiles - 1) + f], i] for h in range(per)
            ]
            part.append(jnp.concatenate(rows, axis=0))
        turned = []
        for e in range(mixed * sx):
            v = part[e]
            for k in range(1, mixed):
                v = jnp.where(lax.rem(gx, mixed) == k, part[(e - k * sx) % (mixed * sx)], v)
            turned.append(v)
        held.append(turned)

    to_low = pick(plan.to_low, gz)
    to_count = pick([b - a + 1 for a, b in zip(plan.to_low, plan.to_high)], gz)

    def route(j):
        w = to_low + j
        z = 0
        for k in range(1, ngz):
            z = z + jnp.where(w >= plan.base[k], 1, 0)
        q = pick([b + c - 1 for b, c in zip(plan.base, plan.counts)], z) - w
        slot = jnp.where(sz * gz > jnp.maximum(own * w - halo, 0), 1, 0)
        return j < to_count, slot, q * ngz + z

    def prepare(j):
        w = to_low + j
        offset = sz * gz - (own * w - halo)
        for t in range(stacks):
            out = None
            for e, v in enumerate(held[t]):
                moved = pltpu.roll(v, lax.rem(offset + (pitch * e + 8 * LANES), LANES), 1)
                out = moved if out is None else jnp.where(lane >= pitch * e, moved, out)
            for h in range(min(per, tiles - per * t)):
                pack[j, per * t + h] = out[sy * h : sy * (h + 1)]

    loop(plan.sends, prepare)

    expected = to_count
    if plan.sends <= 32:
        routes = [route(j) for j in range(plan.sends)]
        for valid, _, d in routes:
            expected = expected - jnp.where(valid & (d == me), 1, 0)
    else:
        routes = None

        def count_self(j, seen):
            valid, _, d = route(j)
            return seen - jnp.where(valid & (d == me), 1, 0)

        expected = lax.fori_loop(0, plan.sends, count_self, expected)
    expected = jnp.where(me == last, total - 1, expected)
    pl.semaphore_wait(barrier, expected)

    def piece(j, start):
        valid, slot, d = routes[j] if routes else route(j)
        dst = recv.at[slot, :, gx, gy]
        remote = pltpu.make_async_remote_copy(
            src_ref=pack.at[j],
            dst_ref=dst,
            send_sem=send_sem.at[0],
            recv_sem=recv_sem.at[slot],
            **where_is(d),
        )
        if start:
            when(valid & (d != me), remote.start)
            when(
                valid & (d == me),
                lambda: pltpu.make_async_copy(pack.at[j], dst, recv_sem.at[slot]).start(),
            )
        else:
            when(valid & (d != me), remote.wait_send)

    loop(plan.sends, lambda j: piece(j, True))

    def announce():
        loop(total - 1, lambda d: pl.semaphore_signal(entered, inc=1, **where_is(d)))

    when(me == last, announce)

    def settle(ref, sem):
        pltpu.make_async_copy(ref, ref, sem).wait()

    def share(ref, slot, d):
        when(
            me != d,
            pltpu.make_async_remote_copy(
                src_ref=ref.at[worker],
                dst_ref=ref.at[worker],
                send_sem=sum_send.at[slot],
                recv_sem=sum_recv.at[slot],
                **where_is(d),
            ).start,
        )

    def work():
        settle(recv.at[0], recv_sem.at[0])
        when(two, lambda: settle(recv.at[1], recv_sem.at[1]))

        wide_lane = lax.broadcasted_iota(jnp.int32, (ny, LANES), 1)
        depth = lax.rem(wide_lane, pitch)
        plane = depth + first
        near = plane < edge
        seg = sx * pitch

        def gather_rows(slot, k, x):
            return jnp.concatenate([recv[slot, k, x, g] for g in range(ngy)], axis=0)

        def source(k, x):
            return jnp.where(near, gather_rows(0, k, x), gather_rows(1, k, x))

        def unpack(k, g):
            parts_in = [source(k, g * mixed + d) for d in range(mixed)]
            out = []
            for f in range(mixed):
                v = None
                for at in range(mixed):
                    u = parts_in[(at - f) % mixed]
                    v = u if v is None else jnp.where(wide_lane >= at * seg, u, v)
                out.append(pltpu.roll(v, LANES - f * seg, 1) if f else v)
            return out

        got = [[None] * groups for _ in range(FIELDS)]
        for g in range(groups):
            for k in range(tiles):
                for f, v in enumerate(unpack(k, g)):
                    got[ORDER[mixed * k + f]][g] = v

        span = range(groups)

        def next_y(a):
            return [pltpu.roll(v, ny - 1, 0) for v in a]

        def last_y(a):
            return [pltpu.roll(v, 1, 0) for v in a]

        def forward(a, x, z):
            moved = [pltpu.roll(v, LANES - pitch * x - z, 1) for v in a]
            if groups == 1 or not x:
                return moved
            wrap = wide_lane >= LANES - pitch
            return [jnp.where(wrap, moved[min(g + 1, groups - 1)], moved[g]) for g in span]

        def backward(a, x, z):
            moved = [pltpu.roll(v, pitch * x + z, 1) for v in a]
            if groups == 1 or not x:
                return moved
            wrap = wide_lane < pitch
            return [jnp.where(wrap, moved[max(g - 1, 0)], moved[g]) for g in span]

        def both(op, *lists):
            return [op(*vs) for vs in zip(*lists)]

        add = functools.partial(both, lambda a, b: a + b)
        sub = functools.partial(both, lambda a, b: a - b)

        def gradient(vector):
            grad = []
            for v in vector:
                above, over, far = forward(v, 0, 1), forward(v, 1, 0), forward(v, 1, 1)
                near_z, far_z = add(v, above), add(over, far)
                wide, flat = sub(far_z, near_z), add(far_z, near_z)
                rise = add(sub(above, v), sub(far, over))
                grad.append([add(next_y(wide), wide), sub(next_y(flat), flat), add(next_y(rise), rise)])
            return grad

        pairs = [(0, 0), (0, 1), (0, 2), (1, 1), (1, 2), (2, 2)]
        free = got[7]
        for c in range(3):
            for g in span:
                basis[0, c, g] = got[3 + c][g] * free[g]
        grad = gradient([got[0], got[1], got[2]])
        mass = []
        high = lax.broadcasted_iota(jnp.int32, (ny, LANES), 0)
        for g in span:
            valid = (high <= ny - 2) & (plane >= 0) & (plane <= plan.nz - 2) & (depth <= plan.span - 2)
            valid = valid & (lax.div(wide_lane, pitch) + g * plan.packed <= nx - 2)
            material = got[6][g]
            zero = jnp.zeros((ny, LANES), F32)
            lame, shear, heavy = zero, zero, zero
            for r in range(table_ref.shape[1]):
                hit = material == float(r)
                lame = jnp.where(hit, table_ref[0, r], lame)
                shear = jnp.where(hit, table_ref[1, r], shear)
                heavy = jnp.where(hit, table_ref[2, r], heavy)
            lame = jnp.where(valid, lame * 0.0625, 0.0)
            shear = jnp.where(valid, shear * 0.0625, 0.0)
            mass.append(jnp.where(valid, heavy * 0.125, 0.0))
            frame = [
                [0.25 * grad[i][j][g] + (1.0 if i == j else 0.0) for j in range(3)] for i in range(3)
            ]
            strain = {}
            for i, j in pairs:
                v = sum(frame[k][i] * frame[k][j] for k in range(3))
                strain[i, j] = 0.5 * (v - 1.0 if i == j else v)
            bulk = lame * (strain[0, 0] + strain[1, 1] + strain[2, 2])
            for i in range(3):
                for j in range(3):
                    state[3 * i + j, g] = frame[i][j]
            for spot, (i, j) in enumerate(pairs):
                v = 2.0 * shear * strain[i, j]
                state[9 + spot, g] = v + bulk if i == j else v
            state[15, g] = lame
            state[16, g] = shear
        mass = add(mass, last_y(mass))
        mass = add(
            add(mass, backward(mass, 0, 1)), add(backward(mass, 1, 0), backward(mass, 1, 1))
        )
        for g in span:
            fields[0, g] = free[g]
            fields[1, g] = free[g] * (1.0 / HALF_WIDTH)
            fields[2, g] = (free[g] * mass[g] + (1.0 - free[g])) * (1.0 / HALF_WIDTH)

        rows8 = [pl.ds(8 * r, 8) for r in range(ny // 8)]

        def apply(j):
            grad = gradient([[basis[j, c, g] * fields[0, g] for g in span] for c in range(3)])
            pio = [[[[None] * len(rows8) for _ in span] for _ in range(3)] for _ in range(3)]
            for g in span:
                for r, at in enumerate(rows8):
                    d = [[grad[c][q][g][8 * r : 8 * r + 8] for q in range(3)] for c in range(3)]
                    f = [[state[3 * i + k, g, at] for k in range(3)] for i in range(3)]
                    pulled = [
                        [sum(f[k][a] * d[k][b] for k in range(3)) for b in range(3)] for a in range(3)
                    ]
                    lame, shear = state[15, g, at], state[16, g, at]
                    bulk = lame * (pulled[0][0] + pulled[1][1] + pulled[2][2])
                    t, s = {}, {}
                    for spot, (a, b) in enumerate(pairs):
                        v = shear * (pulled[a][b] + pulled[b][a])
                        t[a, b] = t[b, a] = v + bulk if a == b else v
                        s[a, b] = s[b, a] = state[9 + spot, g, at]
                    for i in range(3):
                        for b in range(3):
                            v = sum(f[i][k] * t[k, b] for k in range(3))
                            pio[i][b][g][r] = v + sum(d[i][k] * s[k, b] for k in range(3))
            for c in range(3):
                e = [[jnp.concatenate(pio[c][b][g], axis=0) for g in span] for b in range(3)]
                wide = add(e[0], last_y(e[0]))
                tilt = sub(last_y(e[1]), e[1])
                rise = add(e[2], last_y(e[2]))
                minus, plus = sub(tilt, wide), add(tilt, wide)
                out = add(
                    add(sub(minus, rise), backward(add(minus, rise), 0, 1)),
                    add(backward(sub(plus, rise), 1, 0), backward(add(plus, rise), 1, 1)),
                )
                for g in span:
                    basis[j + 1, c, g] = fields[1, g] * out[g] + (
                        fields[2, g] - CHAIN[j] / HALF_WIDTH
                    ) * basis[j, c, g]

        mine = (depth >= halo) & (depth < halo + own) & (plane < plan.nz)
        spots = [(c, g, r) for c in range(3) for g in span for r in range(ny // 8)]
        mine = [mine[8 * r : 8 * r + 8] for r in range(ny // 8)]

        def divide(k):
            v = [jnp.where(mine[r], basis[k, c, g, rows8[r]], 0.0) for c, g, r in spots]
            top = jnp.abs(v[0])
            for u in v[1:]:
                top = jnp.maximum(top, jnp.abs(u))
            grain = top * (32768.0 * max(1, len(v) // 6))
            for s, u in enumerate(v):
                coarse = (u + grain) - grain
                parts[0, k, s] = coarse
                parts[1, k, s] = u - coarse

        def products(i, js):
            acc = {}
            for s in range(len(spots)):
                ch, cl = parts[0, i, s], parts[1, i, s]
                for j in js:
                    dh, dl = parts[0, j, s], parts[1, j, s]
                    new = [ch * dh, cl * (dh + ch + dl) if i == j else ch * dl + cl * (dh + dl)]
                    acc[j] = new if s == 0 else [acc[j][0] + new[0], acc[j][1] + new[1]]
            return {(i, j): tuple(acc[j]) for j in js}

        def merge(a, b, mask, shift):
            first_in, second_in = [], []
            for u, v in zip(a, b):
                if shift == 4:
                    first_in.append(jnp.where(mask, u, v))
                    second_in.append(pltpu.roll(jnp.where(mask, v, u), shift, 0))
                else:
                    first_in.append(jnp.where(mask, u, pltpu.roll(v, shift, 0)))
                    second_in.append(jnp.where(mask, pltpu.roll(u, 8 - shift, 0), v))
            return add_parts(tuple(first_in), tuple(second_in))

        def stack(items, slots):
            none = tuple(jnp.zeros((8, LANES), F32) for _ in next(iter(items.values())))
            it = [items.get(q, none) for q in slots]
            one = [merge(it[r], it[r + 4], row < 4, 4) for r in range(4)]
            twice = [merge(one[r], one[r + 2], lax.rem(row, 4) < 2, 2) for r in range(2)]
            return merge(twice[0], twice[1], lax.rem(row, 2) < 1, 1)

        def slots_of(table, q):
            at = {t: pair for pair, t in table.items()}
            return [at.get(8 * q + r) for r in range(8)]

        quarter = lane // 32

        def fold(tall):
            def turned(j):
                out = []
                for part in range(len(tall[0])):
                    v = None
                    for q in range(len(tall)):
                        u = tall[q][part]
                        u = pltpu.roll(u, LANES - 32 * j, 1) if j else u
                        v = u if v is None else jnp.where(quarter >= q, u, v)
                    out.append(v)
                return tuple(out)

            whole = add_all([turned(j) for j in range(4)])
            whole = add_all(
                [
                    tuple(pltpu.roll(u, LANES - 8 * j, 1) if j else u for u in whole)
                    for j in range(4)
                ]
            )
            whole = add_all(
                [
                    tuple(pltpu.roll(u, 8 - j, 1, stride=1, stride_axis=0) for u in whole)
                    for j in range(8)
                ]
            )
            keep = (lax.rem(lane, 32) == row + 8) & (quarter < len(tall))
            return [jnp.sum(jnp.where(keep, u, 0.0), axis=0, keepdims=True) for u in whole]

        items = {}
        for k in range(STEPS):
            divide(k)
            for i in range(k + 1):
                items.update(products(i, [k]))
            if k == 3:
                single = {q: (items[q][0] + items[q][1],) for q in EARLY}
                early = [stack(single, slots_of(EARLY, q)) for q in range(2)]
                first_sums[worker] = fold(early)[0]
            if k < STEPS - 1:
                apply(k)
        for q in range(3):
            high_part, low_part = stack(items, slots_of(PRODUCTS, q))
            talls[q, 0] = high_part
            talls[q, 1] = low_part
        when(me != last, lambda: pl.semaphore_wait(entered, 1))
        loop(total, lambda d: share(first_sums, 0, d))
        apply(STEPS - 1)
        divide(6)
        items = {}
        for i in range(6):
            items.update(products(i, [6]))
        tall = [(talls[q, 0], talls[q, 1]) for q in range(3)]
        tall = tall + [stack(items, slots_of(PRODUCTS, 3))]
        sums[worker] = jnp.concatenate(fold(tall), axis=0)

    fetched[4].wait()
    when(is_worker, work)
    when(
        jnp.logical_not(is_worker) & (me != last), lambda: pl.semaphore_wait(entered, 1)
    )

    stride = plan.stride

    def give_back():
        loop(total, lambda d: share(sums, 1, d))
        wide_lane = lax.broadcasted_iota(jnp.int32, (ny, LANES), 1)
        for k in range(1, 7):
            for x in range(ngx):
                g, d = x // mixed, x % mixed
                out = None
                for c in range(3):
                    for i in range(sx):
                        e = c * sx + i
                        s = (e * stride - ((d * sx + i) * pitch + halo)) % LANES
                        v = basis[k, c, g]
                        moved = pltpu.roll(v, s, 1) if s else v
                        out = moved if out is None else jnp.where(wide_lane >= e * stride, moved, out)
                for y in range(ngy):
                    back[x, y, k - 1] = out[sy * y : sy * (y + 1)]
        loop(n, lambda q: give(q, True))

    own_low = jnp.minimum(lax.div(own * worker, sz), ngz - 1)
    own_high = lax.div(jnp.minimum(own * worker + own, plan.nz) - 1, sz)
    straddles = sz % own != 0

    def give(q, start):
        x, y = (q // ngy, q % ngy) if isinstance(q, int) else (lax.div(q, ngy), lax.rem(q, ngy))

        def to(z):
            d = q * ngz + z
            dst = vt.at[worker - pick(plan.from_low, z)]
            remote = pltpu.make_async_remote_copy(
                src_ref=back.at[x, y],
                dst_ref=dst,
                send_sem=back_send.at[0],
                recv_sem=back_recv.at[0],
                **where_is(d),
            )
            if start:
                when(d != me, remote.start)
                when(
                    d == me,
                    lambda: pltpu.make_async_copy(back.at[x, y], dst, back_recv.at[0]).start(),
                )
            else:
                when(d != me, remote.wait_send)

        to(own_low)
        if straddles:
            when(own_high > own_low, lambda: to(own_high))

    when(is_worker, give_back)
    fetched[5].wait()

    counts = [b - a + 1 for a, b in zip(plan.from_low, plan.from_high)]
    if min(counts) == plan.returns:
        settle(vt, back_recv.at[0])
    else:
        for z in range(ngz):
            when(gz == z, lambda z=z: settle(vt.at[pl.ds(0, counts[z])], back_recv.at[0]))

    mates = [(k, c, i) for k in range(0, 6, 2) for c in range(3) for i in range(sx)]

    def collect(j, accs):
        w = pick(plan.from_low, gz) + j
        offset = own * w - sz * gz
        inside = (lane >= offset) & (lane < offset + own)
        if min(counts) != plan.returns:
            inside = inside & (j < pick(counts, gz))
        new = []
        stacked = [jnp.concatenate([vt[j, k], vt[j, k + 1]], axis=0) for k in range(0, 6, 2)]
        for (k, c, i), acc in zip(mates, accs):
            s = lax.rem(offset - (c * sx + i) * stride + 2 * LANES, LANES)
            moved = pltpu.roll(stacked[k // 2], s, 1)
            new.append(jnp.where(inside, moved, acc))
        return tuple(new)

    accs = tuple(jnp.zeros((8, LANES), F32) for _ in mates)
    if plan.returns <= 16:
        for j in range(plan.returns):
            accs = collect(j, accs)
    else:
        accs = lax.fori_loop(0, plan.returns, collect, accs)

    active = plan.workers

    def wait_rows(ref, sem, rows):
        while rows:
            now = min(rows, active)
            settle(ref.at[pl.ds(0, now)], sem)
            rows -= now

    def sent():
        loop(n, lambda q: give(q, False))
        wait_rows(first_sums, sum_send.at[0], total - 1)
        wait_rows(sums, sum_send.at[1], total - 1)

    loop(plan.sends, lambda j: piece(j, False))
    when(is_worker, sent)

    def landed(ref, slot):
        when(is_worker, lambda: wait_rows(ref, sum_recv.at[slot], active - 1))
        when(jnp.logical_not(is_worker), lambda: wait_rows(ref, sum_recv.at[slot], active))

    def total_of(ref, pair):
        zero = jnp.zeros(ref.shape[1:], F32)
        rest = (zero,) if pair else ()
        if active <= 32:
            return add_all([(ref[d], *rest) for d in range(active)])
        return lax.fori_loop(
            0, active, lambda d, a: add_parts(a, (ref[d], *rest)), (zero, *rest)
        )

    landed(first_sums, 0)
    first_total = jnp.broadcast_to(total_of(first_sums, False)[0], (8, LANES))

    def entry(i, j):
        s = place(EARLY[min(i, j), max(i, j)])
        return jnp.broadcast_to(first_total[:, s : s + 1], (8, LANES))

    first_gram = [
        [HALF_WIDTH * entry(i, j + 1) + CHAIN[j] * entry(i, j) for j in range(3)]
        for i in range(3)
    ]
    c = solve_small(first_gram, [entry(i, 0) for i in range(3)])

    def affine(c, load_at):
        return ((load_at(0) + c[0] * load_at(1)) + c[1] * load_at(2)) + c[2] * load_at(3)

    def scaled(at, size, x):
        ch, cl, rest = (const[pl.ds(q, size), :] for q in at)
        xh, xl = split(x)
        p = (ch + cl) * x
        return p, (((ch * xh - p) + ch * xl + cl * xh) + cl * xl) + rest * x

    done, weights = [], []
    for v in range(2):
        side = [
            affine(c, lambda a, s=s: const[pl.ds((4 * s + a) * 16 + 8 * v, 8), :])
            for s in range(6)
        ]
        turn = [[24 * 16 + (3 * q + part) * 16 + 8 * v for part in range(3)] for q in range(3)]
        image = [
            add_pair(scaled(turn[q], 8, side[2 + q]), scaled(turn[2], 8, side[4 + q]))
            for q in range(2)
        ]

        def times_pair(x, pair):
            p, e = two_product(x, pair[0])
            return p, e + x * pair[1]

        weight = add_pair(times_pair(side[0], image[1]), times_pair(side[1], image[0]))
        weights.append(weight)

    landed(sums, 1)
    raw_sum, lost = total_of(sums, True)
    gram_high, gram_low = two_sum(raw_sum[0:1], raw_sum[1:2] + lost[0:1])
    gram_high = jnp.broadcast_to(gram_high, (8, LANES))
    gram_low = jnp.broadcast_to(gram_low, (8, LANES))
    for weight in weights:
        high_part, low_part = two_product(gram_high, weight[0])
        pair = (high_part, low_part + (gram_high * weight[1] + gram_low * weight[0]))
        for s, times in ((32, 4), (1, 8)):
            pair = add_all(
                [[pltpu.roll(u, LANES - s * q, 1) if q else u for u in pair] for q in range(times)]
            )
        done.append(jnp.broadcast_to((pair[0] + pair[1])[:, 8:9], (8, LANES)))

    def form(f):
        return jnp.broadcast_to(done[f // 8][f % 8 : f % 8 + 1], (8, LANES))

    gram = [[form(3 * i + j) for j in range(3)] for i in range(3)]
    d = solve_small(gram, [form(9 + i) for i in range(3)])
    base_at = 24 * 16 + 9 * 16
    vector = affine(c, lambda a: const[pl.ds(base_at + 8 * a, 8), :])
    moved = affine(c, lambda a: const[pl.ds(base_at + 32 + 8 * a, 8), :])
    turn = [[base_at + 64 + 8 * (3 * q + part) for part in range(3)] for q in range(2)]
    image = add_pair(scaled(turn[0], 8, vector), scaled(turn[1], 8, moved))
    factor = jnp.where(row == 0, -d[0], jnp.where(row == 1, -d[1], jnp.where(row == 2, -d[2], 1.0)))
    coef = times_pair(factor, image)
    coef = add_pair(coef, [pltpu.roll(u, 6, 0) for u in coef])
    coef = add_pair(coef, [pltpu.roll(u, 7, 0) for u in coef])
    coef = two_sum(coef[0][0:1], coef[1][0:1])

    def spread_coef(part, k):
        return jnp.broadcast_to(coef[part][:, k : k + 1], (8, LANES))

    for slot in range(2):
        sets = [[-spread_coef(0, 32 + k) for k in range(7)]]
        if slot == 1:
            sets = [[spread_coef(part, k) for k in range(7)] for part in range(2)]
        duo = [
            [jnp.where(row < sy, w[k + 1], w[k + 2]) for w in sets] for k in range(0, 6, 2)
        ]
        for cc in range(3):
            for i in range(sx):
                v = None
                for k in range(0, 6, 2):
                    held_k = accs[mates.index((k, cc, i))]
                    u = duo[k // 2][0] * held_k
                    for extra in duo[k // 2][1:]:
                        u = u + extra * held_k
                    v = u if v is None else v + u
                start_part = raw[3 + cc, i] * raw[7, i]
                head = sets[0][0][0:sy] * start_part
                for extra in sets[1:]:
                    head = head + extra[0][0:sy] * start_part
                out_ref[slot, cc, i] = head + (v[0:sy] + v[sy : 2 * sy])


def per_device(displacement, load, material, free_node, table):
    shard = displacement.shape[1:]
    sx, sy, sz = shard
    grid = tuple(lax.axis_size(a) for a in ("gx", "gy", "gz"))
    plan = Plan(grid, shard)
    ngx, ngy, ngz = grid
    ny = ngy * sy
    groups = plan.groups
    const = jnp.asarray(tables())
    buffers = [
        pltpu.VMEM((FIELDS, sx, sy, sz), F32),
        pltpu.VMEM((2, sx, sy, sz), jnp.int32),
        pltpu.VMEM((plan.sends, plan.tiles, sy, LANES), F32),
        pltpu.VMEM((2, plan.tiles, ngx, ngy, sy, LANES), F32),
        pltpu.VMEM((7, 3, groups, ny, LANES), F32),
        pltpu.VMEM((3, groups, ny, LANES), F32),
        pltpu.VMEM((17, groups, ny, LANES), F32),
        pltpu.VMEM((2, 7, 3 * groups * ny // 8, 8, LANES), F32),
        pltpu.VMEM((ngx, ngy, 6, sy, LANES), F32),
        pltpu.VMEM((plan.returns, 6, sy, LANES), F32),
        pltpu.VMEM((plan.workers, 1, LANES), F32),
        pltpu.VMEM((plan.workers, 2, LANES), F32),
        pltpu.VMEM((3, 2, 8, LANES), F32),
        pltpu.VMEM(const.shape, F32),
        pltpu.SMEM(table.shape[::-1], F32),
        pltpu.SemaphoreType.DMA((6,)),
        pltpu.SemaphoreType.DMA((1,)),
        pltpu.SemaphoreType.DMA((2,)),
        pltpu.SemaphoreType.DMA((1,)),
        pltpu.SemaphoreType.DMA((1,)),
        pltpu.SemaphoreType.DMA((2,)),
        pltpu.SemaphoreType.DMA((2,)),
        pltpu.SemaphoreType.REGULAR,
    ]
    operands = (displacement, load, material, free_node, table.T, const)
    both = pl.pallas_call(
        functools.partial(kernel, plan),
        out_shape=jax.ShapeDtypeStruct((2,) + displacement.shape, F32),
        in_specs=[pl.BlockSpec(memory_space=pltpu.HBM)] * 6,
        out_specs=pl.BlockSpec(memory_space=pltpu.VMEM),
        scratch_shapes=buffers,
        compiler_params=pltpu.CompilerParams(
            collective_id=0, has_side_effects=True, vmem_limit_bytes=32 << 20
        ),
    )(*(pltpu.with_memory_space_constraint(a, pltpu.HBM) for a in operands))
    return both[0], both[1]


def solution(mesh):
    in_specs = (
        P(None, "gx", "gy", "gz"),
        P(None, "gx", "gy", "gz"),
        P("gx", "gy", "gz"),
        P("gx", "gy", "gz"),
        P(),
    )
    out_specs = (P(None, "gx", "gy", "gz"), P(None, "gx", "gy", "gz"))
    return jax.shard_map(
        per_device, mesh=mesh, in_specs=in_specs, out_specs=out_specs, check_vma=False
    )
```

```python
import functools

import jax
import jax.numpy as jnp
import numpy as np
from jax import lax
from jax.experimental import pallas as pl
from jax.experimental.pallas import tpu as pltpu
from jax.sharding import PartitionSpec as P

SHIFTS = (9.6, 51.4)
HALF_WIDTH = 29.5
CHAIN = SHIFTS + (30.5,) + SHIFTS + (30.5,)
STEPS = 6
FIELDS = 8
ORDER = (0, 3, 1, 4, 2, 5, 6, 7)
LANES = 128
PRODUCTS = {(i, j): t for t, (i, j) in enumerate((i, j) for i in range(6) for j in range(i, 6))}
PRODUCTS.update({(i, 6): 21 + i for i in range(5)})
FORMS = [(i, j) for i in range(3) for j in range(3)] + [(i, None) for i in range(3)]
SLOTS = [*PRODUCTS.items(), *(((5, 6), t) for t in range(28, 32))]
EARLY = {(i, j): t for t, (i, j) in enumerate((i, j) for i in range(3) for j in range(i, 4))}
F32 = jnp.float32


def place(t, base):
    return (32 * (t // 8) + base + t % 8) % LANES


def bits(x):
    top = np.asarray(x, np.float32)
    t = np.float32(4097.0) * top
    high = t - (t - top)
    return high, top - high, (x - top.astype(np.float64)).astype(np.float32)


def recurrence():
    width = 1.0 / np.float64(np.float32(1.0 / HALF_WIDTH))
    return width, np.array([np.float64(np.float32(x / HALF_WIDTH)) * width for x in CHAIN] + [0.0])


def tables(base):
    width, chain = recurrence()

    def shifted(x):
        return np.concatenate([[0.0], x[:-1]])

    def times(x):
        return chain * x + width * shifted(x)

    unit = np.eye(7)
    b = [[unit[0]] + [-times(unit[j]) for j in range(3)]]
    for j in range(2):
        b.append([(times(x) - SHIFTS[j] * x) / HALF_WIDTH for x in b[j]])
    wide = np.zeros((6, 4, 16, LANES))
    turn = np.zeros((3, 16, LANES))
    for f, (i, j) in enumerate(FORMS):
        for (one, two), t in SLOTS:
            at = place(t, base)
            turn[:, f, at] = (1.0, 1.0, 0.0) if j is None else (chain[one], chain[two], width)
            for a in range(4):
                left, right = b[i][a], b[j or 0][a]
                wide[0, a, f, at] = left[one]
                wide[1, a, f, at] = left[two] if one != two else 0.0
                wide[2, a, f, at] = right[one]
                wide[3, a, f, at] = right[two]
                wide[4, a, f, at] = shifted(right)[one]
                wide[5, a, f, at] = shifted(right)[two]
    last = np.zeros((2, 4, 8, LANES))
    final = np.zeros((2, 8, LANES))
    for k in range(7):
        final[:, :3, k] = np.array([[chain[k]], [width]])
        final[0, :3, 32 + k] = 1.0
        final[0, 3, k] = final[0, 3, 32 + k] = 1.0
        for a in range(4):
            for j in range(3):
                last[0, a, j, k] = last[0, a, j, 32 + k] = b[j][a][k]
                last[1, a, j, k] = shifted(b[j][a])[k]
            last[0, a, 3, k] = b[0][a][k]
            last[0, a, 3, 32 + k] = -1.0 if 0 < a == k + 1 else 0.0
    blocks = [wide, *(np.stack(bits(x)) for x in turn), last, *(np.stack(bits(x)) for x in final)]
    return np.concatenate([x.reshape(-1, LANES).astype(np.float32) for x in blocks])


def solve_small(gram, right):
    sym = [[0.5 * (gram[i][j] + gram[j][i]) for j in range(3)] for i in range(3)]
    r0 = 1.0 / sym[0][0]
    l10 = sym[1][0] * r0
    l20 = sym[2][0] * r0
    r1 = 1.0 / (sym[1][1] - l10 * sym[1][0])
    e = sym[2][1] - l20 * sym[1][0]
    l21 = e * r1
    d2 = sym[2][2] - l20 * sym[2][0] - l21 * e
    y1 = right[1] - l10 * right[0]
    c2 = (right[2] - l20 * right[0] - l21 * y1) / d2
    c1 = y1 * r1 - l21 * c2
    c0 = right[0] * r0 - l10 * c1 - l20 * c2
    return [c0, c1, c2]


def two_sum(a, b):
    s = a + b
    t = s - a
    return s, (a - (s - t)) + (b - t)


def add_pair(p, q):
    s, e = two_sum(p[0], q[0])
    return s, e + (p[1] + q[1])


def add_parts(p, q):
    return add_pair(p, q) if len(p) == 2 else (p[0] + q[0],)


def add_all(terms):
    while len(terms) > 1:
        rest = terms[len(terms) & ~1 :]
        terms = [add_parts(p, q) for p, q in zip(terms[::2], terms[1::2])] + rest
    return terms[0]


def split(a):
    t = 4097.0 * a
    high = t - (t - a)
    return high, a - high


def two_product(a, b):
    p = a * b
    (ah, al), (bh, bl) = split(a), split(b)
    return p, ((ah * bh - p) + ah * bl + al * bh) + al * bl


def loop(count, body):
    if count <= 32:
        for i in range(count):
            body(i)
    else:

        def step(i, carry):
            body(i)
            return carry

        lax.fori_loop(0, count, step, 0)


def when(condition, body):
    if isinstance(condition, bool):
        if condition:
            body()
    else:
        pl.when(condition)(body)


class Plan:
    def __init__(self, grid, shard):
        self.grid, self.shard = grid, shard
        ngx, ngy, ngz = grid
        sx, sy, sz = shard
        self.n = ngx * ngy
        self.nz = ngz * sz
        self.halo = STEPS
        total = self.n * ngz
        self.pitch = 1 << (-(-self.nz // total) + 2 * self.halo - 1).bit_length()
        spare = total - -(-self.nz // (self.pitch - 2 * self.halo))
        self.counts = [self.n] * (ngz - 1) + [max(2, self.n - spare)]
        self.own = -(-self.nz // sum(self.counts))
        self.span = self.own + 2 * self.halo
        self.packed = LANES // self.pitch
        self.groups = ngx * sx // self.packed
        self.mixed = LANES // (sx * self.pitch)
        self.tiles = FIELDS // self.mixed
        self.stride = LANES // (3 * sx)
        self.workers = -(-self.nz // self.own)
        self.base = [sum(self.counts[:z]) for z in range(ngz)]
        own, halo = self.own, self.halo
        self.to_low = [max(0, (sz * z - own - halo) // own + 1) for z in range(ngz)]
        self.to_high = [
            min(self.workers - 1, -(-(sz * z + sz + halo) // own) - 1) for z in range(ngz)
        ]
        self.from_low = [sz * z // own for z in range(ngz)]
        self.from_high = [(sz * z + sz - 1) // own for z in range(ngz)]
        self.sends = max(b - a + 1 for a, b in zip(self.to_low, self.to_high))
        self.returns = max(b - a + 1 for a, b in zip(self.from_low, self.from_high))
        assert sz == LANES and 8 == 2 * sy and own <= self.stride and LANES % self.pitch == 0


def pick(values, z):
    if all(v == values[0] for v in values):
        return values[0]
    out = values[0]
    for k in range(1, len(values)):
        out = jnp.where(z >= k, values[k], out)
    return out


def kernel(
    plan,
    disp_hbm,
    load_hbm,
    mat_hbm,
    free_hbm,
    table_hbm,
    const_hbm,
    out_ref,
    raw,
    flags,
    pack,
    recv,
    basis,
    fields,
    state,
    parts,
    back,
    vt,
    first_sums,
    sums,
    talls,
    square,
    const,
    table_ref,
    in_sem,
    send_sem,
    recv_sem,
    back_send,
    back_recv,
    sum_send,
    sum_recv,
    entered,
):
    ngx, ngy, ngz = plan.grid
    sx, sy, sz = plan.shard
    n, own, halo, pitch = plan.n, plan.own, plan.halo, plan.pitch
    nx, ny = ngx * sx, ngy * sy
    groups, mixed, tiles = plan.groups, plan.mixed, plan.tiles
    total = n * ngz
    gx, gy, gz = lax.axis_index("gx"), lax.axis_index("gy"), lax.axis_index("gz")
    p = gx * ngy + gy
    me = p * ngz + gz
    count = pick(plan.counts, gz)
    worker = pick(plan.base, gz) + count - 1 - p
    is_worker = (p < count) & (worker < plan.workers)
    first = own * worker - halo
    settled = jnp.maximum(first, 0)
    low_slab = jnp.minimum(lax.div(settled, sz), ngz - 1)
    edge = sz * (low_slab + 1)
    two = (first + plan.span > edge) & (low_slab + 1 < ngz)
    last = total - 1

    fetched = [
        pltpu.make_async_copy(disp_hbm, raw.at[pl.ds(0, 3)], in_sem.at[0]),
        pltpu.make_async_copy(load_hbm, raw.at[pl.ds(3, 3)], in_sem.at[1]),
        pltpu.make_async_copy(mat_hbm, flags.at[0], in_sem.at[2]),
        pltpu.make_async_copy(free_hbm, flags.at[1], in_sem.at[3]),
        pltpu.make_async_copy(table_hbm, table_ref, in_sem.at[4]),
        pltpu.make_async_copy(const_hbm, const, in_sem.at[5]),
    ]
    for copy in fetched:
        copy.start()

    def where_is(d):
        return dict(device_id=d, device_id_type=pl.DeviceIdType.LOGICAL)

    barrier = pltpu.get_barrier_semaphore()

    def greet(d):
        pl.semaphore_signal(barrier, inc=1, **where_is(d))

    def greet_slab(z):
        def one(q):
            d = q * ngz + z
            when((d != me) & (d != last), lambda: greet(d))

        loop(n, one)

    when(is_worker, lambda: greet_slab(low_slab))
    when(is_worker & two, lambda: greet_slab(low_slab + 1))
    when(me != last, lambda: greet(last))

    for copy in fetched[:4]:
        copy.wait()
    raw[6] = flags[0].astype(F32)
    raw[7] = flags[1].astype(F32)

    lane = lax.broadcasted_iota(jnp.int32, (8, LANES), 1)
    row = lax.broadcasted_iota(jnp.int32, (8, LANES), 0)
    per = 8 // sy
    stacks = -(-tiles // per)
    held = []
    for t in range(stacks):
        part = []
        for e in range(mixed * sx):
            f, i = e // sx, e % sx
            rows = [
                raw[ORDER[mixed * min(per * t + h, tiles - 1) + f], i] for h in range(per)
            ]
            part.append(jnp.concatenate(rows, axis=0))
        turned = []
        for e in range(mixed * sx):
            v = part[e]
            for k in range(1, mixed):
                v = jnp.where(lax.rem(gx, mixed) == k, part[(e - k * sx) % (mixed * sx)], v)
            turned.append(v)
        held.append(turned)

    to_low = pick(plan.to_low, gz)
    to_count = pick([b - a + 1 for a, b in zip(plan.to_low, plan.to_high)], gz)

    def route(j):
        w = to_low + j
        z = 0
        for k in range(1, ngz):
            z = z + jnp.where(w >= plan.base[k], 1, 0)
        q = pick([b + c - 1 for b, c in zip(plan.base, plan.counts)], z) - w
        slot = jnp.where(sz * gz > jnp.maximum(own * w - halo, 0), 1, 0)
        return j < to_count, slot, q * ngz + z

    def prepare(j):
        w = to_low + j
        offset = sz * gz - (own * w - halo)
        for t in range(stacks):
            out = None
            for e, v in enumerate(held[t]):
                moved = pltpu.roll(v, lax.rem(offset + (pitch * e + 8 * LANES), LANES), 1)
                out = moved if out is None else jnp.where(lane >= pitch * e, moved, out)
            for h in range(min(per, tiles - per * t)):
                pack[j, per * t + h] = out[sy * h : sy * (h + 1)]

    loop(plan.sends, prepare)

    expected = to_count
    if plan.sends <= 32:
        routes = [route(j) for j in range(plan.sends)]
        for valid, _, d in routes:
            expected = expected - jnp.where(valid & (d == me), 1, 0)
    else:
        routes = None

        def count_self(j, seen):
            valid, _, d = route(j)
            return seen - jnp.where(valid & (d == me), 1, 0)

        expected = lax.fori_loop(0, plan.sends, count_self, expected)
    expected = jnp.where(me == last, total - 1, expected)
    pl.semaphore_wait(barrier, expected)

    def piece(j, start):
        valid, slot, d = routes[j] if routes else route(j)
        dst = recv.at[slot, :, gx, gy]
        remote = pltpu.make_async_remote_copy(
            src_ref=pack.at[j],
            dst_ref=dst,
            send_sem=send_sem.at[0],
            recv_sem=recv_sem.at[slot],
            **where_is(d),
        )
        if start:
            when(valid & (d != me), remote.start)
            when(
                valid & (d == me),
                lambda: pltpu.make_async_copy(pack.at[j], dst, recv_sem.at[slot]).start(),
            )
        else:
            when(valid & (d != me), remote.wait_send)

    loop(plan.sends, lambda j: piece(j, True))

    def announce():
        loop(total - 1, lambda d: pl.semaphore_signal(entered, inc=1, **where_is(d)))

    when(me == last, announce)

    def settle(ref, sem):
        pltpu.make_async_copy(ref, ref, sem).wait()

    def share(ref, slot, d):
        when(
            me != d,
            pltpu.make_async_remote_copy(
                src_ref=ref.at[worker],
                dst_ref=ref.at[worker],
                send_sem=sum_send.at[slot],
                recv_sem=sum_recv.at[slot],
                **where_is(d),
            ).start,
        )

    def work():
        settle(recv.at[0], recv_sem.at[0])
        when(two, lambda: settle(recv.at[1], recv_sem.at[1]))

        wide_lane = lax.broadcasted_iota(jnp.int32, (ny, LANES), 1)
        depth = lax.rem(wide_lane, pitch)
        plane = depth + first
        near = plane < edge
        seg = sx * pitch

        def gather_rows(slot, k, x):
            return jnp.concatenate([recv[slot, k, x, g] for g in range(ngy)], axis=0)

        def source(k, x):
            return jnp.where(near, gather_rows(0, k, x), gather_rows(1, k, x))

        def unpack(k, g):
            parts_in = [source(k, g * mixed + d) for d in range(mixed)]
            out = []
            for f in range(mixed):
                v = None
                for at in range(mixed):
                    u = parts_in[(at - f) % mixed]
                    v = u if v is None else jnp.where(wide_lane >= at * seg, u, v)
                out.append(pltpu.roll(v, LANES - f * seg, 1) if f else v)
            return out

        got = [[None] * groups for _ in range(FIELDS)]
        for g in range(groups):
            for k in range(tiles):
                for f, v in enumerate(unpack(k, g)):
                    got[ORDER[mixed * k + f]][g] = v

        span = range(groups)

        def next_y(a):
            return [pltpu.roll(v, ny - 1, 0) for v in a]

        def last_y(a):
            return [pltpu.roll(v, 1, 0) for v in a]

        def forward(a, x, z):
            moved = [pltpu.roll(v, LANES - pitch * x - z, 1) for v in a]
            if groups == 1 or not x:
                return moved
            wrap = wide_lane >= LANES - pitch
            return [jnp.where(wrap, moved[min(g + 1, groups - 1)], moved[g]) for g in span]

        def backward(a, x, z):
            moved = [pltpu.roll(v, pitch * x + z, 1) for v in a]
            if groups == 1 or not x:
                return moved
            wrap = wide_lane < pitch
            return [jnp.where(wrap, moved[max(g - 1, 0)], moved[g]) for g in span]

        def both(op, *lists):
            return [op(*vs) for vs in zip(*lists)]

        add = functools.partial(both, lambda a, b: a + b)
        sub = functools.partial(both, lambda a, b: a - b)

        def gradient(vector):
            grad = []
            for v in vector:
                above, over, far = forward(v, 0, 1), forward(v, 1, 0), forward(v, 1, 1)
                near_z, far_z = add(v, above), add(over, far)
                wide, flat = sub(far_z, near_z), add(far_z, near_z)
                rise = add(sub(above, v), sub(far, over))
                grad.append([add(next_y(wide), wide), sub(next_y(flat), flat), add(next_y(rise), rise)])
            return grad

        pairs = [(0, 0), (0, 1), (0, 2), (1, 1), (1, 2), (2, 2)]
        free = got[7]
        for c in range(3):
            for g in span:
                basis[0, c, g] = got[3 + c][g] * free[g]
        grad = gradient([got[0], got[1], got[2]])
        mass = []
        high = lax.broadcasted_iota(jnp.int32, (ny, LANES), 0)
        for g in span:
            valid = (high <= ny - 2) & (plane >= 0) & (plane <= plan.nz - 2) & (depth <= plan.span - 2)
            valid = valid & (lax.div(wide_lane, pitch) + g * plan.packed <= nx - 2)
            material = got[6][g]
            zero = jnp.zeros((ny, LANES), F32)
            lame, shear, heavy = zero, zero, zero
            for r in range(table_ref.shape[1]):
                hit = material == float(r)
                lame = jnp.where(hit, table_ref[0, r], lame)
                shear = jnp.where(hit, table_ref[1, r], shear)
                heavy = jnp.where(hit, table_ref[2, r], heavy)
            lame = jnp.where(valid, lame * 0.0625, 0.0)
            shear = jnp.where(valid, shear * 0.0625, 0.0)
            mass.append(jnp.where(valid, heavy * 0.125, 0.0))
            frame = [
                [0.25 * grad[i][j][g] + (1.0 if i == j else 0.0) for j in range(3)] for i in range(3)
            ]
            strain = {}
            for i, j in pairs:
                v = sum(frame[k][i] * frame[k][j] for k in range(3))
                strain[i, j] = 0.5 * (v - 1.0 if i == j else v)
            bulk = lame * (strain[0, 0] + strain[1, 1] + strain[2, 2])
            for i in range(3):
                for j in range(3):
                    state[3 * i + j, g] = frame[i][j]
            for spot, (i, j) in enumerate(pairs):
                v = 2.0 * shear * strain[i, j]
                state[9 + spot, g] = v + bulk if i == j else v
            state[15, g] = lame
            state[16, g] = shear
        mass = add(mass, last_y(mass))
        mass = add(
            add(mass, backward(mass, 0, 1)), add(backward(mass, 1, 0), backward(mass, 1, 1))
        )
        for g in span:
            fields[0, g] = free[g]
            fields[1, g] = free[g] * (1.0 / HALF_WIDTH)
            fields[2, g] = (free[g] * mass[g] + (1.0 - free[g])) * (1.0 / HALF_WIDTH)

        rows8 = [pl.ds(8 * r, 8) for r in range(ny // 8)]

        def stress(j):
            grad = gradient([[basis[j, c, g] * fields[0, g] for g in span] for c in range(3)])
            pio = [[[[None] * len(rows8) for _ in span] for _ in range(3)] for _ in range(3)]
            for g in span:
                for r, at in enumerate(rows8):
                    d = [[grad[c][q][g][8 * r : 8 * r + 8] for q in range(3)] for c in range(3)]
                    f = [[state[3 * i + k, g, at] for k in range(3)] for i in range(3)]
                    pulled = [
                        [sum(f[k][a] * d[k][b] for k in range(3)) for b in range(3)] for a in range(3)
                    ]
                    lame, shear = state[15, g, at], state[16, g, at]
                    bulk = lame * (pulled[0][0] + pulled[1][1] + pulled[2][2])
                    t, s = {}, {}
                    for spot, (a, b) in enumerate(pairs):
                        v = shear * (pulled[a][b] + pulled[b][a])
                        t[a, b] = t[b, a] = v + bulk if a == b else v
                        s[a, b] = s[b, a] = state[9 + spot, g, at]
                    for i in range(3):
                        for b in range(3):
                            v = sum(f[i][k] * t[k, b] for k in range(3))
                            pio[i][b][g][r] = v + sum(d[i][k] * s[k, b] for k in range(3))
            pio = [[[jnp.concatenate(pio[c][b][g], axis=0) for g in span] for b in range(3)] for c in range(3)]
            return grad, pio

        def scatter(j, pio):
            for c in range(3):
                e = pio[c]
                wide = add(e[0], last_y(e[0]))
                tilt = sub(last_y(e[1]), e[1])
                rise = add(e[2], last_y(e[2]))
                minus, plus = sub(tilt, wide), add(tilt, wide)
                out = add(
                    add(sub(minus, rise), backward(add(minus, rise), 0, 1)),
                    add(backward(sub(plus, rise), 1, 0), backward(add(plus, rise), 1, 1)),
                )
                for g in span:
                    basis[j + 1, c, g] = fields[1, g] * out[g] + (
                        fields[2, g] - CHAIN[j] / HALF_WIDTH
                    ) * basis[j, c, g]

        def apply(j):
            scatter(j, stress(j)[1])

        mine = (depth >= halo) & (depth < halo + own) & (plane < plan.nz)
        spots = [(c, g, r) for c in range(3) for g in span for r in range(ny // 8)]
        mine = [mine[8 * r : 8 * r + 8] for r in range(ny // 8)]

        def divide(k):
            v = [jnp.where(mine[r], basis[k, c, g, rows8[r]], 0.0) for c, g, r in spots]
            top = jnp.abs(v[0])
            for u in v[1:]:
                top = jnp.maximum(top, jnp.abs(u))
            grain = top * (32768.0 * max(1, len(v) // 6))
            for s, u in enumerate(v):
                coarse = (u + grain) - grain
                parts[0, k, s] = coarse
                parts[1, k, s] = u - coarse

        def products(i, js):
            acc = {}
            for s in range(len(spots)):
                ch, cl = parts[0, i, s], parts[1, i, s]
                for j in js:
                    dh, dl = parts[0, j, s], parts[1, j, s]
                    new = [ch * dh, cl * (dh + ch + dl) if i == j else ch * dl + cl * (dh + dl)]
                    acc[j] = new if s == 0 else [acc[j][0] + new[0], acc[j][1] + new[1]]
            return {(i, j): tuple(acc[j]) for j in js}

        def merge(a, b, mask, shift):
            first_in, second_in = [], []
            for u, v in zip(a, b):
                if shift == 4:
                    first_in.append(jnp.where(mask, u, v))
                    second_in.append(pltpu.roll(jnp.where(mask, v, u), shift, 0))
                else:
                    first_in.append(jnp.where(mask, u, pltpu.roll(v, shift, 0)))
                    second_in.append(jnp.where(mask, pltpu.roll(u, 8 - shift, 0), v))
            return add_parts(tuple(first_in), tuple(second_in))

        def stack(items, slots):
            none = tuple(jnp.zeros((8, LANES), F32) for _ in next(iter(items.values())))
            it = [items.get(q, none) for q in slots]
            one = [merge(it[r], it[r + 4], row < 4, 4) for r in range(4)]
            twice = [merge(one[r], one[r + 2], lax.rem(row, 4) < 2, 2) for r in range(2)]
            return merge(twice[0], twice[1], lax.rem(row, 2) < 1, 1)

        def slots_of(table, q):
            at = {t: pair for pair, t in table.items()}
            return [at.get(8 * q + r) for r in range(8)]

        quarter = lane // 32

        def fold(tall):
            def turned(j):
                out = []
                for part in range(len(tall[0])):
                    v = None
                    for q in range(len(tall)):
                        u = tall[q][part]
                        u = pltpu.roll(u, LANES - 32 * j, 1) if j else u
                        v = u if v is None else jnp.where(quarter >= q, u, v)
                    out.append(v)
                return tuple(out)

            whole = add_all([turned(j) for j in range(4)])
            whole = add_all(
                [
                    tuple(pltpu.roll(u, own - j, 1, stride=1, stride_axis=0) for u in whole)
                    for j in range(own)
                ]
            )
            keep = lax.rem(lane + (2 * LANES - halo - own) - row, 32) == 0
            keep = keep & (lax.rem(lane + (LANES - halo - own) - row, LANES) < 32 * len(tall))
            return [jnp.sum(jnp.where(keep, u, 0.0), axis=0, keepdims=True) for u in whole]

        items = {}
        for k in range(STEPS):
            divide(k)
            for i in range(k + 1):
                items.update(products(i, [k]))
            if k == 3:
                single = {q: (items[q][0] + items[q][1],) for q in EARLY}
                early = [stack(single, slots_of(EARLY, q)) for q in range(2)]
                first_sums[worker] = fold(early)[0]
            if k < STEPS - 1:
                apply(k)
        width, chain = recurrence()
        for i in range(5):
            up, same = items[i + 1, 5], items[i, 5]
            factor = float((chain[i] - chain[5]) / width)
            high_part, low_part = two_sum(up[0], factor * same[0])
            items[i, 6] = (high_part, low_part + (up[1] + factor * same[1]))
        for q in range(4):
            high_part, low_part = stack(items, slots_of(PRODUCTS, q))
            talls[q, 0] = high_part
            talls[q, 1] = low_part
        square[0] = items[5, 5][0]
        square[1] = items[5, 5][1]
        when(me != last, lambda: pl.semaphore_wait(entered, 1))
        loop(total, lambda d: share(first_sums, 0, d))
        grad, pio = stress(5)
        energy = None
        for g in span:
            dense = sum(pio[c][b][g] * grad[c][b][g] for c in range(3) for b in range(3))
            for r in range(ny // 8):
                v = [basis[5, c, g, rows8[r]] for c in range(3)]
                nodes = fields[2, g, rows8[r]] * (v[0] * v[0] + v[1] * v[1] + v[2] * v[2])
                u = dense[8 * r : 8 * r + 8] * (1.0 / HALF_WIDTH) + nodes
                u = jnp.where(mine[r], u, 0.0)
                energy = u if energy is None else energy + u
        factor = float(-chain[5] / width)
        high_part, low_part = two_sum(energy, factor * square[0])
        ends = (high_part, low_part + factor * square[1])
        ends = add_pair(ends, [pltpu.roll(u, 4, 0) for u in ends])
        tall = [(talls[q, 0], talls[q, 1]) for q in range(3)]
        tall.append(tuple(jnp.where(row < 4, talls[3, p], ends[p]) for p in range(2)))
        sums[worker] = jnp.concatenate(fold(tall), axis=0)
        loop(total, lambda d: share(sums, 1, d))
        scatter(5, pio)

    fetched[4].wait()
    when(is_worker, work)
    when(
        jnp.logical_not(is_worker) & (me != last), lambda: pl.semaphore_wait(entered, 1)
    )

    stride = plan.stride

    def give_back():
        wide_lane = lax.broadcasted_iota(jnp.int32, (ny, LANES), 1)
        for k in range(1, 7):
            for x in range(ngx):
                g, d = x // mixed, x % mixed
                out = None
                for c in range(3):
                    for i in range(sx):
                        e = c * sx + i
                        s = (e * stride - ((d * sx + i) * pitch + halo)) % LANES
                        v = basis[k, c, g]
                        moved = pltpu.roll(v, s, 1) if s else v
                        out = moved if out is None else jnp.where(wide_lane >= e * stride, moved, out)
                for y in range(ngy):
                    back[x, y, k - 1] = out[sy * y : sy * (y + 1)]
        loop(n, lambda q: give(q, True))

    own_low = jnp.minimum(lax.div(own * worker, sz), ngz - 1)
    own_high = lax.div(jnp.minimum(own * worker + own, plan.nz) - 1, sz)
    straddles = sz % own != 0

    def give(q, start):
        x, y = (q // ngy, q % ngy) if isinstance(q, int) else (lax.div(q, ngy), lax.rem(q, ngy))

        def to(z):
            d = q * ngz + z
            dst = vt.at[worker - pick(plan.from_low, z)]
            remote = pltpu.make_async_remote_copy(
                src_ref=back.at[x, y],
                dst_ref=dst,
                send_sem=back_send.at[0],
                recv_sem=back_recv.at[0],
                **where_is(d),
            )
            if start:
                when(d != me, remote.start)
                when(
                    d == me,
                    lambda: pltpu.make_async_copy(back.at[x, y], dst, back_recv.at[0]).start(),
                )
            else:
                when(d != me, remote.wait_send)

        to(own_low)
        if straddles:
            when(own_high > own_low, lambda: to(own_high))

    when(is_worker, give_back)
    fetched[5].wait()

    counts = [b - a + 1 for a, b in zip(plan.from_low, plan.from_high)]
    if min(counts) == plan.returns:
        settle(vt, back_recv.at[0])
    else:
        for z in range(ngz):
            when(gz == z, lambda z=z: settle(vt.at[pl.ds(0, counts[z])], back_recv.at[0]))

    mates = [(k, c, i) for k in range(0, 6, 2) for c in range(3) for i in range(sx)]

    def collect(j, accs):
        w = pick(plan.from_low, gz) + j
        offset = own * w - sz * gz
        inside = (lane >= offset) & (lane < offset + own)
        if min(counts) != plan.returns:
            inside = inside & (j < pick(counts, gz))
        new = []
        stacked = [jnp.concatenate([vt[j, k], vt[j, k + 1]], axis=0) for k in range(0, 6, 2)]
        for (k, c, i), acc in zip(mates, accs):
            s = lax.rem(offset - (c * sx + i) * stride + 2 * LANES, LANES)
            moved = pltpu.roll(stacked[k // 2], s, 1)
            new.append(jnp.where(inside, moved, acc))
        return tuple(new)

    accs = tuple(jnp.zeros((8, LANES), F32) for _ in mates)
    if plan.returns <= 16:
        for j in range(plan.returns):
            accs = collect(j, accs)
    else:
        accs = lax.fori_loop(0, plan.returns, collect, accs)

    active = plan.workers

    def wait_rows(ref, sem, rows):
        while rows:
            now = min(rows, active)
            settle(ref.at[pl.ds(0, now)], sem)
            rows -= now

    def sent():
        loop(n, lambda q: give(q, False))
        wait_rows(first_sums, sum_send.at[0], total - 1)
        wait_rows(sums, sum_send.at[1], total - 1)

    loop(plan.sends, lambda j: piece(j, False))
    when(is_worker, sent)

    def landed(ref, slot):
        when(is_worker, lambda: wait_rows(ref, sum_recv.at[slot], active - 1))
        when(jnp.logical_not(is_worker), lambda: wait_rows(ref, sum_recv.at[slot], active))

    def total_of(ref, pair):
        zero = jnp.zeros(ref.shape[1:], F32)
        rest = (zero,) if pair else ()
        if active <= 32:
            return add_all([(ref[d], *rest) for d in range(active)])
        return lax.fori_loop(
            0, active, lambda d, a: add_parts(a, (ref[d], *rest)), (zero, *rest)
        )

    landed(first_sums, 0)
    first_total = jnp.broadcast_to(total_of(first_sums, False)[0], (8, LANES))

    def entry(i, j):
        s = place(EARLY[min(i, j), max(i, j)], halo + own)
        return jnp.broadcast_to(first_total[:, s : s + 1], (8, LANES))

    first_gram = [
        [HALF_WIDTH * entry(i, j + 1) + CHAIN[j] * entry(i, j) for j in range(3)]
        for i in range(3)
    ]
    c = solve_small(first_gram, [entry(i, 0) for i in range(3)])

    def affine(c, load_at):
        return ((load_at(0) + c[0] * load_at(1)) + c[1] * load_at(2)) + c[2] * load_at(3)

    def scaled(at, size, x):
        ch, cl, rest = (const[pl.ds(q, size), :] for q in at)
        xh, xl = split(x)
        p = (ch + cl) * x
        return p, (((ch * xh - p) + ch * xl + cl * xh) + cl * xl) + rest * x

    def times_pair(x, pair):
        p, e = two_product(x, pair[0])
        return p, e + x * pair[1]

    weights = []
    for v in range(2):
        side = [
            affine(c, lambda a, s=s: const[pl.ds((4 * s + a) * 16 + 8 * v, 8), :])
            for s in range(6)
        ]
        turn = [[24 * 16 + (3 * q + part) * 16 + 8 * v for part in range(3)] for q in range(3)]
        image = [
            add_pair(scaled(turn[q], 8, side[2 + q]), scaled(turn[2], 8, side[4 + q]))
            for q in range(2)
        ]
        weights.append(add_pair(times_pair(side[0], image[1]), times_pair(side[1], image[0])))

    landed(sums, 1)
    raw_sum, lost = total_of(sums, True)
    gram_high, gram_low = two_sum(raw_sum[0:1], raw_sum[1:2] + lost[0:1])
    gram_high = jnp.broadcast_to(gram_high, (8, LANES))
    gram_low = jnp.broadcast_to(gram_low, (8, LANES))
    done = []
    for weight in weights:
        high_part, low_part = two_product(gram_high, weight[0])
        pair = (high_part, low_part + (gram_high * weight[1] + gram_low * weight[0]))
        for s, times in ((32, 4), (1, 8)):
            pair = add_all(
                [[pltpu.roll(u, LANES - s * q, 1) if q else u for u in pair] for q in range(times)]
            )
        done.append(
            jnp.broadcast_to((pair[0] + pair[1])[:, halo + own : halo + own + 1], (8, LANES))
        )
    form = {
        q: jnp.broadcast_to(done[f // 8][f % 8 : f % 8 + 1], (8, LANES))
        for f, q in enumerate(FORMS)
    }
    gram = [[form[i, j] for j in range(3)] for i in range(3)]
    d = solve_small(gram, [form[i, None] for i in range(3)])
    base_at = 24 * 16 + 9 * 16
    vector = affine(c, lambda a: const[pl.ds(base_at + 8 * a, 8), :])
    moved = affine(c, lambda a: const[pl.ds(base_at + 32 + 8 * a, 8), :])
    turn = [[base_at + 64 + 8 * (3 * q + part) for part in range(3)] for q in range(2)]
    image = add_pair(scaled(turn[0], 8, vector), scaled(turn[1], 8, moved))
    factor = jnp.where(row == 0, -d[0], jnp.where(row == 1, -d[1], jnp.where(row == 2, -d[2], 1.0)))
    coef = times_pair(factor, image)
    coef = add_pair(coef, [pltpu.roll(u, 6, 0) for u in coef])
    coef = add_pair(coef, [pltpu.roll(u, 7, 0) for u in coef])
    coef = coef[0][0:1] + coef[1][0:1]

    def spread_coef(k):
        return jnp.broadcast_to(coef[:, k : k + 1], (8, LANES))

    for slot in range(2):
        w = [spread_coef(k) if slot else -spread_coef(32 + k) for k in range(7)]
        duo = [jnp.where(row < sy, w[k + 1], w[k + 2]) for k in range(0, 6, 2)]
        for cc in range(3):
            for i in range(sx):
                v = None
                for k in range(0, 6, 2):
                    u = duo[k // 2] * accs[mates.index((k, cc, i))]
                    v = u if v is None else v + u
                head = w[0][0:sy] * (raw[3 + cc, i] * raw[7, i])
                out_ref[slot, cc, i] = head + (v[0:sy] + v[sy : 2 * sy])


def per_device(displacement, load, material, free_node, table):
    shard = displacement.shape[1:]
    sx, sy, sz = shard
    grid = tuple(lax.axis_size(a) for a in ("gx", "gy", "gz"))
    plan = Plan(grid, shard)
    ngx, ngy, ngz = grid
    ny = ngy * sy
    groups = plan.groups
    const = jnp.asarray(tables(plan.halo + plan.own))
    buffers = [
        pltpu.VMEM((FIELDS, sx, sy, sz), F32),
        pltpu.VMEM((2, sx, sy, sz), jnp.int32),
        pltpu.VMEM((plan.sends, plan.tiles, sy, LANES), F32),
        pltpu.VMEM((2, plan.tiles, ngx, ngy, sy, LANES), F32),
        pltpu.VMEM((7, 3, groups, ny, LANES), F32),
        pltpu.VMEM((3, groups, ny, LANES), F32),
        pltpu.VMEM((17, groups, ny, LANES), F32),
        pltpu.VMEM((2, 7, 3 * groups * ny // 8, 8, LANES), F32),
        pltpu.VMEM((ngx, ngy, 6, sy, LANES), F32),
        pltpu.VMEM((plan.returns, 6, sy, LANES), F32),
        pltpu.VMEM((plan.workers, 1, LANES), F32),
        pltpu.VMEM((plan.workers, 2, LANES), F32),
        pltpu.VMEM((4, 2, 8, LANES), F32),
        pltpu.VMEM((2, 8, LANES), F32),
        pltpu.VMEM(const.shape, F32),
        pltpu.SMEM(table.shape[::-1], F32),
        pltpu.SemaphoreType.DMA((6,)),
        pltpu.SemaphoreType.DMA((1,)),
        pltpu.SemaphoreType.DMA((2,)),
        pltpu.SemaphoreType.DMA((1,)),
        pltpu.SemaphoreType.DMA((1,)),
        pltpu.SemaphoreType.DMA((2,)),
        pltpu.SemaphoreType.DMA((2,)),
        pltpu.SemaphoreType.REGULAR,
    ]
    operands = (displacement, load, material, free_node, table.T, const)
    both = pl.pallas_call(
        functools.partial(kernel, plan),
        out_shape=jax.ShapeDtypeStruct((2,) + displacement.shape, F32),
        in_specs=[pl.BlockSpec(memory_space=pltpu.HBM)] * 6,
        out_specs=pl.BlockSpec(memory_space=pltpu.VMEM),
        scratch_shapes=buffers,
        compiler_params=pltpu.CompilerParams(
            collective_id=0, has_side_effects=True, vmem_limit_bytes=32 << 20
        ),
    )(*(pltpu.with_memory_space_constraint(a, pltpu.HBM) for a in operands))
    return both[0], both[1]


def solution(mesh):
    in_specs = (
        P(None, "gx", "gy", "gz"),
        P(None, "gx", "gy", "gz"),
        P("gx", "gy", "gz"),
        P("gx", "gy", "gz"),
        P(),
    )
    out_specs = (P(None, "gx", "gy", "gz"), P(None, "gx", "gy", "gz"))
    return jax.shard_map(
        per_device, mesh=mesh, in_specs=in_specs, out_specs=out_specs, check_vma=False
    )
```

```python
import functools

import jax
import jax.numpy as jnp
import numpy as np
from jax import lax
from jax.experimental import pallas as pl
from jax.experimental.pallas import tpu as pltpu
from jax.sharding import PartitionSpec as P

SHIFTS = (9.6, 51.4)
HALF_WIDTH = 29.5
CHAIN = SHIFTS + (30.5,) + SHIFTS + (30.5,)
STEPS = 6
FIELDS = 8
ORDER = (0, 3, 1, 4, 2, 5, 6, 7)
LANES = 128
PRODUCTS = {(i, j): t for t, (i, j) in enumerate((i, j) for i in range(6) for j in range(i, 6))}
PRODUCTS.update({(i, 6): 21 + i for i in range(5)})
FORMS = [(i, j) for i in range(3) for j in range(3)] + [(i, None) for i in range(3)]
SLOTS = [*PRODUCTS.items(), *(((5, 6), t) for t in range(28, 32))]
EARLY = {(i, j): t for t, (i, j) in enumerate((i, j) for i in range(3) for j in range(i, 4))}
F32 = jnp.float32


def place(t, base):
    return (32 * (t // 8) + base + t % 8) % LANES


def bits(x):
    top = np.asarray(x, np.float32)
    t = np.float32(4097.0) * top
    high = t - (t - top)
    return high, top - high, (x - top.astype(np.float64)).astype(np.float32)


def recurrence():
    width = 1.0 / np.float64(np.float32(1.0 / HALF_WIDTH))
    return width, np.array([np.float64(np.float32(x / HALF_WIDTH)) * width for x in CHAIN] + [0.0])


def tables(base):
    width, chain = recurrence()

    def shifted(x):
        return np.concatenate([[0.0], x[:-1]])

    def times(x):
        return chain * x + width * shifted(x)

    unit = np.eye(7)
    b = [[unit[0]] + [-times(unit[j]) for j in range(3)]]
    for j in range(2):
        b.append([(times(x) - SHIFTS[j] * x) / HALF_WIDTH for x in b[j]])
    wide = np.zeros((6, 4, 16, LANES))
    turn = np.zeros((3, 16, LANES))
    for f, (i, j) in enumerate(FORMS):
        for (one, two), t in SLOTS:
            at = place(t, base)
            turn[:, f, at] = (1.0, 1.0, 0.0) if j is None else (chain[one], chain[two], width)
            for a in range(4):
                left, right = b[i][a], b[j or 0][a]
                wide[0, a, f, at] = left[one]
                wide[1, a, f, at] = left[two] if one != two else 0.0
                wide[2, a, f, at] = right[one]
                wide[3, a, f, at] = right[two]
                wide[4, a, f, at] = shifted(right)[one]
                wide[5, a, f, at] = shifted(right)[two]
    last = np.zeros((2, 4, 8, LANES))
    final = np.zeros((2, 8, LANES))
    for k in range(7):
        final[:, :3, k] = np.array([[chain[k]], [width]])
        final[0, :3, 32 + k] = 1.0
        final[0, 3, k] = final[0, 3, 32 + k] = 1.0
        for a in range(4):
            for j in range(3):
                last[0, a, j, k] = last[0, a, j, 32 + k] = b[j][a][k]
                last[1, a, j, k] = shifted(b[j][a])[k]
            last[0, a, 3, k] = b[0][a][k]
            last[0, a, 3, 32 + k] = -1.0 if 0 < a == k + 1 else 0.0
    blocks = [wide, *(np.stack(bits(x)) for x in turn), last, *(np.stack(bits(x)) for x in final)]
    return np.concatenate([x.reshape(-1, LANES).astype(np.float32) for x in blocks])


def solve_small(gram, right):
    sym = [[0.5 * (gram[i][j] + gram[j][i]) for j in range(3)] for i in range(3)]
    r0 = 1.0 / sym[0][0]
    l10 = sym[1][0] * r0
    l20 = sym[2][0] * r0
    r1 = 1.0 / (sym[1][1] - l10 * sym[1][0])
    e = sym[2][1] - l20 * sym[1][0]
    l21 = e * r1
    d2 = sym[2][2] - l20 * sym[2][0] - l21 * e
    y1 = right[1] - l10 * right[0]
    c2 = (right[2] - l20 * right[0] - l21 * y1) / d2
    c1 = y1 * r1 - l21 * c2
    c0 = right[0] * r0 - l10 * c1 - l20 * c2
    return [c0, c1, c2]


def two_sum(a, b):
    s = a + b
    t = s - a
    return s, (a - (s - t)) + (b - t)


def add_pair(p, q):
    s, e = two_sum(p[0], q[0])
    return s, e + (p[1] + q[1])


def add_parts(p, q):
    return add_pair(p, q) if len(p) == 2 else (p[0] + q[0],)


def add_all(terms):
    while len(terms) > 1:
        rest = terms[len(terms) & ~1 :]
        terms = [add_parts(p, q) for p, q in zip(terms[::2], terms[1::2])] + rest
    return terms[0]


def split(a):
    t = 4097.0 * a
    high = t - (t - a)
    return high, a - high


def two_product(a, b):
    p = a * b
    (ah, al), (bh, bl) = split(a), split(b)
    return p, ((ah * bh - p) + ah * bl + al * bh) + al * bl


def loop(count, body):
    if count <= 32:
        for i in range(count):
            body(i)
    else:

        def step(i, carry):
            body(i)
            return carry

        lax.fori_loop(0, count, step, 0)


def when(condition, body):
    if isinstance(condition, bool):
        if condition:
            body()
    else:
        pl.when(condition)(body)


class Plan:
    def __init__(self, grid, shard):
        self.grid, self.shard = grid, shard
        ngx, ngy, ngz = grid
        sx, sy, sz = shard
        self.n = ngx * ngy
        self.nz = ngz * sz
        self.halo = STEPS
        total = self.n * ngz
        self.pitch = 1 << (-(-self.nz // total) + 2 * self.halo - 1).bit_length()
        spare = total - -(-self.nz // (self.pitch - 2 * self.halo))
        self.counts = [self.n] * (ngz - 1) + [max(2, self.n - spare)]
        self.own = -(-self.nz // sum(self.counts))
        self.span = self.own + 2 * self.halo
        self.packed = LANES // self.pitch
        self.groups = ngx * sx // self.packed
        self.mixed = LANES // (sx * self.pitch)
        self.tiles = FIELDS // self.mixed
        self.stride = LANES // (3 * sx)
        self.workers = -(-self.nz // self.own)
        self.base = [sum(self.counts[:z]) for z in range(ngz)]
        own, halo = self.own, self.halo
        self.to_low = [max(0, (sz * z - own - halo) // own + 1) for z in range(ngz)]
        self.to_high = [
            min(self.workers - 1, -(-(sz * z + sz + halo) // own) - 1) for z in range(ngz)
        ]
        self.from_low = [sz * z // own for z in range(ngz)]
        self.from_high = [(sz * z + sz - 1) // own for z in range(ngz)]
        self.sends = max(b - a + 1 for a, b in zip(self.to_low, self.to_high))
        self.returns = max(b - a + 1 for a, b in zip(self.from_low, self.from_high))
        assert sz == LANES and 8 == 2 * sy and own <= self.stride and halo + own <= 56


def pick(values, z):
    if all(v == values[0] for v in values):
        return values[0]
    out = values[0]
    for k in range(1, len(values)):
        out = jnp.where(z >= k, values[k], out)
    return out


def kernel(
    plan,
    disp_hbm,
    load_hbm,
    mat_hbm,
    free_hbm,
    table_hbm,
    const_hbm,
    out_ref,
    raw,
    flags,
    pack,
    recv,
    basis,
    fields,
    state,
    parts,
    back,
    vt,
    first_sums,
    sums,
    talls,
    square,
    const,
    table_ref,
    in_sem,
    send_sem,
    recv_sem,
    back_send,
    back_recv,
    sum_send,
    sum_recv,
    entered,
):
    ngx, ngy, ngz = plan.grid
    sx, sy, sz = plan.shard
    n, own, halo, pitch = plan.n, plan.own, plan.halo, plan.pitch
    nx, ny = ngx * sx, ngy * sy
    groups, mixed, tiles = plan.groups, plan.mixed, plan.tiles
    total = n * ngz
    gx, gy, gz = lax.axis_index("gx"), lax.axis_index("gy"), lax.axis_index("gz")
    p = gx * ngy + gy
    me = p * ngz + gz
    count = pick(plan.counts, gz)
    worker = pick(plan.base, gz) + count - 1 - p
    is_worker = (p < count) & (worker < plan.workers)
    first = own * worker - halo
    settled = jnp.maximum(first, 0)
    low_slab = jnp.minimum(lax.div(settled, sz), ngz - 1)
    edge = sz * (low_slab + 1)
    two = (first + plan.span > edge) & (low_slab + 1 < ngz)
    last = total - 1

    fetched = [
        pltpu.make_async_copy(disp_hbm, raw.at[pl.ds(0, 3)], in_sem.at[0]),
        pltpu.make_async_copy(load_hbm, raw.at[pl.ds(3, 3)], in_sem.at[1]),
        pltpu.make_async_copy(mat_hbm, flags.at[0], in_sem.at[2]),
        pltpu.make_async_copy(free_hbm, flags.at[1], in_sem.at[3]),
        pltpu.make_async_copy(table_hbm, table_ref, in_sem.at[4]),
        pltpu.make_async_copy(const_hbm, const, in_sem.at[5]),
    ]
    for copy in fetched:
        copy.start()

    def where_is(d):
        return dict(device_id=d, device_id_type=pl.DeviceIdType.LOGICAL)

    barrier = pltpu.get_barrier_semaphore()

    def greet(d):
        pl.semaphore_signal(barrier, inc=1, **where_is(d))

    def greet_slab(z):
        def one(q):
            d = q * ngz + z
            when((d != me) & (d != last), lambda: greet(d))

        loop(n, one)

    when(is_worker, lambda: greet_slab(low_slab))
    when(is_worker & two, lambda: greet_slab(low_slab + 1))
    when(me != last, lambda: greet(last))

    for copy in fetched[:4]:
        copy.wait()
    raw[6] = flags[0].astype(F32)
    raw[7] = flags[1].astype(F32)

    lane = lax.broadcasted_iota(jnp.int32, (8, LANES), 1)
    row = lax.broadcasted_iota(jnp.int32, (8, LANES), 0)
    per = 8 // sy
    stacks = -(-tiles // per)
    held = []
    for t in range(stacks):
        part = []
        for e in range(mixed * sx):
            f, i = e // sx, e % sx
            rows = [
                raw[ORDER[mixed * min(per * t + h, tiles - 1) + f], i] for h in range(per)
            ]
            part.append(jnp.concatenate(rows, axis=0))
        turned = []
        for e in range(mixed * sx):
            v = part[e]
            for k in range(1, mixed):
                v = jnp.where(lax.rem(gx, mixed) == k, part[(e - k * sx) % (mixed * sx)], v)
            turned.append(v)
        held.append(turned)

    to_low = pick(plan.to_low, gz)
    to_count = pick([b - a + 1 for a, b in zip(plan.to_low, plan.to_high)], gz)

    def route(j):
        w = to_low + j
        z = 0
        for k in range(1, ngz):
            z = z + jnp.where(w >= plan.base[k], 1, 0)
        q = pick([b + c - 1 for b, c in zip(plan.base, plan.counts)], z) - w
        slot = jnp.where(sz * gz > jnp.maximum(own * w - halo, 0), 1, 0)
        return j < to_count, slot, q * ngz + z

    def prepare(j):
        w = to_low + j
        offset = sz * gz - (own * w - halo)
        for t in range(stacks):
            out = None
            for e, v in enumerate(held[t]):
                moved = pltpu.roll(v, lax.rem(offset + (pitch * e + 8 * LANES), LANES), 1)
                out = moved if out is None else jnp.where(lane >= pitch * e, moved, out)
            for h in range(min(per, tiles - per * t)):
                pack[j, per * t + h] = out[sy * h : sy * (h + 1)]

    loop(plan.sends, prepare)

    expected = to_count
    if plan.sends <= 32:
        routes = [route(j) for j in range(plan.sends)]
        for valid, _, d in routes:
            expected = expected - jnp.where(valid & (d == me), 1, 0)
    else:
        routes = None

        def count_self(j, seen):
            valid, _, d = route(j)
            return seen - jnp.where(valid & (d == me), 1, 0)

        expected = lax.fori_loop(0, plan.sends, count_self, expected)
    expected = jnp.where(me == last, total - 1, expected)
    pl.semaphore_wait(barrier, expected)

    def piece(j, start):
        valid, slot, d = routes[j] if routes else route(j)
        dst = recv.at[slot, gx, gy]
        remote = pltpu.make_async_remote_copy(
            src_ref=pack.at[j],
            dst_ref=dst,
            send_sem=send_sem.at[0],
            recv_sem=recv_sem.at[slot],
            **where_is(d),
        )
        if start:
            when(valid & (d != me), remote.start)
            when(
                valid & (d == me),
                lambda: pltpu.make_async_copy(pack.at[j], dst, recv_sem.at[slot]).start(),
            )
        else:
            when(valid & (d != me), remote.wait_send)

    loop(plan.sends, lambda j: piece(j, True))

    def announce():
        loop(total - 1, lambda d: pl.semaphore_signal(entered, inc=1, **where_is(d)))

    when(me == last, announce)

    def settle(ref, sem):
        pltpu.make_async_copy(ref, ref, sem).wait()

    def share(ref, slot, d):
        when(
            me != d,
            pltpu.make_async_remote_copy(
                src_ref=ref.at[worker],
                dst_ref=ref.at[worker],
                send_sem=sum_send.at[slot],
                recv_sem=sum_recv.at[slot],
                **where_is(d),
            ).start,
        )

    def work():
        settle(recv.at[0], recv_sem.at[0])
        when(two, lambda: settle(recv.at[1], recv_sem.at[1]))

        wide_lane = lax.broadcasted_iota(jnp.int32, (ny, LANES), 1)
        depth = lax.rem(wide_lane, pitch)
        plane = depth + first
        near = plane < edge
        seg = sx * pitch

        def gather_rows(slot, k, x):
            return jnp.concatenate([recv[slot, x, g, k] for g in range(ngy)], axis=0)

        def source(k, x):
            return jnp.where(near, gather_rows(0, k, x), gather_rows(1, k, x))

        def unpack(k, g):
            parts_in = [source(k, g * mixed + d) for d in range(mixed)]
            out = []
            for f in range(mixed):
                v = None
                for at in range(mixed):
                    u = parts_in[(at - f) % mixed]
                    v = u if v is None else jnp.where(wide_lane >= at * seg, u, v)
                out.append(pltpu.roll(v, LANES - f * seg, 1) if f else v)
            return out

        got = [[None] * groups for _ in range(FIELDS)]
        for g in range(groups):
            for k in range(tiles):
                for f, v in enumerate(unpack(k, g)):
                    got[ORDER[mixed * k + f]][g] = v

        span = range(groups)

        def next_y(a):
            return [pltpu.roll(v, ny - 1, 0) for v in a]

        def last_y(a):
            return [pltpu.roll(v, 1, 0) for v in a]

        def forward(a, x, z):
            moved = [pltpu.roll(v, LANES - pitch * x - z, 1) for v in a]
            if groups == 1 or not x:
                return moved
            wrap = wide_lane >= LANES - pitch
            return [jnp.where(wrap, moved[min(g + 1, groups - 1)], moved[g]) for g in span]

        def backward(a, x, z):
            moved = [pltpu.roll(v, pitch * x + z, 1) for v in a]
            if groups == 1 or not x:
                return moved
            wrap = wide_lane < pitch
            return [jnp.where(wrap, moved[max(g - 1, 0)], moved[g]) for g in span]

        def both(op, *lists):
            return [op(*vs) for vs in zip(*lists)]

        add = functools.partial(both, lambda a, b: a + b)
        sub = functools.partial(both, lambda a, b: a - b)

        def gradient(vector):
            grad = []
            for v in vector:
                above, over, far = forward(v, 0, 1), forward(v, 1, 0), forward(v, 1, 1)
                near_z, far_z = add(v, above), add(over, far)
                wide, flat = sub(far_z, near_z), add(far_z, near_z)
                rise = add(sub(above, v), sub(far, over))
                grad.append([add(next_y(wide), wide), sub(next_y(flat), flat), add(next_y(rise), rise)])
            return grad

        pairs = [(0, 0), (0, 1), (0, 2), (1, 1), (1, 2), (2, 2)]
        free = got[7]
        for c in range(3):
            for g in span:
                basis[0, c, g] = got[3 + c][g] * free[g]
        grad = gradient([got[0], got[1], got[2]])
        mass = []
        high = lax.broadcasted_iota(jnp.int32, (ny, LANES), 0)
        for g in span:
            valid = (high <= ny - 2) & (plane >= 0) & (plane <= plan.nz - 2) & (depth <= plan.span - 2)
            valid = valid & (lax.div(wide_lane, pitch) + g * plan.packed <= nx - 2)
            material = got[6][g]
            zero = jnp.zeros((ny, LANES), F32)
            lame, shear, heavy = zero, zero, zero
            for r in range(table_ref.shape[1]):
                hit = material == float(r)
                lame = jnp.where(hit, table_ref[0, r], lame)
                shear = jnp.where(hit, table_ref[1, r], shear)
                heavy = jnp.where(hit, table_ref[2, r], heavy)
            lame = jnp.where(valid, lame * 0.0625, 0.0)
            shear = jnp.where(valid, shear * 0.0625, 0.0)
            mass.append(jnp.where(valid, heavy * 0.125, 0.0))
            frame = [
                [0.25 * grad[i][j][g] + (1.0 if i == j else 0.0) for j in range(3)] for i in range(3)
            ]
            strain = {}
            for i, j in pairs:
                v = sum(frame[k][i] * frame[k][j] for k in range(3))
                strain[i, j] = 0.5 * (v - 1.0 if i == j else v)
            bulk = lame * (strain[0, 0] + strain[1, 1] + strain[2, 2])
            for i in range(3):
                for j in range(3):
                    state[3 * i + j, g] = frame[i][j]
            for spot, (i, j) in enumerate(pairs):
                v = 2.0 * shear * strain[i, j]
                state[9 + spot, g] = v + bulk if i == j else v
            state[15, g] = lame
            state[16, g] = shear
        mass = add(mass, last_y(mass))
        mass = add(
            add(mass, backward(mass, 0, 1)), add(backward(mass, 1, 0), backward(mass, 1, 1))
        )
        for g in span:
            fields[0, g] = free[g]
            fields[1, g] = free[g] * (1.0 / HALF_WIDTH)
            fields[2, g] = (free[g] * mass[g] + (1.0 - free[g])) * (1.0 / HALF_WIDTH)

        rows8 = [pl.ds(8 * r, 8) for r in range(ny // 8)]

        def stress(j):
            grad = gradient([[basis[j, c, g] * fields[0, g] for g in span] for c in range(3)])
            pio = [[[[None] * len(rows8) for _ in span] for _ in range(3)] for _ in range(3)]
            for g in span:
                for r, at in enumerate(rows8):
                    d = [[grad[c][q][g][8 * r : 8 * r + 8] for q in range(3)] for c in range(3)]
                    f = [[state[3 * i + k, g, at] for k in range(3)] for i in range(3)]
                    pulled = [
                        [sum(f[k][a] * d[k][b] for k in range(3)) for b in range(3)] for a in range(3)
                    ]
                    lame, shear = state[15, g, at], state[16, g, at]
                    bulk = lame * (pulled[0][0] + pulled[1][1] + pulled[2][2])
                    t, s = {}, {}
                    for spot, (a, b) in enumerate(pairs):
                        v = shear * (pulled[a][b] + pulled[b][a])
                        t[a, b] = t[b, a] = v + bulk if a == b else v
                        s[a, b] = s[b, a] = state[9 + spot, g, at]
                    for i in range(3):
                        for b in range(3):
                            v = sum(f[i][k] * t[k, b] for k in range(3))
                            pio[i][b][g][r] = v + sum(d[i][k] * s[k, b] for k in range(3))
            pio = [[[jnp.concatenate(pio[c][b][g], axis=0) for g in span] for b in range(3)] for c in range(3)]
            return grad, pio

        def scatter(j, pio):
            for c in range(3):
                e = pio[c]
                wide = add(e[0], last_y(e[0]))
                tilt = sub(last_y(e[1]), e[1])
                rise = add(e[2], last_y(e[2]))
                minus, plus = sub(tilt, wide), add(tilt, wide)
                out = add(
                    add(sub(minus, rise), backward(add(minus, rise), 0, 1)),
                    add(backward(sub(plus, rise), 1, 0), backward(add(plus, rise), 1, 1)),
                )
                for g in span:
                    basis[j + 1, c, g] = fields[1, g] * out[g] + (
                        fields[2, g] - CHAIN[j] / HALF_WIDTH
                    ) * basis[j, c, g]

        def apply(j):
            scatter(j, stress(j)[1])

        mine = (depth >= halo) & (depth < halo + own) & (plane < plan.nz)
        spots = [(c, g, r) for c in range(3) for g in span for r in range(ny // 8)]
        mine = [mine[8 * r : 8 * r + 8] for r in range(ny // 8)]

        def divide(k):
            v = [jnp.where(mine[r], basis[k, c, g, rows8[r]], 0.0) for c, g, r in spots]
            top = jnp.abs(v[0])
            for u in v[1:]:
                top = jnp.maximum(top, jnp.abs(u))
            grain = top * (32768.0 * max(1, len(v) // 6))
            for s, u in enumerate(v):
                coarse = (u + grain) - grain
                parts[0, k, s] = coarse
                parts[1, k, s] = u - coarse

        def products(i, js):
            acc = {}
            for s in range(len(spots)):
                ch, cl = parts[0, i, s], parts[1, i, s]
                for j in js:
                    dh, dl = parts[0, j, s], parts[1, j, s]
                    new = [ch * dh, cl * (dh + ch + dl) if i == j else ch * dl + cl * (dh + dl)]
                    acc[j] = new if s == 0 else [acc[j][0] + new[0], acc[j][1] + new[1]]
            return {(i, j): tuple(acc[j]) for j in js}

        def merge(a, b, mask, shift):
            first_in, second_in = [], []
            for u, v in zip(a, b):
                if shift == 4:
                    first_in.append(jnp.where(mask, u, v))
                    second_in.append(pltpu.roll(jnp.where(mask, v, u), shift, 0))
                else:
                    first_in.append(jnp.where(mask, u, pltpu.roll(v, shift, 0)))
                    second_in.append(jnp.where(mask, pltpu.roll(u, 8 - shift, 0), v))
            return add_parts(tuple(first_in), tuple(second_in))

        def stack(items, slots):
            none = tuple(jnp.zeros((8, LANES), F32) for _ in next(iter(items.values())))
            it = [items.get(q, none) for q in slots]
            one = [merge(it[r], it[r + 4], row < 4, 4) for r in range(4)]
            twice = [merge(one[r], one[r + 2], lax.rem(row, 4) < 2, 2) for r in range(2)]
            return merge(twice[0], twice[1], lax.rem(row, 2) < 1, 1)

        def slots_of(table, q):
            at = {t: pair for pair, t in table.items()}
            return [at.get(8 * q + r) for r in range(8)]

        quarter = lane // 32

        def fold(tall):
            def turned(j):
                out = []
                for part in range(len(tall[0])):
                    v = None
                    for q in range(len(tall)):
                        u = tall[q][part]
                        u = pltpu.roll(u, LANES - 32 * j, 1) if j else u
                        v = u if v is None else jnp.where(quarter >= q, u, v)
                    out.append(v)
                return tuple(out)

            whole = add_all([turned(j) for j in range(4)])
            whole = add_all(
                [
                    tuple(pltpu.roll(u, own - j, 1, stride=1, stride_axis=0) for u in whole)
                    for j in range(own)
                ]
            )
            keep = lax.rem(lane + (2 * LANES - halo - own) - row, 32) == 0
            keep = keep & (lax.rem(lane + (LANES - halo - own) - row, LANES) < 32 * len(tall))
            return [jnp.sum(jnp.where(keep, u, 0.0), axis=0, keepdims=True) for u in whole]

        items = {}
        for k in range(STEPS):
            divide(k)
            for i in range(k + 1):
                items.update(products(i, [k]))
            if k == 3:
                single = {q: (items[q][0] + items[q][1],) for q in EARLY}
                early = [stack(single, slots_of(EARLY, q)) for q in range(2)]
                first_sums[worker] = fold(early)[0]
            if k < STEPS - 1:
                apply(k)
        width, chain = recurrence()
        for i in range(5):
            up, same = items[i + 1, 5], items[i, 5]
            factor = float((chain[i] - chain[5]) / width)
            high_part, low_part = two_sum(up[0], factor * same[0])
            items[i, 6] = (high_part, low_part + (up[1] + factor * same[1]))
        for q in range(4):
            high_part, low_part = stack(items, slots_of(PRODUCTS, q))
            talls[q, 0] = high_part
            talls[q, 1] = low_part
        square[0] = items[5, 5][0]
        square[1] = items[5, 5][1]
        when(me != last, lambda: pl.semaphore_wait(entered, 1))
        loop(total, lambda d: share(first_sums, 0, d))
        grad, pio = stress(5)
        energy = None
        for g in span:
            dense = sum(pio[c][b][g] * grad[c][b][g] for c in range(3) for b in range(3))
            for r in range(ny // 8):
                v = [basis[5, c, g, rows8[r]] for c in range(3)]
                nodes = fields[2, g, rows8[r]] * (v[0] * v[0] + v[1] * v[1] + v[2] * v[2])
                u = dense[8 * r : 8 * r + 8] * (1.0 / HALF_WIDTH) + nodes
                u = jnp.where(mine[r], u, 0.0)
                energy = u if energy is None else energy + u
        factor = float(-chain[5] / width)
        high_part, low_part = two_sum(energy, factor * square[0])
        ends = (high_part, low_part + factor * square[1])
        ends = add_pair(ends, [pltpu.roll(u, 4, 0) for u in ends])
        tall = [(talls[q, 0], talls[q, 1]) for q in range(3)]
        tall.append(tuple(jnp.where(row < 4, talls[3, p], ends[p]) for p in range(2)))
        sums[worker] = jnp.concatenate(fold(tall), axis=0)
        loop(total, lambda d: share(sums, 1, d))
        scatter(5, pio)

    fetched[4].wait()
    when(is_worker, work)
    when(
        jnp.logical_not(is_worker) & (me != last), lambda: pl.semaphore_wait(entered, 1)
    )

    stride = plan.stride

    def give_back():
        wide_lane = lax.broadcasted_iota(jnp.int32, (ny, LANES), 1)
        for k in range(1, 7):
            for x in range(ngx):
                g, d = x // mixed, x % mixed
                out = None
                for c in range(3):
                    for i in range(sx):
                        e = c * sx + i
                        s = (e * stride - ((d * sx + i) * pitch + halo)) % LANES
                        v = basis[k, c, g]
                        moved = pltpu.roll(v, s, 1) if s else v
                        out = moved if out is None else jnp.where(wide_lane >= e * stride, moved, out)
                for y in range(ngy):
                    back[x, y, k - 1] = out[sy * y : sy * (y + 1)]
        loop(n, lambda q: give(q, True))

    own_low = jnp.minimum(lax.div(own * worker, sz), ngz - 1)
    own_high = lax.div(jnp.minimum(own * worker + own, plan.nz) - 1, sz)
    straddles = sz % own != 0

    def give(q, start):
        x, y = (q // ngy, q % ngy) if isinstance(q, int) else (lax.div(q, ngy), lax.rem(q, ngy))

        def to(z):
            d = q * ngz + z
            dst = vt.at[worker - pick(plan.from_low, z)]
            remote = pltpu.make_async_remote_copy(
                src_ref=back.at[x, y],
                dst_ref=dst,
                send_sem=back_send.at[0],
                recv_sem=back_recv.at[0],
                **where_is(d),
            )
            if start:
                when(d != me, remote.start)
                when(
                    d == me,
                    lambda: pltpu.make_async_copy(back.at[x, y], dst, back_recv.at[0]).start(),
                )
            else:
                when(d != me, remote.wait_send)

        to(own_low)
        if straddles:
            when(own_high > own_low, lambda: to(own_high))

    when(is_worker, give_back)
    fetched[5].wait()

    counts = [b - a + 1 for a, b in zip(plan.from_low, plan.from_high)]
    if min(counts) == plan.returns:
        settle(vt, back_recv.at[0])
    else:
        for z in range(ngz):
            when(gz == z, lambda z=z: settle(vt.at[pl.ds(0, counts[z])], back_recv.at[0]))

    mates = [(k, c, i) for k in range(0, 6, 2) for c in range(3) for i in range(sx)]

    def collect(j, accs):
        w = pick(plan.from_low, gz) + j
        offset = own * w - sz * gz
        inside = (lane >= offset) & (lane < offset + own)
        if min(counts) != plan.returns:
            inside = inside & (j < pick(counts, gz))
        new = []
        stacked = [jnp.concatenate([vt[j, k], vt[j, k + 1]], axis=0) for k in range(0, 6, 2)]
        for (k, c, i), acc in zip(mates, accs):
            s = lax.rem(offset - (c * sx + i) * stride + 2 * LANES, LANES)
            moved = pltpu.roll(stacked[k // 2], s, 1)
            new.append(jnp.where(inside, moved, acc))
        return tuple(new)

    accs = tuple(jnp.zeros((8, LANES), F32) for _ in mates)
    if plan.returns <= 16:
        for j in range(plan.returns):
            accs = collect(j, accs)
    else:
        accs = lax.fori_loop(0, plan.returns, collect, accs)

    active = plan.workers

    def wait_rows(ref, sem, rows):
        while rows:
            now = min(rows, active)
            settle(ref.at[pl.ds(0, now)], sem)
            rows -= now

    def sent():
        loop(n, lambda q: give(q, False))
        wait_rows(first_sums, sum_send.at[0], total - 1)
        wait_rows(sums, sum_send.at[1], total - 1)

    loop(plan.sends, lambda j: piece(j, False))
    when(is_worker, sent)

    def landed(ref, slot):
        when(is_worker, lambda: wait_rows(ref, sum_recv.at[slot], active - 1))
        when(jnp.logical_not(is_worker), lambda: wait_rows(ref, sum_recv.at[slot], active))

    def total_of(ref, pair):
        zero = jnp.zeros(ref.shape[1:], F32)
        rest = (zero,) if pair else ()
        if active <= 32:
            return add_all([(ref[d], *rest) for d in range(active)])
        return lax.fori_loop(
            0, active, lambda d, a: add_parts(a, (ref[d], *rest)), (zero, *rest)
        )

    landed(first_sums, 0)
    first_total = jnp.broadcast_to(total_of(first_sums, False)[0], (8, LANES))

    def entry(i, j):
        s = place(EARLY[min(i, j), max(i, j)], halo + own)
        return jnp.broadcast_to(first_total[:, s : s + 1], (8, LANES))

    first_gram = [
        [HALF_WIDTH * entry(i, j + 1) + CHAIN[j] * entry(i, j) for j in range(3)]
        for i in range(3)
    ]
    c = solve_small(first_gram, [entry(i, 0) for i in range(3)])

    def affine(c, load_at):
        return ((load_at(0) + c[0] * load_at(1)) + c[1] * load_at(2)) + c[2] * load_at(3)

    def scaled(at, size, x):
        ch, cl, rest = (const[pl.ds(q, size), :] for q in at)
        xh, xl = split(x)
        p = (ch + cl) * x
        return p, (((ch * xh - p) + ch * xl + cl * xh) + cl * xl) + rest * x

    def times_pair(x, pair):
        p, e = two_product(x, pair[0])
        return p, e + x * pair[1]

    weights = []
    for v in range(2):
        side = [
            affine(c, lambda a, s=s: const[pl.ds((4 * s + a) * 16 + 8 * v, 8), :])
            for s in range(6)
        ]
        turn = [[24 * 16 + (3 * q + part) * 16 + 8 * v for part in range(3)] for q in range(3)]
        image = [
            add_pair(scaled(turn[q], 8, side[2 + q]), scaled(turn[2], 8, side[4 + q]))
            for q in range(2)
        ]
        weights.append(add_pair(times_pair(side[0], image[1]), times_pair(side[1], image[0])))

    landed(sums, 1)
    raw_sum, lost = total_of(sums, True)
    gram_high, gram_low = two_sum(raw_sum[0:1], raw_sum[1:2] + lost[0:1])
    gram_high = jnp.broadcast_to(gram_high, (8, LANES))
    gram_low = jnp.broadcast_to(gram_low, (8, LANES))
    halves = []
    for weight in weights:
        high_part, low_part = two_product(gram_high, weight[0])
        pair = (high_part, low_part + (gram_high * weight[1] + gram_low * weight[0]))
        halves.append(
            add_all([[pltpu.roll(u, LANES - 32 * q, 1) if q else u for u in pair] for q in range(4)])
        )
    pair = [jnp.where(lane < 64, u, v) for u, v in zip(*halves)]
    pair = add_all([[pltpu.roll(u, LANES - q, 1) if q else u for u in pair] for q in range(8)])
    value = pair[0] + pair[1]
    done = []
    for v in range(2):
        at = halo + own + 64 * v
        done.append(jnp.broadcast_to(value[:, at : at + 1], (8, LANES)))
    form = {
        q: jnp.broadcast_to(done[f // 8][f % 8 : f % 8 + 1], (8, LANES))
        for f, q in enumerate(FORMS)
    }
    gram = [[form[i, j] for j in range(3)] for i in range(3)]
    d = solve_small(gram, [form[i, None] for i in range(3)])
    base_at = 24 * 16 + 9 * 16
    vector = affine(c, lambda a: const[pl.ds(base_at + 8 * a, 8), :])
    moved = affine(c, lambda a: const[pl.ds(base_at + 32 + 8 * a, 8), :])
    turn = [[base_at + 64 + 8 * (3 * q + part) for part in range(3)] for q in range(2)]
    image = add_pair(scaled(turn[0], 8, vector), scaled(turn[1], 8, moved))
    factor = jnp.where(row == 0, -d[0], jnp.where(row == 1, -d[1], jnp.where(row == 2, -d[2], 1.0)))
    coef = times_pair(factor, image)
    coef = add_pair(coef, [pltpu.roll(u, 6, 0) for u in coef])
    coef = add_pair(coef, [pltpu.roll(u, 7, 0) for u in coef])
    coef = coef[0][0:1] + coef[1][0:1]

    def spread_coef(k):
        return jnp.broadcast_to(coef[:, k : k + 1], (8, LANES))

    for slot in range(2):
        w = [spread_coef(k) if slot else -spread_coef(32 + k) for k in range(7)]
        duo = [jnp.where(row < sy, w[k + 1], w[k + 2]) for k in range(0, 6, 2)]
        for cc in range(3):
            for i in range(sx):
                v = None
                for k in range(0, 6, 2):
                    u = duo[k // 2] * accs[mates.index((k, cc, i))]
                    v = u if v is None else v + u
                head = w[0][0:sy] * (raw[3 + cc, i] * raw[7, i])
                out_ref[slot, cc, sy * i : sy * (i + 1)] = head + (v[0:sy] + v[sy : 2 * sy])


def per_device(displacement, load, material, free_node, table):
    shard = displacement.shape[1:]
    sx, sy, sz = shard
    grid = tuple(lax.axis_size(a) for a in ("gx", "gy", "gz"))
    plan = Plan(grid, shard)
    ngx, ngy, ngz = grid
    ny = ngy * sy
    groups = plan.groups
    const = jnp.asarray(tables(plan.halo + plan.own))
    buffers = [
        pltpu.VMEM((FIELDS, sx, sy, sz), F32),
        pltpu.VMEM((2, sx, sy, sz), jnp.int32),
        pltpu.VMEM((plan.sends, plan.tiles, sy, LANES), F32),
        pltpu.VMEM((2, ngx, ngy, plan.tiles, sy, LANES), F32),
        pltpu.VMEM((7, 3, groups, ny, LANES), F32),
        pltpu.VMEM((3, groups, ny, LANES), F32),
        pltpu.VMEM((17, groups, ny, LANES), F32),
        pltpu.VMEM((2, 7, 3 * groups * ny // 8, 8, LANES), F32),
        pltpu.VMEM((ngx, ngy, 6, sy, LANES), F32),
        pltpu.VMEM((plan.returns, 6, sy, LANES), F32),
        pltpu.VMEM((plan.workers, 1, LANES), F32),
        pltpu.VMEM((plan.workers, 2, LANES), F32),
        pltpu.VMEM((4, 2, 8, LANES), F32),
        pltpu.VMEM((2, 8, LANES), F32),
        pltpu.VMEM(const.shape, F32),
        pltpu.SMEM(table.shape[::-1], F32),
        pltpu.SemaphoreType.DMA((6,)),
        pltpu.SemaphoreType.DMA((1,)),
        pltpu.SemaphoreType.DMA((2,)),
        pltpu.SemaphoreType.DMA((1,)),
        pltpu.SemaphoreType.DMA((1,)),
        pltpu.SemaphoreType.DMA((2,)),
        pltpu.SemaphoreType.DMA((2,)),
        pltpu.SemaphoreType.REGULAR,
    ]
    operands = (displacement, load, material, free_node, table.T, const)
    both = pl.pallas_call(
        functools.partial(kernel, plan),
        out_shape=jax.ShapeDtypeStruct((2, 3, sx * sy, sz), F32),
        in_specs=[pl.BlockSpec(memory_space=pltpu.HBM)] * 6,
        out_specs=pl.BlockSpec(memory_space=pltpu.VMEM),
        scratch_shapes=buffers,
        compiler_params=pltpu.CompilerParams(
            collective_id=0, has_side_effects=True, vmem_limit_bytes=32 << 20
        ),
    )(*(pltpu.with_memory_space_constraint(a, pltpu.HBM) for a in operands))
    return both[0].reshape(displacement.shape), both[1].reshape(displacement.shape)


def solution(mesh):
    in_specs = (
        P(None, "gx", "gy", "gz"),
        P(None, "gx", "gy", "gz"),
        P("gx", "gy", "gz"),
        P("gx", "gy", "gz"),
        P(),
    )
    out_specs = (P(None, "gx", "gy", "gz"), P(None, "gx", "gy", "gz"))
    return jax.shard_map(
        per_device, mesh=mesh, in_specs=in_specs, out_specs=out_specs, check_vma=False
    )
```

```python
import functools

import jax
import jax.numpy as jnp
import numpy as np
from jax import lax
from jax.experimental import pallas as pl
from jax.experimental.pallas import tpu as pltpu
from jax.sharding import PartitionSpec as P

SHIFTS = (9.6, 51.4)
HALF_WIDTH = 29.5
CHAIN = SHIFTS + (30.5,) + SHIFTS + (30.5,)
STEPS = 6
FIELDS = 8
ORDER = (0, 3, 1, 4, 2, 5, 6, 7)
LANES = 128
PRODUCTS = {(i, j): t for t, (i, j) in enumerate((i, j) for i in range(6) for j in range(i, 6))}
PRODUCTS.update({(i, 6): 21 + i for i in range(5)})
FORMS = [(i, j) for i in range(3) for j in range(3)] + [(i, None) for i in range(3)]
EARLY = {(i, j): t for t, (i, j) in enumerate((i, j) for i in range(3) for j in range(i, 4))}
F32 = jnp.float32


def place(t, base):
    return (32 * (t // 8) + base + t % 8) % LANES


def bits(x):
    top = np.asarray(x, np.float32)
    t = np.float32(4097.0) * top
    high = t - (t - top)
    return high, top - high, (x - top.astype(np.float64)).astype(np.float32)


def recurrence():
    width = 1.0 / np.float64(np.float32(1.0 / HALF_WIDTH))
    return width, np.array([np.float64(np.float32(x / HALF_WIDTH)) * width for x in CHAIN] + [0.0])


def tables(plan):
    width, chain = recurrence()

    def shifted(x):
        return np.concatenate([[0.0], x[:-1]])

    def times(x):
        return chain * x + width * shifted(x)

    unit = np.eye(7)
    b = [[unit[0]] + [-times(unit[j]) for j in range(3)]]
    for j in range(2):
        b.append([(times(x) - SHIFTS[j] * x) / HALF_WIDTH for x in b[j]])
    base = plan.halo + plan.own
    lanes = [(*q, place(t, base)) for q, t in PRODUCTS.items()]
    lanes += [(5, 6, at) for at in range(LANES) if plan.halo <= at % plan.pitch < base]
    assert len({at for _, _, at in lanes}) == len(lanes)
    wide = np.zeros((6, 4, 16, LANES))
    turn = np.zeros((3, 16, LANES))
    for f, (i, j) in enumerate(FORMS):
        for one, two, at in lanes:
            turn[:, f, at] = (1.0, 1.0, 0.0) if j is None else (chain[one], chain[two], width)
            for a in range(4):
                left, right = b[i][a], b[j or 0][a]
                wide[0, a, f, at] = left[one]
                wide[1, a, f, at] = left[two] if one != two else 0.0
                wide[2, a, f, at] = right[one]
                wide[3, a, f, at] = right[two]
                wide[4, a, f, at] = shifted(right)[one]
                wide[5, a, f, at] = shifted(right)[two]
    last = np.zeros((2, 4, 8, LANES))
    final = np.zeros((2, 8, LANES))
    for k in range(7):
        final[:, :3, k] = np.array([[chain[k]], [width]])
        final[0, :3, 32 + k] = 1.0
        final[0, 3, k] = final[0, 3, 32 + k] = 1.0
        for a in range(4):
            for j in range(3):
                last[0, a, j, k] = last[0, a, j, 32 + k] = b[j][a][k]
                last[1, a, j, k] = shifted(b[j][a])[k]
            last[0, a, 3, k] = b[0][a][k]
            last[0, a, 3, 32 + k] = -1.0 if 0 < a == k + 1 else 0.0
    blocks = [wide, *(np.stack(bits(x)) for x in turn), last, *(np.stack(bits(x)) for x in final)]
    return np.concatenate([x.reshape(-1, LANES).astype(np.float32) for x in blocks])


def solve_small(gram, right):
    sym = [[0.5 * (gram[i][j] + gram[j][i]) for j in range(3)] for i in range(3)]
    r0 = 1.0 / sym[0][0]
    l10 = sym[1][0] * r0
    l20 = sym[2][0] * r0
    r1 = 1.0 / (sym[1][1] - l10 * sym[1][0])
    e = sym[2][1] - l20 * sym[1][0]
    l21 = e * r1
    d2 = sym[2][2] - l20 * sym[2][0] - l21 * e
    y1 = right[1] - l10 * right[0]
    c2 = (right[2] - l20 * right[0] - l21 * y1) / d2
    c1 = y1 * r1 - l21 * c2
    c0 = right[0] * r0 - l10 * c1 - l20 * c2
    return [c0, c1, c2]


def two_sum(a, b):
    s = a + b
    t = s - a
    return s, (a - (s - t)) + (b - t)


def add_pair(p, q):
    s, e = two_sum(p[0], q[0])
    return s, e + (p[1] + q[1])


def add_parts(p, q):
    return add_pair(p, q) if len(p) == 2 else (p[0] + q[0],)


def add_all(terms):
    while len(terms) > 1:
        rest = terms[len(terms) & ~1 :]
        terms = [add_parts(p, q) for p, q in zip(terms[::2], terms[1::2])] + rest
    return terms[0]


def split(a):
    t = 4097.0 * a
    high = t - (t - a)
    return high, a - high


def two_product(a, b):
    p = a * b
    (ah, al), (bh, bl) = split(a), split(b)
    return p, ((ah * bh - p) + ah * bl + al * bh) + al * bl


def loop(count, body):
    if count <= 32:
        for i in range(count):
            body(i)
    else:

        def step(i, carry):
            body(i)
            return carry

        lax.fori_loop(0, count, step, 0)


def when(condition, body):
    if isinstance(condition, bool):
        if condition:
            body()
    else:
        pl.when(condition)(body)


class Plan:
    def __init__(self, grid, shard):
        self.grid, self.shard = grid, shard
        ngx, ngy, ngz = grid
        sx, sy, sz = shard
        self.n = ngx * ngy
        self.nz = ngz * sz
        self.halo = STEPS
        total = self.n * ngz
        self.pitch = 1 << (-(-self.nz // total) + 2 * self.halo - 1).bit_length()
        spare = total - -(-self.nz // (self.pitch - 2 * self.halo))
        self.counts = [self.n] * (ngz - 1) + [max(2, self.n - spare)]
        self.own = -(-self.nz // sum(self.counts))
        self.span = self.own + 2 * self.halo
        self.packed = LANES // self.pitch
        self.groups = ngx * sx // self.packed
        self.mixed = LANES // (sx * self.pitch)
        self.tiles = FIELDS // self.mixed
        self.stride = LANES // (3 * sx)
        self.workers = -(-self.nz // self.own)
        self.base = [sum(self.counts[:z]) for z in range(ngz)]
        own, halo = self.own, self.halo
        self.to_low = [max(0, (sz * z - own - halo) // own + 1) for z in range(ngz)]
        self.to_high = [
            min(self.workers - 1, -(-(sz * z + sz + halo) // own) - 1) for z in range(ngz)
        ]
        self.from_low = [sz * z // own for z in range(ngz)]
        self.from_high = [(sz * z + sz - 1) // own for z in range(ngz)]
        self.sends = max(b - a + 1 for a, b in zip(self.to_low, self.to_high))
        self.returns = max(b - a + 1 for a, b in zip(self.from_low, self.from_high))
        assert sz == LANES and 8 == 2 * sy and own <= self.stride and halo + own <= 56


def pick(values, z):
    if all(v == values[0] for v in values):
        return values[0]
    out = values[0]
    for k in range(1, len(values)):
        out = jnp.where(z >= k, values[k], out)
    return out


def kernel(
    plan,
    disp_hbm,
    load_hbm,
    mat_hbm,
    free_hbm,
    table_hbm,
    const_hbm,
    out_ref,
    raw,
    flags,
    pack,
    recv,
    basis,
    fields,
    state,
    parts,
    back,
    vt,
    first_sums,
    sums,
    talls,
    square,
    const,
    table_ref,
    in_sem,
    send_sem,
    recv_sem,
    back_send,
    back_recv,
    sum_send,
    sum_recv,
    entered,
):
    ngx, ngy, ngz = plan.grid
    sx, sy, sz = plan.shard
    n, own, halo, pitch = plan.n, plan.own, plan.halo, plan.pitch
    nx, ny = ngx * sx, ngy * sy
    groups, mixed, tiles = plan.groups, plan.mixed, plan.tiles
    total = n * ngz
    gx, gy, gz = lax.axis_index("gx"), lax.axis_index("gy"), lax.axis_index("gz")
    p = gx * ngy + gy
    me = p * ngz + gz
    count = pick(plan.counts, gz)
    worker = pick(plan.base, gz) + count - 1 - p
    is_worker = (p < count) & (worker < plan.workers)
    first = own * worker - halo
    settled = jnp.maximum(first, 0)
    low_slab = jnp.minimum(lax.div(settled, sz), ngz - 1)
    edge = sz * (low_slab + 1)
    two = (first + plan.span > edge) & (low_slab + 1 < ngz)
    last = total - 1

    fetched = [
        pltpu.make_async_copy(disp_hbm, raw.at[pl.ds(0, 3)], in_sem.at[0]),
        pltpu.make_async_copy(load_hbm, raw.at[pl.ds(3, 3)], in_sem.at[1]),
        pltpu.make_async_copy(mat_hbm, flags.at[0], in_sem.at[2]),
        pltpu.make_async_copy(free_hbm, flags.at[1], in_sem.at[3]),
        pltpu.make_async_copy(table_hbm, table_ref, in_sem.at[4]),
        pltpu.make_async_copy(const_hbm, const, in_sem.at[5]),
    ]
    for copy in fetched:
        copy.start()

    def where_is(d):
        return dict(device_id=d, device_id_type=pl.DeviceIdType.LOGICAL)

    barrier = pltpu.get_barrier_semaphore()

    def greet(d):
        pl.semaphore_signal(barrier, inc=1, **where_is(d))

    def greet_slab(z):
        def one(q):
            d = q * ngz + z
            when((d != me) & (d != last), lambda: greet(d))

        loop(n, one)

    when(is_worker, lambda: greet_slab(low_slab))
    when(is_worker & two, lambda: greet_slab(low_slab + 1))
    when(me != last, lambda: greet(last))

    for copy in fetched[:4]:
        copy.wait()
    raw[6] = flags[0].astype(F32)
    raw[7] = flags[1].astype(F32)

    lane = lax.broadcasted_iota(jnp.int32, (8, LANES), 1)
    row = lax.broadcasted_iota(jnp.int32, (8, LANES), 0)
    per = 8 // sy
    stacks = -(-tiles // per)
    held = []
    for t in range(stacks):
        part = []
        for e in range(mixed * sx):
            f, i = e // sx, e % sx
            rows = [
                raw[ORDER[mixed * min(per * t + h, tiles - 1) + f], i] for h in range(per)
            ]
            part.append(jnp.concatenate(rows, axis=0))
        turned = []
        for e in range(mixed * sx):
            v = part[e]
            for k in range(1, mixed):
                v = jnp.where(lax.rem(gx, mixed) == k, part[(e - k * sx) % (mixed * sx)], v)
            turned.append(v)
        held.append(turned)

    to_low = pick(plan.to_low, gz)
    to_count = pick([b - a + 1 for a, b in zip(plan.to_low, plan.to_high)], gz)

    def route(j):
        w = to_low + j
        z = 0
        for k in range(1, ngz):
            z = z + jnp.where(w >= plan.base[k], 1, 0)
        q = pick([b + c - 1 for b, c in zip(plan.base, plan.counts)], z) - w
        slot = jnp.where(sz * gz > jnp.maximum(own * w - halo, 0), 1, 0)
        return j < to_count, slot, q * ngz + z

    def prepare(j):
        w = to_low + j
        offset = sz * gz - (own * w - halo)
        for t in range(stacks):
            out = None
            for e, v in enumerate(held[t]):
                moved = pltpu.roll(v, lax.rem(offset + (pitch * e + 8 * LANES), LANES), 1)
                out = moved if out is None else jnp.where(lane >= pitch * e, moved, out)
            for h in range(min(per, tiles - per * t)):
                pack[j, per * t + h] = out[sy * h : sy * (h + 1)]

    loop(plan.sends, prepare)

    expected = to_count
    if plan.sends <= 32:
        routes = [route(j) for j in range(plan.sends)]
        for valid, _, d in routes:
            expected = expected - jnp.where(valid & (d == me), 1, 0)
    else:
        routes = None

        def count_self(j, seen):
            valid, _, d = route(j)
            return seen - jnp.where(valid & (d == me), 1, 0)

        expected = lax.fori_loop(0, plan.sends, count_self, expected)
    expected = jnp.where(me == last, total - 1, expected)
    pl.semaphore_wait(barrier, expected)

    def piece(j, start):
        valid, slot, d = routes[j] if routes else route(j)
        dst = recv.at[slot, gx, gy]
        remote = pltpu.make_async_remote_copy(
            src_ref=pack.at[j],
            dst_ref=dst,
            send_sem=send_sem.at[0],
            recv_sem=recv_sem.at[slot],
            **where_is(d),
        )
        if start:
            when(valid & (d != me), remote.start)
            when(
                valid & (d == me),
                lambda: pltpu.make_async_copy(pack.at[j], dst, recv_sem.at[slot]).start(),
            )
        else:
            when(valid & (d != me), remote.wait_send)

    loop(plan.sends, lambda j: piece(j, True))

    def announce():
        loop(total - 1, lambda d: pl.semaphore_signal(entered, inc=1, **where_is(d)))

    when(me == last, announce)

    def settle(ref, sem):
        pltpu.make_async_copy(ref, ref, sem).wait()

    def share(ref, slot, d):
        when(
            me != d,
            pltpu.make_async_remote_copy(
                src_ref=ref.at[worker],
                dst_ref=ref.at[worker],
                send_sem=sum_send.at[slot],
                recv_sem=sum_recv.at[slot],
                **where_is(d),
            ).start,
        )

    def work():
        settle(recv.at[0], recv_sem.at[0])
        when(two, lambda: settle(recv.at[1], recv_sem.at[1]))

        wide_lane = lax.broadcasted_iota(jnp.int32, (ny, LANES), 1)
        depth = lax.rem(wide_lane, pitch)
        plane = depth + first
        near = plane < edge
        seg = sx * pitch

        def gather_rows(slot, k, x):
            return jnp.concatenate([recv[slot, x, g, k] for g in range(ngy)], axis=0)

        def source(k, x):
            return jnp.where(near, gather_rows(0, k, x), gather_rows(1, k, x))

        def unpack(k, g):
            parts_in = [source(k, g * mixed + d) for d in range(mixed)]
            out = []
            for f in range(mixed):
                v = None
                for at in range(mixed):
                    u = parts_in[(at - f) % mixed]
                    v = u if v is None else jnp.where(wide_lane >= at * seg, u, v)
                out.append(pltpu.roll(v, LANES - f * seg, 1) if f else v)
            return out

        got = [[None] * groups for _ in range(FIELDS)]
        for g in range(groups):
            for k in range(tiles):
                for f, v in enumerate(unpack(k, g)):
                    got[ORDER[mixed * k + f]][g] = v

        span = range(groups)

        def next_y(a):
            return [pltpu.roll(v, ny - 1, 0) for v in a]

        def last_y(a):
            return [pltpu.roll(v, 1, 0) for v in a]

        def forward(a, x, z):
            moved = [pltpu.roll(v, LANES - pitch * x - z, 1) for v in a]
            if groups == 1 or not x:
                return moved
            wrap = wide_lane >= LANES - pitch
            return [jnp.where(wrap, moved[min(g + 1, groups - 1)], moved[g]) for g in span]

        def backward(a, x, z):
            moved = [pltpu.roll(v, pitch * x + z, 1) for v in a]
            if groups == 1 or not x:
                return moved
            wrap = wide_lane < pitch
            return [jnp.where(wrap, moved[max(g - 1, 0)], moved[g]) for g in span]

        def both(op, *lists):
            return [op(*vs) for vs in zip(*lists)]

        add = functools.partial(both, lambda a, b: a + b)
        sub = functools.partial(both, lambda a, b: a - b)

        def gradient(vector):
            grad = []
            for v in vector:
                above, over, far = forward(v, 0, 1), forward(v, 1, 0), forward(v, 1, 1)
                near_z, far_z = add(v, above), add(over, far)
                wide, flat = sub(far_z, near_z), add(far_z, near_z)
                rise = add(sub(above, v), sub(far, over))
                grad.append([add(next_y(wide), wide), sub(next_y(flat), flat), add(next_y(rise), rise)])
            return grad

        pairs = [(0, 0), (0, 1), (0, 2), (1, 1), (1, 2), (2, 2)]
        free = got[7]
        for c in range(3):
            for g in span:
                basis[0, c, g] = got[3 + c][g] * free[g]
        grad = gradient([got[0], got[1], got[2]])
        mass = []
        high = lax.broadcasted_iota(jnp.int32, (ny, LANES), 0)
        for g in span:
            valid = (high <= ny - 2) & (plane >= 0) & (plane <= plan.nz - 2) & (depth <= plan.span - 2)
            valid = valid & (lax.div(wide_lane, pitch) + g * plan.packed <= nx - 2)
            material = got[6][g]
            zero = jnp.zeros((ny, LANES), F32)
            lame, shear, heavy = zero, zero, zero
            for r in range(table_ref.shape[1]):
                hit = material == float(r)
                lame = jnp.where(hit, table_ref[0, r], lame)
                shear = jnp.where(hit, table_ref[1, r], shear)
                heavy = jnp.where(hit, table_ref[2, r], heavy)
            lame = jnp.where(valid, lame * 0.0625, 0.0)
            shear = jnp.where(valid, shear * 0.0625, 0.0)
            mass.append(jnp.where(valid, heavy * 0.125, 0.0))
            frame = [
                [0.25 * grad[i][j][g] + (1.0 if i == j else 0.0) for j in range(3)] for i in range(3)
            ]
            strain = {}
            for i, j in pairs:
                v = sum(frame[k][i] * frame[k][j] for k in range(3))
                strain[i, j] = 0.5 * (v - 1.0 if i == j else v)
            bulk = lame * (strain[0, 0] + strain[1, 1] + strain[2, 2])
            for i in range(3):
                for j in range(3):
                    state[3 * i + j, g] = frame[i][j]
            for spot, (i, j) in enumerate(pairs):
                v = 2.0 * shear * strain[i, j]
                state[9 + spot, g] = v + bulk if i == j else v
            state[15, g] = lame
            state[16, g] = shear
        mass = add(mass, last_y(mass))
        mass = add(
            add(mass, backward(mass, 0, 1)), add(backward(mass, 1, 0), backward(mass, 1, 1))
        )
        for g in span:
            fields[0, g] = free[g]
            fields[1, g] = free[g] * (1.0 / HALF_WIDTH)
            fields[2, g] = (free[g] * mass[g] + (1.0 - free[g])) * (1.0 / HALF_WIDTH)

        rows8 = [pl.ds(8 * r, 8) for r in range(ny // 8)]

        def stress(j):
            grad = gradient([[basis[j, c, g] * fields[0, g] for g in span] for c in range(3)])
            pio = [[[[None] * len(rows8) for _ in span] for _ in range(3)] for _ in range(3)]
            for g in span:
                for r, at in enumerate(rows8):
                    d = [[grad[c][q][g][8 * r : 8 * r + 8] for q in range(3)] for c in range(3)]
                    f = [[state[3 * i + k, g, at] for k in range(3)] for i in range(3)]
                    pulled = [
                        [sum(f[k][a] * d[k][b] for k in range(3)) for b in range(3)] for a in range(3)
                    ]
                    lame, shear = state[15, g, at], state[16, g, at]
                    bulk = lame * (pulled[0][0] + pulled[1][1] + pulled[2][2])
                    t, s = {}, {}
                    for spot, (a, b) in enumerate(pairs):
                        v = shear * (pulled[a][b] + pulled[b][a])
                        t[a, b] = t[b, a] = v + bulk if a == b else v
                        s[a, b] = s[b, a] = state[9 + spot, g, at]
                    for i in range(3):
                        for b in range(3):
                            v = sum(f[i][k] * t[k, b] for k in range(3))
                            pio[i][b][g][r] = v + sum(d[i][k] * s[k, b] for k in range(3))
            pio = [[[jnp.concatenate(pio[c][b][g], axis=0) for g in span] for b in range(3)] for c in range(3)]
            return grad, pio

        def scatter(j, pio):
            for c in range(3):
                e = pio[c]
                wide = add(e[0], last_y(e[0]))
                tilt = sub(last_y(e[1]), e[1])
                rise = add(e[2], last_y(e[2]))
                minus, plus = sub(tilt, wide), add(tilt, wide)
                out = add(
                    add(sub(minus, rise), backward(add(minus, rise), 0, 1)),
                    add(backward(sub(plus, rise), 1, 0), backward(add(plus, rise), 1, 1)),
                )
                for g in span:
                    basis[j + 1, c, g] = fields[1, g] * out[g] + (
                        fields[2, g] - CHAIN[j] / HALF_WIDTH
                    ) * basis[j, c, g]

        def apply(j):
            scatter(j, stress(j)[1])

        mine = (depth >= halo) & (depth < halo + own) & (plane < plan.nz)
        spots = [(c, g, r) for c in range(3) for g in span for r in range(ny // 8)]
        mine = [mine[8 * r : 8 * r + 8] for r in range(ny // 8)]

        def divide(k):
            v = [jnp.where(mine[r], basis[k, c, g, rows8[r]], 0.0) for c, g, r in spots]
            top = jnp.abs(v[0])
            for u in v[1:]:
                top = jnp.maximum(top, jnp.abs(u))
            grain = top * (32768.0 * max(1, len(v) // 6))
            for s, u in enumerate(v):
                coarse = (u + grain) - grain
                parts[0, k, s] = coarse
                parts[1, k, s] = u - coarse

        def products(i, js):
            acc = {}
            for s in range(len(spots)):
                ch, cl = parts[0, i, s], parts[1, i, s]
                for j in js:
                    dh, dl = parts[0, j, s], parts[1, j, s]
                    new = [ch * dh, cl * (dh + ch + dl) if i == j else ch * dl + cl * (dh + dl)]
                    acc[j] = new if s == 0 else [acc[j][0] + new[0], acc[j][1] + new[1]]
            return {(i, j): tuple(acc[j]) for j in js}

        def merge(a, b, mask, shift):
            first_in, second_in = [], []
            for u, v in zip(a, b):
                if shift == 4:
                    first_in.append(jnp.where(mask, u, v))
                    second_in.append(pltpu.roll(jnp.where(mask, v, u), shift, 0))
                else:
                    first_in.append(jnp.where(mask, u, pltpu.roll(v, shift, 0)))
                    second_in.append(jnp.where(mask, pltpu.roll(u, 8 - shift, 0), v))
            return add_parts(tuple(first_in), tuple(second_in))

        def stack(items, slots):
            none = tuple(jnp.zeros((8, LANES), F32) for _ in next(iter(items.values())))
            it = [items.get(q, none) for q in slots]
            one = [merge(it[r], it[r + 4], row < 4, 4) for r in range(4)]
            twice = [merge(one[r], one[r + 2], lax.rem(row, 4) < 2, 2) for r in range(2)]
            return merge(twice[0], twice[1], lax.rem(row, 2) < 1, 1)

        def slots_of(table, q):
            at = {t: pair for pair, t in table.items()}
            return [at.get(8 * q + r) for r in range(8)]

        quarter = lane // 32

        def fold(tall):
            def turned(j):
                out = []
                for part in range(len(tall[0])):
                    v = None
                    for q in range(len(tall)):
                        u = tall[q][part]
                        u = pltpu.roll(u, LANES - 32 * j, 1) if j else u
                        v = u if v is None else jnp.where(quarter >= q, u, v)
                    out.append(v)
                return tuple(out)

            whole = add_all([turned(j) for j in range(4)])
            whole = add_all(
                [
                    tuple(pltpu.roll(u, own - j, 1, stride=1, stride_axis=0) for u in whole)
                    for j in range(own)
                ]
            )
            keep = lax.rem(lane + (2 * LANES - halo - own) - row, 32) == 0
            keep = keep & (lax.rem(lane + (LANES - halo - own) - row, LANES) < 32 * len(tall))
            return [jnp.sum(jnp.where(keep, u, 0.0), axis=0, keepdims=True) for u in whole]

        items = {}
        for k in range(STEPS):
            divide(k)
            for i in range(k + 1):
                items.update(products(i, [k]))
            if k == 3:
                single = {q: (items[q][0] + items[q][1],) for q in EARLY}
                early = [stack(single, slots_of(EARLY, q)) for q in range(2)]
                first_sums[worker] = fold(early)[0]
            if k < STEPS - 1:
                apply(k)
            if k == 3:
                when(me != last, lambda: pl.semaphore_wait(entered, 1))
                loop(total, lambda d: share(first_sums, 0, d))
        width, chain = recurrence()
        for i in range(5):
            up, same = items[i + 1, 5], items[i, 5]
            factor = float((chain[i] - chain[5]) / width)
            high_part, low_part = two_sum(up[0], factor * same[0])
            items[i, 6] = (high_part, low_part + (up[1] + factor * same[1]))
        tall = [stack(items, slots_of(PRODUCTS, q)) for q in range(4)]
        talls[...] = jnp.concatenate(fold(tall), axis=0)
        square[0] = items[5, 5][0]
        square[1] = items[5, 5][1]
        grad, pio = stress(5)
        energy = None
        for g in span:
            dense = sum(pio[c][b][g] * grad[c][b][g] for c in range(3) for b in range(3))
            for r in range(ny // 8):
                v = [basis[5, c, g, rows8[r]] for c in range(3)]
                nodes = fields[2, g, rows8[r]] * (v[0] * v[0] + v[1] * v[1] + v[2] * v[2])
                u = dense[8 * r : 8 * r + 8] * (1.0 / HALF_WIDTH) + nodes
                u = jnp.where(mine[r], u, 0.0)
                energy = u if energy is None else energy + u
        factor = float(-chain[5] / width)
        high_part, low_part = two_sum(energy, factor * square[0])
        ends = (high_part, low_part + factor * square[1])
        for shift in (4, 2, 1):
            ends = add_pair(ends, [pltpu.roll(u, shift, 0) for u in ends])
        sums[worker] = talls[...] + jnp.concatenate([u[0:1] for u in ends], axis=0)
        loop(total, lambda d: share(sums, 1, d))
        scatter(5, pio)

    fetched[4].wait()
    when(is_worker, work)
    when(
        jnp.logical_not(is_worker) & (me != last), lambda: pl.semaphore_wait(entered, 1)
    )

    stride = plan.stride

    def give_back():
        wide_lane = lax.broadcasted_iota(jnp.int32, (ny, LANES), 1)
        for k in range(1, 7):
            for x in range(ngx):
                g, d = x // mixed, x % mixed
                out = None
                for c in range(3):
                    for i in range(sx):
                        e = c * sx + i
                        s = (e * stride - ((d * sx + i) * pitch + halo)) % LANES
                        v = basis[k, c, g]
                        moved = pltpu.roll(v, s, 1) if s else v
                        out = moved if out is None else jnp.where(wide_lane >= e * stride, moved, out)
                for y in range(ngy):
                    back[x, y, k - 1] = out[sy * y : sy * (y + 1)]
        loop(n, lambda q: give(q, True))

    own_low = jnp.minimum(lax.div(own * worker, sz), ngz - 1)
    own_high = lax.div(jnp.minimum(own * worker + own, plan.nz) - 1, sz)
    straddles = sz % own != 0

    def give(q, start):
        x, y = (q // ngy, q % ngy) if isinstance(q, int) else (lax.div(q, ngy), lax.rem(q, ngy))

        def to(z):
            d = q * ngz + z
            dst = vt.at[worker - pick(plan.from_low, z)]
            remote = pltpu.make_async_remote_copy(
                src_ref=back.at[x, y],
                dst_ref=dst,
                send_sem=back_send.at[0],
                recv_sem=back_recv.at[0],
                **where_is(d),
            )
            if start:
                when(d != me, remote.start)
                when(
                    d == me,
                    lambda: pltpu.make_async_copy(back.at[x, y], dst, back_recv.at[0]).start(),
                )
            else:
                when(d != me, remote.wait_send)

        to(own_low)
        if straddles:
            when(own_high > own_low, lambda: to(own_high))

    when(is_worker, give_back)
    fetched[5].wait()

    counts = [b - a + 1 for a, b in zip(plan.from_low, plan.from_high)]
    if min(counts) == plan.returns:
        settle(vt, back_recv.at[0])
    else:
        for z in range(ngz):
            when(gz == z, lambda z=z: settle(vt.at[pl.ds(0, counts[z])], back_recv.at[0]))

    mates = [(k, c, i) for k in range(0, 6, 2) for c in range(3) for i in range(sx)]

    def collect(j, accs):
        w = pick(plan.from_low, gz) + j
        offset = own * w - sz * gz
        inside = (lane >= offset) & (lane < offset + own)
        if min(counts) != plan.returns:
            inside = inside & (j < pick(counts, gz))
        new = []
        stacked = [jnp.concatenate([vt[j, k], vt[j, k + 1]], axis=0) for k in range(0, 6, 2)]
        for (k, c, i), acc in zip(mates, accs):
            s = lax.rem(offset - (c * sx + i) * stride + 2 * LANES, LANES)
            moved = pltpu.roll(stacked[k // 2], s, 1)
            new.append(jnp.where(inside, moved, acc))
        return tuple(new)

    accs = tuple(jnp.zeros((8, LANES), F32) for _ in mates)
    if plan.returns <= 16:
        for j in range(plan.returns):
            accs = collect(j, accs)
    else:
        accs = lax.fori_loop(0, plan.returns, collect, accs)

    active = plan.workers

    def wait_rows(ref, sem, rows):
        while rows:
            now = min(rows, active)
            settle(ref.at[pl.ds(0, now)], sem)
            rows -= now

    def sent():
        loop(n, lambda q: give(q, False))
        wait_rows(first_sums, sum_send.at[0], total - 1)
        wait_rows(sums, sum_send.at[1], total - 1)

    loop(plan.sends, lambda j: piece(j, False))
    when(is_worker, sent)

    def landed(ref, slot):
        when(is_worker, lambda: wait_rows(ref, sum_recv.at[slot], active - 1))
        when(jnp.logical_not(is_worker), lambda: wait_rows(ref, sum_recv.at[slot], active))

    def total_of(ref, pair):
        zero = jnp.zeros(ref.shape[1:], F32)
        rest = (zero,) if pair else ()
        if active <= 32:
            return add_all([(ref[d], *rest) for d in range(active)])
        return lax.fori_loop(
            0, active, lambda d, a: add_parts(a, (ref[d], *rest)), (zero, *rest)
        )

    landed(first_sums, 0)
    first_total = jnp.broadcast_to(total_of(first_sums, False)[0], (8, LANES))

    def entry(i, j):
        s = place(EARLY[min(i, j), max(i, j)], halo + own)
        return jnp.broadcast_to(first_total[:, s : s + 1], (8, LANES))

    first_gram = [
        [HALF_WIDTH * entry(i, j + 1) + CHAIN[j] * entry(i, j) for j in range(3)]
        for i in range(3)
    ]
    c = solve_small(first_gram, [entry(i, 0) for i in range(3)])

    def affine(c, load_at):
        return ((load_at(0) + c[0] * load_at(1)) + c[1] * load_at(2)) + c[2] * load_at(3)

    def scaled(at, size, x):
        ch, cl, rest = (const[pl.ds(q, size), :] for q in at)
        xh, xl = split(x)
        p = (ch + cl) * x
        return p, (((ch * xh - p) + ch * xl + cl * xh) + cl * xl) + rest * x

    def times_pair(x, pair):
        p, e = two_product(x, pair[0])
        return p, e + x * pair[1]

    weights = []
    for v in range(2):
        side = [
            affine(c, lambda a, s=s: const[pl.ds((4 * s + a) * 16 + 8 * v, 8), :])
            for s in range(6)
        ]
        turn = [[24 * 16 + (3 * q + part) * 16 + 8 * v for part in range(3)] for q in range(3)]
        image = [
            add_pair(scaled(turn[q], 8, side[2 + q]), scaled(turn[2], 8, side[4 + q]))
            for q in range(2)
        ]
        weights.append(add_pair(times_pair(side[0], image[1]), times_pair(side[1], image[0])))

    landed(sums, 1)
    raw_sum, lost = total_of(sums, True)
    gram_high, gram_low = two_sum(raw_sum[0:1], raw_sum[1:2] + lost[0:1])
    gram_high = jnp.broadcast_to(gram_high, (8, LANES))
    gram_low = jnp.broadcast_to(gram_low, (8, LANES))
    halves = []
    for weight in weights:
        high_part, low_part = two_product(gram_high, weight[0])
        pair = (high_part, low_part + (gram_high * weight[1] + gram_low * weight[0]))
        halves.append(
            add_all([[pltpu.roll(u, LANES - 32 * q, 1) if q else u for u in pair] for q in range(4)])
        )
    pair = [jnp.where(lane < 64, u, v) for u, v in zip(*halves)]
    for s, times in ((8, 4), (1, 8)):
        pair = add_all(
            [[pltpu.roll(u, LANES - s * q, 1) if q else u for u in pair] for q in range(times)]
        )
    value = pair[0] + pair[1]
    done = [jnp.broadcast_to(value[:, 64 * v : 64 * v + 1], (8, LANES)) for v in range(2)]
    form = {
        q: jnp.broadcast_to(done[f // 8][f % 8 : f % 8 + 1], (8, LANES))
        for f, q in enumerate(FORMS)
    }
    gram = [[form[i, j] for j in range(3)] for i in range(3)]
    d = solve_small(gram, [form[i, None] for i in range(3)])
    base_at = 24 * 16 + 9 * 16
    vector = affine(c, lambda a: const[pl.ds(base_at + 8 * a, 8), :])
    moved = affine(c, lambda a: const[pl.ds(base_at + 32 + 8 * a, 8), :])
    turn = [[base_at + 64 + 8 * (3 * q + part) for part in range(3)] for q in range(2)]
    image = add_pair(scaled(turn[0], 8, vector), scaled(turn[1], 8, moved))
    factor = jnp.where(row == 0, -d[0], jnp.where(row == 1, -d[1], jnp.where(row == 2, -d[2], 1.0)))
    coef = times_pair(factor, image)
    coef = add_pair(coef, [pltpu.roll(u, 6, 0) for u in coef])
    coef = add_pair(coef, [pltpu.roll(u, 7, 0) for u in coef])
    coef = coef[0][0:1] + coef[1][0:1]

    def spread_coef(k):
        return jnp.broadcast_to(coef[:, k : k + 1], (8, LANES))

    for slot in range(2):
        w = [spread_coef(k) if slot else -spread_coef(32 + k) for k in range(7)]
        duo = [jnp.where(row < sy, w[k + 1], w[k + 2]) for k in range(0, 6, 2)]
        for cc in range(3):
            for i in range(sx):
                v = None
                for k in range(0, 6, 2):
                    u = duo[k // 2] * accs[mates.index((k, cc, i))]
                    v = u if v is None else v + u
                head = w[0][0:sy] * (raw[3 + cc, i] * raw[7, i])
                out_ref[slot, cc, sy * i : sy * (i + 1)] = head + (v[0:sy] + v[sy : 2 * sy])


def per_device(displacement, load, material, free_node, table):
    shard = displacement.shape[1:]
    sx, sy, sz = shard
    grid = tuple(lax.axis_size(a) for a in ("gx", "gy", "gz"))
    plan = Plan(grid, shard)
    ngx, ngy, ngz = grid
    ny = ngy * sy
    groups = plan.groups
    const = jnp.asarray(tables(plan))
    buffers = [
        pltpu.VMEM((FIELDS, sx, sy, sz), F32),
        pltpu.VMEM((2, sx, sy, sz), jnp.int32),
        pltpu.VMEM((plan.sends, plan.tiles, sy, LANES), F32),
        pltpu.VMEM((2, ngx, ngy, plan.tiles, sy, LANES), F32),
        pltpu.VMEM((7, 3, groups, ny, LANES), F32),
        pltpu.VMEM((3, groups, ny, LANES), F32),
        pltpu.VMEM((17, groups, ny, LANES), F32),
        pltpu.VMEM((2, 7, 3 * groups * ny // 8, 8, LANES), F32),
        pltpu.VMEM((ngx, ngy, 6, sy, LANES), F32),
        pltpu.VMEM((plan.returns, 6, sy, LANES), F32),
        pltpu.VMEM((plan.workers, 1, LANES), F32),
        pltpu.VMEM((plan.workers, 2, LANES), F32),
        pltpu.VMEM((2, LANES), F32),
        pltpu.VMEM((2, 8, LANES), F32),
        pltpu.VMEM(const.shape, F32),
        pltpu.SMEM(table.shape[::-1], F32),
        pltpu.SemaphoreType.DMA((6,)),
        pltpu.SemaphoreType.DMA((1,)),
        pltpu.SemaphoreType.DMA((2,)),
        pltpu.SemaphoreType.DMA((1,)),
        pltpu.SemaphoreType.DMA((1,)),
        pltpu.SemaphoreType.DMA((2,)),
        pltpu.SemaphoreType.DMA((2,)),
        pltpu.SemaphoreType.REGULAR,
    ]
    operands = (displacement, load, material, free_node, table.T, const)
    both = pl.pallas_call(
        functools.partial(kernel, plan),
        out_shape=jax.ShapeDtypeStruct((2, 3, sx * sy, sz), F32),
        in_specs=[pl.BlockSpec(memory_space=pltpu.HBM)] * 6,
        out_specs=pl.BlockSpec(memory_space=pltpu.VMEM),
        scratch_shapes=buffers,
        compiler_params=pltpu.CompilerParams(
            collective_id=0, has_side_effects=True, vmem_limit_bytes=32 << 20
        ),
    )(*(pltpu.with_memory_space_constraint(a, pltpu.HBM) for a in operands))
    return both[0].reshape(displacement.shape), both[1].reshape(displacement.shape)


def solution(mesh):
    in_specs = (
        P(None, "gx", "gy", "gz"),
        P(None, "gx", "gy", "gz"),
        P("gx", "gy", "gz"),
        P("gx", "gy", "gz"),
        P(),
    )
    out_specs = (P(None, "gx", "gy", "gz"), P(None, "gx", "gy", "gz"))
    return jax.shard_map(
        per_device, mesh=mesh, in_specs=in_specs, out_specs=out_specs, check_vma=False
    )
```

```python
import functools

import jax
import jax.numpy as jnp
import numpy as np
from jax import lax
from jax.experimental import pallas as pl
from jax.experimental.pallas import tpu as pltpu
from jax.sharding import PartitionSpec as P

SHIFTS = (9.6, 51.4)
HALF_WIDTH = 29.5
CHAIN = SHIFTS + (30.5,) + SHIFTS + (30.5,)
STEPS = 6
FIELDS = 8
ORDER = (0, 3, 1, 4, 2, 5, 6, 7)
LANES = 128
PRODUCTS = {(i, j): t for t, (i, j) in enumerate((i, j) for i in range(6) for j in range(i, 6))}
PRODUCTS.update({(i, 6): 21 + i for i in range(5)})
FORMS = [(i, j) for i in range(3) for j in range(3)] + [(i, None) for i in range(3)]
SLOTS = [*PRODUCTS.items(), *(((5, 6), t) for t in range(28, 32))]
EARLY = {(i, j): t for t, (i, j) in enumerate((i, j) for i in range(3) for j in range(i, 4))}
F32 = jnp.float32


def place(t, base):
    return (32 * (t // 8) + base + t % 8) % LANES


def bits(x):
    top = np.asarray(x, np.float32)
    t = np.float32(4097.0) * top
    high = t - (t - top)
    return high, top - high, (x - top.astype(np.float64)).astype(np.float32)


def recurrence():
    width = 1.0 / np.float64(np.float32(1.0 / HALF_WIDTH))
    return width, np.array([np.float64(np.float32(x / HALF_WIDTH)) * width for x in CHAIN] + [0.0])


def tables(base):
    width, chain = recurrence()

    def shifted(x):
        return np.concatenate([[0.0], x[:-1]])

    def times(x):
        return chain * x + width * shifted(x)

    unit = np.eye(7)
    b = [[unit[0]] + [-times(unit[j]) for j in range(3)]]
    for j in range(2):
        b.append([(times(x) - SHIFTS[j] * x) / HALF_WIDTH for x in b[j]])
    wide = np.zeros((6, 4, 16, LANES))
    turn = np.zeros((3, 16, LANES))
    for f, (i, j) in enumerate(FORMS):
        for (one, two), t in SLOTS:
            at = place(t, base)
            turn[:, f, at] = (1.0, 1.0, 0.0) if j is None else (chain[one], chain[two], width)
            for a in range(4):
                left, right = b[i][a], b[j or 0][a]
                wide[0, a, f, at] = left[one]
                wide[1, a, f, at] = left[two] if one != two else 0.0
                wide[2, a, f, at] = right[one]
                wide[3, a, f, at] = right[two]
                wide[4, a, f, at] = shifted(right)[one]
                wide[5, a, f, at] = shifted(right)[two]
    last = np.zeros((2, 4, 8, LANES))
    final = np.zeros((2, 8, LANES))
    for k in range(7):
        final[:, :3, k] = np.array([[chain[k]], [width]])
        final[0, :3, 32 + k] = 1.0
        final[0, 3, k] = final[0, 3, 32 + k] = 1.0
        for a in range(4):
            for j in range(3):
                last[0, a, j, k] = last[0, a, j, 32 + k] = b[j][a][k]
                last[1, a, j, k] = shifted(b[j][a])[k]
            last[0, a, 3, k] = b[0][a][k]
            last[0, a, 3, 32 + k] = -1.0 if 0 < a == k + 1 else 0.0
    blocks = [wide, *(np.stack(bits(x)) for x in turn), last, *(np.stack(bits(x)) for x in final)]
    return np.concatenate([x.reshape(-1, LANES).astype(np.float32) for x in blocks])


def solve_small(gram, right):
    sym = [[0.5 * (gram[i][j] + gram[j][i]) for j in range(3)] for i in range(3)]
    r0 = 1.0 / sym[0][0]
    l10 = sym[1][0] * r0
    l20 = sym[2][0] * r0
    r1 = 1.0 / (sym[1][1] - l10 * sym[1][0])
    e = sym[2][1] - l20 * sym[1][0]
    l21 = e * r1
    d2 = sym[2][2] - l20 * sym[2][0] - l21 * e
    y1 = right[1] - l10 * right[0]
    c2 = (right[2] - l20 * right[0] - l21 * y1) / d2
    c1 = y1 * r1 - l21 * c2
    c0 = right[0] * r0 - l10 * c1 - l20 * c2
    return [c0, c1, c2]


def two_sum(a, b):
    s = a + b
    t = s - a
    return s, (a - (s - t)) + (b - t)


def add_pair(p, q):
    s, e = two_sum(p[0], q[0])
    return s, e + (p[1] + q[1])


def add_parts(p, q):
    return add_pair(p, q) if len(p) == 2 else (p[0] + q[0],)


def add_all(terms):
    while len(terms) > 1:
        rest = terms[len(terms) & ~1 :]
        terms = [add_parts(p, q) for p, q in zip(terms[::2], terms[1::2])] + rest
    return terms[0]


def split(a):
    t = 4097.0 * a
    high = t - (t - a)
    return high, a - high


def two_product(a, b):
    p = a * b
    (ah, al), (bh, bl) = split(a), split(b)
    return p, ((ah * bh - p) + ah * bl + al * bh) + al * bl


def loop(count, body):
    if count <= 32:
        for i in range(count):
            body(i)
    else:

        def step(i, carry):
            body(i)
            return carry

        lax.fori_loop(0, count, step, 0)


def when(condition, body):
    if isinstance(condition, bool):
        if condition:
            body()
    else:
        pl.when(condition)(body)


class Plan:
    def __init__(self, grid, shard):
        self.grid, self.shard = grid, shard
        ngx, ngy, ngz = grid
        sx, sy, sz = shard
        self.n = ngx * ngy
        self.nz = ngz * sz
        self.halo = STEPS
        total = self.n * ngz
        self.pitch = 1 << (-(-self.nz // total) + 2 * self.halo - 1).bit_length()
        spare = total - -(-self.nz // (self.pitch - 2 * self.halo))
        self.counts = [self.n] * (ngz - 1) + [max(2, self.n - spare)]
        self.own = -(-self.nz // sum(self.counts))
        self.span = self.own + 2 * self.halo
        self.packed = LANES // self.pitch
        self.groups = ngx * sx // self.packed
        self.mixed = LANES // (sx * self.pitch)
        self.tiles = FIELDS // self.mixed
        self.stride = LANES // (3 * sx)
        self.workers = -(-self.nz // self.own)
        self.base = [sum(self.counts[:z]) for z in range(ngz)]
        own, halo = self.own, self.halo
        self.to_low = [max(0, (sz * z - own - halo) // own + 1) for z in range(ngz)]
        self.to_high = [
            min(self.workers - 1, -(-(sz * z + sz + halo) // own) - 1) for z in range(ngz)
        ]
        self.from_low = [sz * z // own for z in range(ngz)]
        self.from_high = [(sz * z + sz - 1) // own for z in range(ngz)]
        self.sends = max(b - a + 1 for a, b in zip(self.to_low, self.to_high))
        self.returns = max(b - a + 1 for a, b in zip(self.from_low, self.from_high))
        assert sz == LANES and 8 == 2 * sy and own <= self.stride and halo + own <= 56


def pick(values, z):
    if all(v == values[0] for v in values):
        return values[0]
    out = values[0]
    for k in range(1, len(values)):
        out = jnp.where(z >= k, values[k], out)
    return out


def kernel(
    plan,
    disp_hbm,
    load_hbm,
    mat_hbm,
    free_hbm,
    table_hbm,
    const_hbm,
    out_ref,
    raw,
    flags,
    pack,
    recv,
    basis,
    fields,
    state,
    parts,
    back,
    vt,
    first_sums,
    sums,
    talls,
    square,
    const,
    table_ref,
    in_sem,
    send_sem,
    recv_sem,
    back_send,
    back_recv,
    sum_send,
    sum_recv,
    entered,
):
    ngx, ngy, ngz = plan.grid
    sx, sy, sz = plan.shard
    n, own, halo, pitch = plan.n, plan.own, plan.halo, plan.pitch
    nx, ny = ngx * sx, ngy * sy
    groups, mixed, tiles = plan.groups, plan.mixed, plan.tiles
    total = n * ngz
    gx, gy, gz = lax.axis_index("gx"), lax.axis_index("gy"), lax.axis_index("gz")
    p = gx * ngy + gy
    me = p * ngz + gz
    count = pick(plan.counts, gz)
    worker = pick(plan.base, gz) + count - 1 - p
    is_worker = (p < count) & (worker < plan.workers)
    first = own * worker - halo
    settled = jnp.maximum(first, 0)
    low_slab = jnp.minimum(lax.div(settled, sz), ngz - 1)
    edge = sz * (low_slab + 1)
    two = (first + plan.span > edge) & (low_slab + 1 < ngz)
    last = total - 1

    fetched = [
        pltpu.make_async_copy(disp_hbm, raw.at[pl.ds(0, 3)], in_sem.at[0]),
        pltpu.make_async_copy(load_hbm, raw.at[pl.ds(3, 3)], in_sem.at[1]),
        pltpu.make_async_copy(mat_hbm, flags.at[0], in_sem.at[2]),
        pltpu.make_async_copy(free_hbm, flags.at[1], in_sem.at[3]),
        pltpu.make_async_copy(table_hbm, table_ref, in_sem.at[4]),
        pltpu.make_async_copy(const_hbm, const, in_sem.at[5]),
    ]
    for copy in fetched:
        copy.start()

    def where_is(d):
        return dict(device_id=d, device_id_type=pl.DeviceIdType.LOGICAL)

    barrier = pltpu.get_barrier_semaphore()

    def greet(d):
        pl.semaphore_signal(barrier, inc=1, **where_is(d))

    def greet_slab(z):
        def one(q):
            d = q * ngz + z
            when((d != me) & (d != last), lambda: greet(d))

        loop(n, one)

    when(is_worker, lambda: greet_slab(low_slab))
    when(is_worker & two, lambda: greet_slab(low_slab + 1))
    when(me != last, lambda: greet(last))

    for copy in fetched[:4]:
        copy.wait()
    raw[6] = flags[0].astype(F32)
    raw[7] = flags[1].astype(F32)

    lane = lax.broadcasted_iota(jnp.int32, (8, LANES), 1)
    row = lax.broadcasted_iota(jnp.int32, (8, LANES), 0)
    per = 8 // sy
    stacks = -(-tiles // per)
    held = []
    for t in range(stacks):
        part = []
        for e in range(mixed * sx):
            f, i = e // sx, e % sx
            rows = [
                raw[ORDER[mixed * min(per * t + h, tiles - 1) + f], i] for h in range(per)
            ]
            part.append(jnp.concatenate(rows, axis=0))
        turned = []
        for e in range(mixed * sx):
            v = part[e]
            for k in range(1, mixed):
                v = jnp.where(lax.rem(gx, mixed) == k, part[(e - k * sx) % (mixed * sx)], v)
            turned.append(v)
        held.append(turned)

    to_low = pick(plan.to_low, gz)
    to_count = pick([b - a + 1 for a, b in zip(plan.to_low, plan.to_high)], gz)

    def route(j):
        w = to_low + j
        z = 0
        for k in range(1, ngz):
            z = z + jnp.where(w >= plan.base[k], 1, 0)
        q = pick([b + c - 1 for b, c in zip(plan.base, plan.counts)], z) - w
        slot = jnp.where(sz * gz > jnp.maximum(own * w - halo, 0), 1, 0)
        return j < to_count, slot, q * ngz + z

    def prepare(j):
        w = to_low + j
        offset = sz * gz - (own * w - halo)
        for t in range(stacks):
            out = None
            for e, v in enumerate(held[t]):
                moved = pltpu.roll(v, lax.rem(offset + (pitch * e + 8 * LANES), LANES), 1)
                out = moved if out is None else jnp.where(lane >= pitch * e, moved, out)
            for h in range(min(per, tiles - per * t)):
                pack[j, per * t + h] = out[sy * h : sy * (h + 1)]

    loop(plan.sends, prepare)

    expected = to_count
    if plan.sends <= 32:
        routes = [route(j) for j in range(plan.sends)]
        for valid, _, d in routes:
            expected = expected - jnp.where(valid & (d == me), 1, 0)
    else:
        routes = None

        def count_self(j, seen):
            valid, _, d = route(j)
            return seen - jnp.where(valid & (d == me), 1, 0)

        expected = lax.fori_loop(0, plan.sends, count_self, expected)
    expected = jnp.where(me == last, total - 1, expected)
    pl.semaphore_wait(barrier, expected)

    def piece(j, start):
        valid, slot, d = routes[j] if routes else route(j)
        dst = recv.at[slot, gx, gy]
        remote = pltpu.make_async_remote_copy(
            src_ref=pack.at[j],
            dst_ref=dst,
            send_sem=send_sem.at[0],
            recv_sem=recv_sem.at[slot],
            **where_is(d),
        )
        if start:
            when(valid & (d != me), remote.start)
            when(
                valid & (d == me),
                lambda: pltpu.make_async_copy(pack.at[j], dst, recv_sem.at[slot]).start(),
            )
        else:
            when(valid & (d != me), remote.wait_send)

    loop(plan.sends, lambda j: piece(j, True))

    def announce():
        loop(total - 1, lambda d: pl.semaphore_signal(entered, inc=1, **where_is(d)))

    when(me == last, announce)

    def settle(ref, sem):
        pltpu.make_async_copy(ref, ref, sem).wait()

    def share(ref, slot, d):
        when(
            me != d,
            pltpu.make_async_remote_copy(
                src_ref=ref.at[worker],
                dst_ref=ref.at[worker],
                send_sem=sum_send.at[slot],
                recv_sem=sum_recv.at[slot],
                **where_is(d),
            ).start,
        )

    def work():
        settle(recv.at[0], recv_sem.at[0])
        when(two, lambda: settle(recv.at[1], recv_sem.at[1]))

        wide_lane = lax.broadcasted_iota(jnp.int32, (ny, LANES), 1)
        depth = lax.rem(wide_lane, pitch)
        plane = depth + first
        near = plane < edge
        seg = sx * pitch

        def gather_rows(slot, k, x):
            return jnp.concatenate([recv[slot, x, g, k] for g in range(ngy)], axis=0)

        def source(k, x):
            return jnp.where(near, gather_rows(0, k, x), gather_rows(1, k, x))

        def unpack(k, g):
            parts_in = [source(k, g * mixed + d) for d in range(mixed)]
            out = []
            for f in range(mixed):
                v = None
                for at in range(mixed):
                    u = parts_in[(at - f) % mixed]
                    v = u if v is None else jnp.where(wide_lane >= at * seg, u, v)
                out.append(pltpu.roll(v, LANES - f * seg, 1) if f else v)
            return out

        got = [[None] * groups for _ in range(FIELDS)]
        for g in range(groups):
            for k in range(tiles):
                for f, v in enumerate(unpack(k, g)):
                    got[ORDER[mixed * k + f]][g] = v

        span = range(groups)

        def next_y(a):
            return [pltpu.roll(v, ny - 1, 0) for v in a]

        def last_y(a):
            return [pltpu.roll(v, 1, 0) for v in a]

        def forward(a, x, z):
            moved = [pltpu.roll(v, LANES - pitch * x - z, 1) for v in a]
            if groups == 1 or not x:
                return moved
            wrap = wide_lane >= LANES - pitch
            return [jnp.where(wrap, moved[min(g + 1, groups - 1)], moved[g]) for g in span]

        def backward(a, x, z):
            moved = [pltpu.roll(v, pitch * x + z, 1) for v in a]
            if groups == 1 or not x:
                return moved
            wrap = wide_lane < pitch
            return [jnp.where(wrap, moved[max(g - 1, 0)], moved[g]) for g in span]

        def both(op, *lists):
            return [op(*vs) for vs in zip(*lists)]

        add = functools.partial(both, lambda a, b: a + b)
        sub = functools.partial(both, lambda a, b: a - b)

        def gradient(vector):
            grad = []
            for v in vector:
                above, over, far = forward(v, 0, 1), forward(v, 1, 0), forward(v, 1, 1)
                near_z, far_z = add(v, above), add(over, far)
                wide, flat = sub(far_z, near_z), add(far_z, near_z)
                rise = add(sub(above, v), sub(far, over))
                grad.append([add(next_y(wide), wide), sub(next_y(flat), flat), add(next_y(rise), rise)])
            return grad

        pairs = [(0, 0), (0, 1), (0, 2), (1, 1), (1, 2), (2, 2)]
        free = got[7]
        for c in range(3):
            for g in span:
                basis[0, c, g] = got[3 + c][g] * free[g]
        grad = gradient([got[0], got[1], got[2]])
        mass = []
        high = lax.broadcasted_iota(jnp.int32, (ny, LANES), 0)
        for g in span:
            valid = (high <= ny - 2) & (plane >= 0) & (plane <= plan.nz - 2) & (depth <= plan.span - 2)
            valid = valid & (lax.div(wide_lane, pitch) + g * plan.packed <= nx - 2)
            material = got[6][g]
            zero = jnp.zeros((ny, LANES), F32)
            lame, shear, heavy = zero, zero, zero
            for r in range(table_ref.shape[1]):
                hit = material == float(r)
                lame = jnp.where(hit, table_ref[0, r], lame)
                shear = jnp.where(hit, table_ref[1, r], shear)
                heavy = jnp.where(hit, table_ref[2, r], heavy)
            lame = jnp.where(valid, lame * 0.0625, 0.0)
            shear = jnp.where(valid, shear * 0.0625, 0.0)
            mass.append(jnp.where(valid, heavy * 0.125, 0.0))
            frame = [
                [0.25 * grad[i][j][g] + (1.0 if i == j else 0.0) for j in range(3)] for i in range(3)
            ]
            strain = {}
            for i, j in pairs:
                v = sum(frame[k][i] * frame[k][j] for k in range(3))
                strain[i, j] = 0.5 * (v - 1.0 if i == j else v)
            bulk = lame * (strain[0, 0] + strain[1, 1] + strain[2, 2])
            for i in range(3):
                for j in range(3):
                    state[3 * i + j, g] = frame[i][j]
            for spot, (i, j) in enumerate(pairs):
                v = 2.0 * shear * strain[i, j]
                state[9 + spot, g] = v + bulk if i == j else v
            state[15, g] = lame
            state[16, g] = shear
        mass = add(mass, last_y(mass))
        mass = add(
            add(mass, backward(mass, 0, 1)), add(backward(mass, 1, 0), backward(mass, 1, 1))
        )
        for g in span:
            fields[0, g] = free[g]
            fields[1, g] = free[g] * (1.0 / HALF_WIDTH)
            fields[2, g] = (free[g] * mass[g] + (1.0 - free[g])) * (1.0 / HALF_WIDTH)

        rows8 = [pl.ds(8 * r, 8) for r in range(ny // 8)]

        def stress(j):
            grad = gradient([[basis[j, c, g] * fields[0, g] for g in span] for c in range(3)])
            pio = [[[[None] * len(rows8) for _ in span] for _ in range(3)] for _ in range(3)]
            for g in span:
                for r, at in enumerate(rows8):
                    d = [[grad[c][q][g][8 * r : 8 * r + 8] for q in range(3)] for c in range(3)]
                    f = [[state[3 * i + k, g, at] for k in range(3)] for i in range(3)]
                    pulled = [
                        [sum(f[k][a] * d[k][b] for k in range(3)) for b in range(3)] for a in range(3)
                    ]
                    lame, shear = state[15, g, at], state[16, g, at]
                    bulk = lame * (pulled[0][0] + pulled[1][1] + pulled[2][2])
                    t, s = {}, {}
                    for spot, (a, b) in enumerate(pairs):
                        v = shear * (pulled[a][b] + pulled[b][a])
                        t[a, b] = t[b, a] = v + bulk if a == b else v
                        s[a, b] = s[b, a] = state[9 + spot, g, at]
                    for i in range(3):
                        for b in range(3):
                            v = sum(f[i][k] * t[k, b] for k in range(3))
                            pio[i][b][g][r] = v + sum(d[i][k] * s[k, b] for k in range(3))
            pio = [[[jnp.concatenate(pio[c][b][g], axis=0) for g in span] for b in range(3)] for c in range(3)]
            return grad, pio

        def scatter(j, pio):
            for c in range(3):
                e = pio[c]
                wide = add(e[0], last_y(e[0]))
                tilt = sub(last_y(e[1]), e[1])
                rise = add(e[2], last_y(e[2]))
                minus, plus = sub(tilt, wide), add(tilt, wide)
                out = add(
                    add(sub(minus, rise), backward(add(minus, rise), 0, 1)),
                    add(backward(sub(plus, rise), 1, 0), backward(add(plus, rise), 1, 1)),
                )
                for g in span:
                    basis[j + 1, c, g] = fields[1, g] * out[g] + (
                        fields[2, g] - CHAIN[j] / HALF_WIDTH
                    ) * basis[j, c, g]

        def apply(j):
            scatter(j, stress(j)[1])

        mine = (depth >= halo) & (depth < halo + own) & (plane < plan.nz)
        spots = [(c, g, r) for c in range(3) for g in span for r in range(ny // 8)]
        mine = [mine[8 * r : 8 * r + 8] for r in range(ny // 8)]

        def divide(k):
            v = [jnp.where(mine[r], basis[k, c, g, rows8[r]], 0.0) for c, g, r in spots]
            top = jnp.abs(v[0])
            for u in v[1:]:
                top = jnp.maximum(top, jnp.abs(u))
            grain = top * (32768.0 * max(1, len(v) // 6))
            for s, u in enumerate(v):
                coarse = (u + grain) - grain
                parts[0, k, s] = coarse
                parts[1, k, s] = u - coarse

        def products(i, js):
            acc = {}
            for s in range(len(spots)):
                ch, cl = parts[0, i, s], parts[1, i, s]
                for j in js:
                    dh, dl = parts[0, j, s], parts[1, j, s]
                    new = [ch * dh, cl * (dh + ch + dl) if i == j else ch * dl + cl * (dh + dl)]
                    acc[j] = new if s == 0 else [acc[j][0] + new[0], acc[j][1] + new[1]]
            return {(i, j): tuple(acc[j]) for j in js}

        def merge(a, b, mask, shift):
            first_in, second_in = [], []
            for u, v in zip(a, b):
                if shift == 4:
                    first_in.append(jnp.where(mask, u, v))
                    second_in.append(pltpu.roll(jnp.where(mask, v, u), shift, 0))
                else:
                    first_in.append(jnp.where(mask, u, pltpu.roll(v, shift, 0)))
                    second_in.append(jnp.where(mask, pltpu.roll(u, 8 - shift, 0), v))
            return add_parts(tuple(first_in), tuple(second_in))

        def stack(items, slots):
            none = tuple(jnp.zeros((8, LANES), F32) for _ in next(iter(items.values())))
            it = [items.get(q, none) for q in slots]
            one = [merge(it[r], it[r + 4], row < 4, 4) for r in range(4)]
            twice = [merge(one[r], one[r + 2], lax.rem(row, 4) < 2, 2) for r in range(2)]
            return merge(twice[0], twice[1], lax.rem(row, 2) < 1, 1)

        def slots_of(table, q):
            at = {t: pair for pair, t in table.items()}
            return [at.get(8 * q + r) for r in range(8)]

        quarter = lane // 32

        def squeeze(tall):
            def turned(j):
                out = []
                for part in range(len(tall[0])):
                    v = None
                    for q in range(len(tall)):
                        u = tall[q][part]
                        u = pltpu.roll(u, LANES - 32 * j, 1) if j else u
                        v = u if v is None else jnp.where(quarter >= q, u, v)
                    out.append(v)
                return tuple(out)

            return add_all([turned(j) for j in range(4)])

        def spread(whole, count):
            whole = add_all(
                [
                    tuple(pltpu.roll(u, own - j, 1, stride=1, stride_axis=0) for u in whole)
                    for j in range(own)
                ]
            )
            keep = lax.rem(lane + (2 * LANES - halo - own) - row, 32) == 0
            keep = keep & (lax.rem(lane + (LANES - halo - own) - row, LANES) < 32 * count)
            return [jnp.sum(jnp.where(keep, u, 0.0), axis=0, keepdims=True) for u in whole]

        items = {}
        for k in range(STEPS):
            divide(k)
            for i in range(k + 1):
                items.update(products(i, [k]))
            if k == 3:
                single = {q: (items[q][0] + items[q][1],) for q in EARLY}
                early = [stack(single, slots_of(EARLY, q)) for q in range(2)]
                first_sums[worker] = spread(squeeze(early), 2)[0]
            if k < STEPS - 1:
                apply(k)
        width, chain = recurrence()
        for i in range(5):
            up, same = items[i + 1, 5], items[i, 5]
            factor = float((chain[i] - chain[5]) / width)
            high_part, low_part = two_sum(up[0], factor * same[0])
            items[i, 6] = (high_part, low_part + (up[1] + factor * same[1]))
        ready = squeeze([stack(items, slots_of(PRODUCTS, q)) for q in range(3)])
        fourth = stack(items, slots_of(PRODUCTS, 3))
        for part in range(2):
            talls[0, part] = ready[part]
            talls[1, part] = fourth[part]
        square[0] = items[5, 5][0]
        square[1] = items[5, 5][1]
        when(me != last, lambda: pl.semaphore_wait(entered, 1))
        loop(total, lambda d: share(first_sums, 0, d))
        grad, pio = stress(5)
        energy = None
        for g in span:
            dense = sum(pio[c][b][g] * grad[c][b][g] for c in range(3) for b in range(3))
            for r in range(ny // 8):
                v = [basis[5, c, g, rows8[r]] for c in range(3)]
                nodes = fields[2, g, rows8[r]] * (v[0] * v[0] + v[1] * v[1] + v[2] * v[2])
                u = dense[8 * r : 8 * r + 8] * (1.0 / HALF_WIDTH) + nodes
                u = jnp.where(mine[r], u, 0.0)
                energy = u if energy is None else energy + u
        factor = float(-chain[5] / width)
        high_part, low_part = two_sum(energy, factor * square[0])
        ends = (high_part, low_part + factor * square[1])
        ends = add_pair(ends, [pltpu.roll(u, 4, 0) for u in ends])
        newest = squeeze([tuple(jnp.where(row < 4, talls[1, p], ends[p]) for p in range(2))])
        whole = tuple(jnp.where(quarter == 3, newest[p], talls[0, p]) for p in range(2))
        sums[worker] = jnp.concatenate(spread(whole, 4), axis=0)
        loop(total, lambda d: share(sums, 1, d))
        scatter(5, pio)

    fetched[4].wait()
    when(is_worker, work)
    when(
        jnp.logical_not(is_worker) & (me != last), lambda: pl.semaphore_wait(entered, 1)
    )

    stride = plan.stride

    def give_back():
        wide_lane = lax.broadcasted_iota(jnp.int32, (ny, LANES), 1)
        for k in range(1, 7):
            for x in range(ngx):
                g, d = x // mixed, x % mixed
                out = None
                for c in range(3):
                    for i in range(sx):
                        e = c * sx + i
                        s = (e * stride - ((d * sx + i) * pitch + halo)) % LANES
                        v = basis[k, c, g]
                        moved = pltpu.roll(v, s, 1) if s else v
                        out = moved if out is None else jnp.where(wide_lane >= e * stride, moved, out)
                for y in range(ngy):
                    back[x, y, k - 1] = out[sy * y : sy * (y + 1)]
        loop(n, lambda q: give(q, True))

    own_low = jnp.minimum(lax.div(own * worker, sz), ngz - 1)
    own_high = lax.div(jnp.minimum(own * worker + own, plan.nz) - 1, sz)
    straddles = sz % own != 0

    def give(q, start):
        x, y = (q // ngy, q % ngy) if isinstance(q, int) else (lax.div(q, ngy), lax.rem(q, ngy))

        def to(z):
            d = q * ngz + z
            dst = vt.at[worker - pick(plan.from_low, z)]
            remote = pltpu.make_async_remote_copy(
                src_ref=back.at[x, y],
                dst_ref=dst,
                send_sem=back_send.at[0],
                recv_sem=back_recv.at[0],
                **where_is(d),
            )
            if start:
                when(d != me, remote.start)
                when(
                    d == me,
                    lambda: pltpu.make_async_copy(back.at[x, y], dst, back_recv.at[0]).start(),
                )
            else:
                when(d != me, remote.wait_send)

        to(own_low)
        if straddles:
            when(own_high > own_low, lambda: to(own_high))

    when(is_worker, give_back)
    fetched[5].wait()

    counts = [b - a + 1 for a, b in zip(plan.from_low, plan.from_high)]
    if min(counts) == plan.returns:
        settle(vt, back_recv.at[0])
    else:
        for z in range(ngz):
            when(gz == z, lambda z=z: settle(vt.at[pl.ds(0, counts[z])], back_recv.at[0]))

    mates = [(k, c, i) for k in range(0, 6, 2) for c in range(3) for i in range(sx)]

    def collect(j, accs):
        w = pick(plan.from_low, gz) + j
        offset = own * w - sz * gz
        inside = (lane >= offset) & (lane < offset + own)
        if min(counts) != plan.returns:
            inside = inside & (j < pick(counts, gz))
        new = []
        stacked = [jnp.concatenate([vt[j, k], vt[j, k + 1]], axis=0) for k in range(0, 6, 2)]
        for (k, c, i), acc in zip(mates, accs):
            s = lax.rem(offset - (c * sx + i) * stride + 2 * LANES, LANES)
            moved = pltpu.roll(stacked[k // 2], s, 1)
            new.append(jnp.where(inside, moved, acc))
        return tuple(new)

    accs = tuple(jnp.zeros((8, LANES), F32) for _ in mates)
    if plan.returns <= 16:
        for j in range(plan.returns):
            accs = collect(j, accs)
    else:
        accs = lax.fori_loop(0, plan.returns, collect, accs)

    active = plan.workers

    def wait_rows(ref, sem, rows):
        while rows:
            now = min(rows, active)
            settle(ref.at[pl.ds(0, now)], sem)
            rows -= now

    def sent():
        loop(n, lambda q: give(q, False))
        wait_rows(first_sums, sum_send.at[0], total - 1)
        wait_rows(sums, sum_send.at[1], total - 1)

    loop(plan.sends, lambda j: piece(j, False))
    when(is_worker, sent)

    def landed(ref, slot):
        when(is_worker, lambda: wait_rows(ref, sum_recv.at[slot], active - 1))
        when(jnp.logical_not(is_worker), lambda: wait_rows(ref, sum_recv.at[slot], active))

    def total_of(ref, pair):
        zero = jnp.zeros(ref.shape[1:], F32)
        rest = (zero,) if pair else ()
        if active <= 32:
            return add_all([(ref[d], *rest) for d in range(active)])
        return lax.fori_loop(
            0, active, lambda d, a: add_parts(a, (ref[d], *rest)), (zero, *rest)
        )

    landed(first_sums, 0)
    first_total = jnp.broadcast_to(total_of(first_sums, False)[0], (8, LANES))

    def entry(i, j):
        s = place(EARLY[min(i, j), max(i, j)], halo + own)
        return jnp.broadcast_to(first_total[:, s : s + 1], (8, LANES))

    first_gram = [
        [HALF_WIDTH * entry(i, j + 1) + CHAIN[j] * entry(i, j) for j in range(3)]
        for i in range(3)
    ]
    c = solve_small(first_gram, [entry(i, 0) for i in range(3)])

    def affine(c, load_at):
        return ((load_at(0) + c[0] * load_at(1)) + c[1] * load_at(2)) + c[2] * load_at(3)

    def scaled(at, size, x):
        ch, cl, rest = (const[pl.ds(q, size), :] for q in at)
        xh, xl = split(x)
        p = (ch + cl) * x
        return p, (((ch * xh - p) + ch * xl + cl * xh) + cl * xl) + rest * x

    def times_pair(x, pair):
        p, e = two_product(x, pair[0])
        return p, e + x * pair[1]

    weights = []
    for v in range(2):
        side = [
            affine(c, lambda a, s=s: const[pl.ds((4 * s + a) * 16 + 8 * v, 8), :])
            for s in range(6)
        ]
        turn = [[24 * 16 + (3 * q + part) * 16 + 8 * v for part in range(3)] for q in range(3)]
        image = [
            add_pair(scaled(turn[q], 8, side[2 + q]), scaled(turn[2], 8, side[4 + q]))
            for q in range(2)
        ]
        weights.append(add_pair(times_pair(side[0], image[1]), times_pair(side[1], image[0])))

    landed(sums, 1)
    raw_sum, lost = total_of(sums, True)
    gram_high, gram_low = two_sum(raw_sum[0:1], raw_sum[1:2] + lost[0:1])
    gram_high = jnp.broadcast_to(gram_high, (8, LANES))
    gram_low = jnp.broadcast_to(gram_low, (8, LANES))
    halves = []
    for weight in weights:
        high_part, low_part = two_product(gram_high, weight[0])
        pair = (high_part, low_part + (gram_high * weight[1] + gram_low * weight[0]))
        halves.append(
            add_all([[pltpu.roll(u, LANES - 32 * q, 1) if q else u for u in pair] for q in range(4)])
        )
    pair = [jnp.where(lane < 64, u, v) for u, v in zip(*halves)]
    pair = add_all([[pltpu.roll(u, LANES - q, 1) if q else u for u in pair] for q in range(8)])
    value = pair[0] + pair[1]
    done = []
    for v in range(2):
        at = halo + own + 64 * v
        done.append(jnp.broadcast_to(value[:, at : at + 1], (8, LANES)))
    form = {
        q: jnp.broadcast_to(done[f // 8][f % 8 : f % 8 + 1], (8, LANES))
        for f, q in enumerate(FORMS)
    }
    gram = [[form[i, j] for j in range(3)] for i in range(3)]
    d = solve_small(gram, [form[i, None] for i in range(3)])
    base_at = 24 * 16 + 9 * 16
    vector = affine(c, lambda a: const[pl.ds(base_at + 8 * a, 8), :])
    moved = affine(c, lambda a: const[pl.ds(base_at + 32 + 8 * a, 8), :])
    turn = [[base_at + 64 + 8 * (3 * q + part) for part in range(3)] for q in range(2)]
    image = add_pair(scaled(turn[0], 8, vector), scaled(turn[1], 8, moved))
    factor = jnp.where(row == 0, -d[0], jnp.where(row == 1, -d[1], jnp.where(row == 2, -d[2], 1.0)))
    coef = times_pair(factor, image)
    coef = add_pair(coef, [pltpu.roll(u, 6, 0) for u in coef])
    coef = add_pair(coef, [pltpu.roll(u, 7, 0) for u in coef])
    coef = coef[0][0:1] + coef[1][0:1]

    def spread_coef(k):
        return jnp.broadcast_to(coef[:, k : k + 1], (8, LANES))

    for slot in range(2):
        w = [spread_coef(k) if slot else -spread_coef(32 + k) for k in range(7)]
        duo = [jnp.where(row < sy, w[k + 1], w[k + 2]) for k in range(0, 6, 2)]
        for cc in range(3):
            for i in range(sx):
                v = None
                for k in range(0, 6, 2):
                    u = duo[k // 2] * accs[mates.index((k, cc, i))]
                    v = u if v is None else v + u
                head = w[0][0:sy] * (raw[3 + cc, i] * raw[7, i])
                out_ref[slot, cc, sy * i : sy * (i + 1)] = head + (v[0:sy] + v[sy : 2 * sy])


def per_device(displacement, load, material, free_node, table):
    shard = displacement.shape[1:]
    sx, sy, sz = shard
    grid = tuple(lax.axis_size(a) for a in ("gx", "gy", "gz"))
    plan = Plan(grid, shard)
    ngx, ngy, ngz = grid
    ny = ngy * sy
    groups = plan.groups
    const = jnp.asarray(tables(plan.halo + plan.own))
    buffers = [
        pltpu.VMEM((FIELDS, sx, sy, sz), F32),
        pltpu.VMEM((2, sx, sy, sz), jnp.int32),
        pltpu.VMEM((plan.sends, plan.tiles, sy, LANES), F32),
        pltpu.VMEM((2, ngx, ngy, plan.tiles, sy, LANES), F32),
        pltpu.VMEM((7, 3, groups, ny, LANES), F32),
        pltpu.VMEM((3, groups, ny, LANES), F32),
        pltpu.VMEM((17, groups, ny, LANES), F32),
        pltpu.VMEM((2, 7, 3 * groups * ny // 8, 8, LANES), F32),
        pltpu.VMEM((ngx, ngy, 6, sy, LANES), F32),
        pltpu.VMEM((plan.returns, 6, sy, LANES), F32),
        pltpu.VMEM((plan.workers, 1, LANES), F32),
        pltpu.VMEM((plan.workers, 2, LANES), F32),
        pltpu.VMEM((2, 2, 8, LANES), F32),
        pltpu.VMEM((2, 8, LANES), F32),
        pltpu.VMEM(const.shape, F32),
        pltpu.SMEM(table.shape[::-1], F32),
        pltpu.SemaphoreType.DMA((6,)),
        pltpu.SemaphoreType.DMA((1,)),
        pltpu.SemaphoreType.DMA((2,)),
        pltpu.SemaphoreType.DMA((1,)),
        pltpu.SemaphoreType.DMA((1,)),
        pltpu.SemaphoreType.DMA((2,)),
        pltpu.SemaphoreType.DMA((2,)),
        pltpu.SemaphoreType.REGULAR,
    ]
    operands = (displacement, load, material, free_node, table.T, const)
    both = pl.pallas_call(
        functools.partial(kernel, plan),
        out_shape=jax.ShapeDtypeStruct((2, 3, sx * sy, sz), F32),
        in_specs=[pl.BlockSpec(memory_space=pltpu.HBM)] * 6,
        out_specs=pl.BlockSpec(memory_space=pltpu.VMEM),
        scratch_shapes=buffers,
        compiler_params=pltpu.CompilerParams(
            collective_id=0, has_side_effects=True, vmem_limit_bytes=32 << 20
        ),
    )(*(pltpu.with_memory_space_constraint(a, pltpu.HBM) for a in operands))
    return both[0].reshape(displacement.shape), both[1].reshape(displacement.shape)


def solution(mesh):
    in_specs = (
        P(None, "gx", "gy", "gz"),
        P(None, "gx", "gy", "gz"),
        P("gx", "gy", "gz"),
        P("gx", "gy", "gz"),
        P(),
    )
    out_specs = (P(None, "gx", "gy", "gz"), P(None, "gx", "gy", "gz"))
    return jax.shard_map(
        per_device, mesh=mesh, in_specs=in_specs, out_specs=out_specs, check_vma=False
    )
```
